32 devices in a mesh: groups: 2 (over y), expert: 8 (over z, core), section: 2 (over x), tensor: 1.
Axes of the slice: x: 2, y: 2, z: 4, core: 2. Of those that a mesh axis runs over, the one named last changes fastest.
Arguments:
- opening_residual: bfloat16 [2, 2048, 2048], P('section', ('groups', 'expert'), 'tensor'), parts along dimension 1, may hold values from -12 to 12
- incoming_residual: bfloat16 [1, 2048, 2048], P(None, ('groups', 'expert'), 'tensor'), parts along dimension 1, may hold values from -12 to 12
- stored_summaries: bfloat16 [2, 2, 16, 768, 512], P(None, 'section', ('groups', 'expert')), parts along dimension 2, may hold values from -40 to 40
- stored_counts: int32 [3, 16], P(None, ('groups', 'expert')), parts along dimension 1, may hold values from 1 to 768, as said below
- picked_specialists: int32 [2, 2, 2048, 6], P(None, 'section', ('groups', 'expert')), parts along dimension 2, may hold values from 0 to 15, all different within a row; in each aligned block of 128 rows (0 to 127, 128 to 255, ..., all dimensions but the last counted through in order) at most 64 rows name the same one
- chooser_mixing_share: float32 [2, 2, 2048, 6], P(None, 'section', ('groups', 'expert')), parts along dimension 2, may hold values from 0.05 to 0.4
- mixing_scale_factor: float32 [2, 2048], P('section'), may hold values from 0.25 to 1.75
- asking_projection: bfloat16 [2, 2048, 1024], P('section', None, 'tensor'), may hold values from -0.125 to 0.125
- summary_lookup_factor: bfloat16 [2, 8, 128, 512], P('section', 'tensor'), may hold values from -0.5 to 0.5
- summary_content_factor: bfloat16 [2, 8, 512, 128], P('section', 'tensor'), may hold values from -0.25 to 0.25
- merging_projection: bfloat16 [2, 1024, 2048], P('section', 'tensor'), may hold values from -0.1875 to 0.1875
- compress_projection: bfloat16 [2, 2048, 512], P('section', None, 'tensor'), may hold values from -0.125 to 0.125
- summary_scale_factor: float32 [2, 512], P('section'), may hold values from 0.25 to 1.75
- specialist_scale_factor: float32 [2, 2048], P('section', 'tensor'), may hold values from 0.25 to 1.75
- specialist_switch_factor: bfloat16 [2, 16, 2048, 704], P('section', 'expert', None, 'tensor'), may hold values from -0.125 to 0.125
- specialist_widen_factor: bfloat16 [2, 16, 2048, 704], P('section', 'expert', None, 'tensor'), may hold values from -0.125 to 0.125
- specialist_contract_factor: bfloat16 [2, 16, 704, 2048], P('section', 'expert', 'tensor'), may hold values from -0.21875 to 0.21875
Outputs:
- results: bfloat16 [2, 2, 2048, 2048], P(None, 'section', ('groups', 'expert'), 'tensor'), parts along dimension 2
The draws below stay inside these ranges and needn't reach their ends.
There are 2 independent parts, one for each index of `groups`. The reference program is written for one: setup_inputs(seed, part) draws one part's arguments, and reference() takes and returns one part's arrays. A program takes and returns all parts, laid end to end along the dimension named above; an argument that names none is the same for every part. Nothing has to cross between parts.
Inputs may be any that keep to these rules, and one draw needn't show every extreme that they name: `picked_specialists`: in each aligned block of 128 rows (one sequence) no expert is chosen by more than 64 rows, a bound that some block reaches; each row names 6 different experts. `stored_counts`: in every microbatch some sequence has exactly 768 cached tokens.
All inputs are finite; a program needn't handle non-finite values.
Results may differ from the reference program's by a relative error of at most 0.04.
Values may be sent and summed in bfloat16 or wider, within the bound.
A program may use at most 128 MiB of HBM per device.

```python
import math
import jax
import jax.numpy as jnp
import numpy as np
from jax import lax

D = 2048
HD = 128
LAT = 512
TOP = 6
HEADS = 8
FFE = 704
EXPERTS = 16
TICKS = 2
TOK_DEV = 128
CTX = 768
SECTIONS = 2
SEQS = 8
ROWS = 1024
MICRO = 3
CAP = 64
N_TENSOR = 1


def activation_draw(key, array_shape):
    key_values, key_scale, key_column = jax.random.split(key, 3)
    row_scale = jnp.exp(jax.random.uniform(key_scale, array_shape[:-1] + (1,), jnp.float32, math.log(0.3), math.log(1.5)))
    width = array_shape[-1]
    ramp = jnp.arange(width, dtype=jnp.float32) / (width - 1)
    jitter = jnp.exp(jax.random.uniform(key_column, (width,), jnp.float32, -0.15, 0.15))
    column_scale = jnp.exp(math.log(0.5) + ramp * math.log(4.0)) * jitter
    values = jnp.clip(jax.random.normal(key_values, array_shape, jnp.float32), -3.5, 3.5)
    return jnp.clip(values * row_scale * column_scale, -12.0, 12.0)


def draw_opening_residual(key, part):
    return activation_draw(jax.random.fold_in(key, 11), (SECTIONS, ROWS, D)).astype(jnp.bfloat16)


def draw_incoming_residual(key, part):
    return activation_draw(jax.random.fold_in(key, 23), (TICKS - 1, ROWS, D)).astype(jnp.bfloat16)


def draw_stored_summaries(key, part):
    key_values = jax.random.fold_in(jax.random.fold_in(key, 37), 0)
    array_shape = (TICKS, SECTIONS, SEQS, CTX, LAT)
    values = jnp.clip(jax.random.normal(key_values, array_shape, jnp.float32), -4.0, 4.0)
    return values.astype(jnp.bfloat16)


def draw_stored_counts(key, part):
    key_values, key_full = jax.random.split(jax.random.fold_in(key, 41))
    values = jax.random.randint(key_values, (MICRO, SEQS), 1, CTX + 1).astype(jnp.int32)
    full_seq = jax.random.randint(key_full, (MICRO, 1), 0, SEQS).astype(jnp.int32)
    seq_index = jnp.arange(SEQS, dtype=jnp.int32)[None, :]
    return jnp.where(seq_index == full_seq, CTX, values).astype(jnp.int32)


def block_scale(own_key, extent, pieces, low, largest):
    loudness = 1.0
    for dim, parts in pieces:
        steps = jax.random.uniform(jax.random.fold_in(jax.random.fold_in(own_key, 6), dim), (parts,), jnp.float32, low / len(pieces), largest / len(pieces))
        loudness = loudness * jnp.repeat(jnp.exp(steps), extent[dim] // parts).reshape((-1,) + (1,) * (len(extent) - 1 - dim))
    return loudness


def routed_block(stream_key, own, number, rows, number_of, top, limit, slope):
    ranking = jax.random.permutation(stream_key, number_of)
    heavy_load, ordinary = shares(number_of, rows * top, limit, slope, True), shares(number_of, rows * top, limit, slope, False)
    places = jnp.arange(number_of)

    def named(sizes, offset_by):
        used = int((sizes > 0).sum())
        fixed = max(1, used // 4)
        moved = fixed + (places - fixed + offset_by * (used - fixed)) % max(1, number_of - fixed)
        return jnp.zeros((number_of,), jnp.int32).at[ranking[jnp.where(places < fixed, places, moved)]].set(jnp.asarray(sizes, jnp.int32))

    sizes = jnp.where(number % 4 == 0, named(heavy_load, number // 4), named(ordinary, number - number // 4 - 1))
    mixed = jax.random.permutation(jax.random.fold_in(own, 3), number_of)
    giver, receiver = mixed[0:number_of // 2 * 2:2], mixed[1:number_of // 2 * 2:2]
    margin = jnp.minimum(sizes[giver] - 1, limit - sizes[receiver]) // 2
    margin = jnp.where((giver == ranking[0]) | (receiver == ranking[0]) | (sizes[receiver] == 0), 0, jnp.maximum(margin, 0))
    moved = jax.random.randint(jax.random.fold_in(own, 4), (number_of // 2,), 0, 1 << 20) % (margin + 1)
    sizes = sizes.at[giver].add(-moved).at[receiver].add(moved)
    members = jnp.searchsorted(jnp.cumsum(sizes), jnp.arange(rows * top), side="right").astype(jnp.int32)
    listing = members.reshape(top, rows).T
    listing = listing[jax.random.permutation(jax.random.fold_in(own, 1), rows)]
    offset_by = jax.random.randint(jax.random.fold_in(own, 2), (rows, 1), 0, top)
    return jnp.take_along_axis(listing, (jnp.arange(top)[None, :] + offset_by) % top, axis=1)


def shares(amount, total, reach, lean, full):
    weights = [(1 << 20) // math.isqrt(standing ** lean) + 1 for standing in range(1, amount + 1)]
    largest = reach if full else min(reach, max(-(-total // amount), total * weights[0] // sum(weights)))
    least = 1 if total - largest >= amount - 1 else 0
    holding, surplus = [largest] + [least] * (amount - 1), total - largest - least * (amount - 1)
    while surplus > 0:
        candidates = [i for i in range(1, amount) if holding[i] < largest] or [i for i in range(1, amount) if holding[i] < reach]
        pool, left = sum([weights[i] for i in candidates]), surplus
        for i in candidates:
            addition = min(reach - holding[i], max(1, left * weights[i] // pool), surplus)
            holding[i] = holding[i] + addition
            surplus = surplus - addition
    return np.array(holding)


def bell_draw(stream_key, extent, scale, reach, shards=(), kind=jnp.bfloat16):
    result = jax.random.normal(stream_key, extent, jnp.float32) * scale
    if len(shards) > 0:
        result = block_scale(stream_key, extent, shards, -0.22, 0.18) * result
    return jnp.clip(result, min=-reach, max=reach).astype(kind)


def setup_inputs(seed: int = 0, part: int = 0) -> dict:
    seeds = jax.random.split(jax.random.key(seed), 18)
    part_keys = jax.random.split(jax.random.fold_in(seeds[17], part), 18)
    opening_residual = draw_opening_residual(jax.random.fold_in(jax.random.fold_in(seeds[17], part), 71), part)
    incoming_residual = draw_incoming_residual(jax.random.fold_in(jax.random.fold_in(seeds[17], part), 71), part)
    stored_summaries = draw_stored_summaries(jax.random.fold_in(jax.random.fold_in(seeds[17], part), 71), part)
    stored_counts = draw_stored_counts(jax.random.fold_in(jax.random.fold_in(seeds[17], part), 71), part)
    picked_specialists_keys = jax.random.split(jax.random.fold_in(part_keys[4], 1), TICKS * SECTIONS * ROWS // TOK_DEV)
    picked_specialists_turns = jax.random.permutation(jax.random.fold_in(part_keys[4], 3), TICKS * SECTIONS * ROWS // TOK_DEV)
    picked_specialists = jax.vmap(lambda own, number: routed_block(jax.random.fold_in(part_keys[4], 2), own, number, TOK_DEV, EXPERTS, TOP, CAP, 2))(picked_specialists_keys, picked_specialists_turns).reshape((TICKS, SECTIONS, ROWS, TOP))
    chooser_mixing_share = jnp.clip(0.05 + 0.35 * jax.random.uniform(part_keys[5], (TICKS, SECTIONS, ROWS, TOP), jnp.float32) ** block_scale(part_keys[5], (TICKS, SECTIONS, ROWS, TOP), ((1, 2), (2, 8)), -0.2, 0.2), 0.05, 0.4)
    mixing_scale_factor = jnp.clip(1.0 + 0.15 * jax.random.normal(seeds[6], (SECTIONS, D), jnp.float32), 0.25, 1.75)
    asking_projection = bell_draw(seeds[7], (SECTIONS, D, HEADS * HD), D ** -0.5, 0.125, ((0, 2),))
    summary_lookup_factor = bell_draw(seeds[8], (SECTIONS, HEADS, HD, LAT), HD ** -0.5, 0.5, ((0, 2),))
    summary_content_factor = bell_draw(seeds[9], (SECTIONS, HEADS, LAT, HD), LAT ** -0.5, 0.25, ((0, 2),))
    merging_projection = bell_draw(seeds[10], (SECTIONS, HEADS * HD, D), (HEADS * HD) ** -0.5, 0.1875, ((0, 2),))
    compress_projection = bell_draw(seeds[11], (SECTIONS, D, LAT), D ** -0.5, 0.125, ((0, 2),))
    summary_scale_factor = jnp.clip(1.0 + 0.15 * jax.random.normal(seeds[12], (SECTIONS, LAT), jnp.float32), 0.25, 1.75)
    specialist_scale_factor = jnp.clip(1.0 + 0.15 * jax.random.normal(seeds[13], (SECTIONS, D), jnp.float32), 0.25, 1.75)
    specialist_switch_factor = bell_draw(seeds[14], (SECTIONS, EXPERTS, D, FFE), D ** -0.5, 0.125, ((0, 2), (1, 8)))
    specialist_widen_factor = bell_draw(seeds[15], (SECTIONS, EXPERTS, D, FFE), D ** -0.5, 0.125, ((0, 2), (1, 8)))
    specialist_contract_factor = bell_draw(seeds[16], (SECTIONS, EXPERTS, FFE, D), FFE ** -0.5, 0.21875, ((0, 2), (1, 8)))
    return {"opening_residual": opening_residual, "incoming_residual": incoming_residual, "stored_summaries": stored_summaries, "stored_counts": stored_counts, "picked_specialists": picked_specialists, "chooser_mixing_share": chooser_mixing_share, "mixing_scale_factor": mixing_scale_factor, "asking_projection": asking_projection, "summary_lookup_factor": summary_lookup_factor, "summary_content_factor": summary_content_factor, "merging_projection": merging_projection, "compress_projection": compress_projection, "summary_scale_factor": summary_scale_factor, "specialist_scale_factor": specialist_scale_factor, "specialist_switch_factor": specialist_switch_factor, "specialist_widen_factor": specialist_widen_factor, "specialist_contract_factor": specialist_contract_factor}


epsilon = 1e-06

def row_norm(values, gain_row):
    return values * lax.rsqrt(lax.optimization_barrier(jnp.mean(values * values, axis=-1, keepdims=True)) + epsilon) * gain_row

def attend(q_lat, cache_rows, new_rows, length):
    key_rows = jnp.concatenate([cache_rows, new_rows], axis=0)
    scores = jnp.einsum('thl,kl->thk', q_lat.astype(jnp.float32), key_rows.astype(jnp.float32)) * HD ** (-0.5)
    position = jnp.arange(CTX + TOK_DEV, dtype=jnp.int32)[None, :]
    query_pos = jnp.arange(TOK_DEV, dtype=jnp.int32)[:, None]
    visible = jnp.where(position < CTX, position < length, position - CTX <= query_pos)
    scores = jnp.where(visible[:, None, :], scores, -jnp.inf)
    row_max = lax.optimization_barrier(jnp.max(scores, axis=-1, keepdims=True))
    expd = jnp.where(visible[:, None, :], jnp.exp(scores - row_max), 0.0)
    attention = (expd / lax.optimization_barrier(jnp.sum(expd, axis=-1, keepdims=True))).astype(jnp.bfloat16)
    return jnp.einsum('thk,kl->thl', attention.astype(jnp.float32), key_rows.astype(jnp.float32)).astype(jnp.bfloat16)

def run_layer(inner_response, cache_now, lengths_now, route, gates, segment_ordinal, mixing_scale_factor, asking_projection, summary_lookup_factor, summary_content_factor, merging_projection, compress_projection, summary_scale_factor, specialist_scale_factor, specialist_switch_factor, specialist_widen_factor, specialist_contract_factor):
    start_rows = inner_response.astype(jnp.float32)
    normed = row_norm(start_rows, mixing_scale_factor[segment_ordinal]).astype(jnp.bfloat16)
    queries = jnp.dot(normed, asking_projection[segment_ordinal], preferred_element_type=jnp.float32).astype(jnp.bfloat16)
    queries = queries.reshape(ROWS, HEADS, HD)
    q_lat = jnp.einsum('rnd,ndl->rnl', queries.astype(jnp.float32), summary_lookup_factor[segment_ordinal].astype(jnp.float32)).astype(jnp.bfloat16)
    latent_raw = jnp.dot(normed, compress_projection[segment_ordinal], preferred_element_type=jnp.float32)
    new_latent = row_norm(latent_raw, summary_scale_factor[segment_ordinal]).astype(jnp.bfloat16)
    o_lat = lax.map(lambda packed: attend(packed[0], packed[1], packed[2], packed[3]), (q_lat.reshape(SEQS, TOK_DEV, HEADS, LAT), cache_now, new_latent.reshape(SEQS, TOK_DEV, LAT), lengths_now))
    o_lat = o_lat.reshape(ROWS, HEADS, LAT)
    heads_out = jnp.einsum('rnl,nld->rnd', o_lat.astype(jnp.float32), summary_content_factor[segment_ordinal].astype(jnp.float32)).astype(jnp.bfloat16)
    heads_out = heads_out.reshape(ROWS, HEADS * HD)
    residual = start_rows + jnp.dot(heads_out, merging_projection[segment_ordinal], preferred_element_type=jnp.float32)
    moe_input = row_norm(residual, specialist_scale_factor[segment_ordinal]).astype(jnp.bfloat16)
    choices = route.reshape(SEQS, TOK_DEV * TOP).astype(jnp.int32)
    onehot = (choices[:, :, None] == jnp.arange(EXPERTS, dtype=jnp.int32)[None, None, :]).astype(jnp.int32)
    earlier = jnp.cumsum(onehot, axis=1) - onehot
    slot_index = lax.optimization_barrier(jnp.sum(earlier * onehot, axis=2))
    block_index = jnp.arange(SEQS, dtype=jnp.int32)[:, None]
    target = (choices * (SEQS * CAP) + block_index * CAP + slot_index).reshape(-1).astype(jnp.int32)
    source = jnp.repeat(jnp.arange(ROWS, dtype=jnp.int32), TOP)
    buffer = jnp.zeros((EXPERTS * SEQS * CAP, D), jnp.bfloat16).at[target].set(moe_input[source])
    buffer = buffer.reshape(EXPERTS, SEQS * CAP, D)

    def one_expert(packed):
        rows_in, gate_mat, up_mat, down_mat = packed
        gate_values = jnp.dot(rows_in, gate_mat, preferred_element_type=jnp.float32)
        up_values = jnp.dot(rows_in, up_mat, preferred_element_type=jnp.float32)
        hidden = (jax.nn.silu(gate_values) * up_values).astype(jnp.bfloat16)
        hidden_parts = hidden.reshape(SEQS * CAP, N_TENSOR, FFE // N_TENSOR).astype(jnp.float32)
        down_parts = down_mat.reshape(N_TENSOR, FFE // N_TENSOR, D).astype(jnp.float32)
        partial_value = jnp.einsum('mpf,pfd->pmd', hidden_parts, down_parts).astype(jnp.bfloat16)
        return lax.optimization_barrier(jnp.sum(partial_value.astype(jnp.float32), axis=0)).astype(jnp.bfloat16)
    expert_out = lax.map(one_expert, (buffer, specialist_switch_factor[segment_ordinal], specialist_widen_factor[segment_ordinal], specialist_contract_factor[segment_ordinal]))
    picked = expert_out.reshape(EXPERTS * SEQS * CAP, D)[target].astype(jnp.float32).reshape(ROWS, TOP, D)
    routed = lax.optimization_barrier(jnp.sum(picked * gates[:, :, None], axis=1))
    return (residual + routed).astype(jnp.bfloat16)

def reference(opening_residual, incoming_residual, stored_summaries, stored_counts, picked_specialists, chooser_mixing_share, mixing_scale_factor, asking_projection, summary_lookup_factor, summary_content_factor, merging_projection, compress_projection, summary_scale_factor, specialist_scale_factor, specialist_switch_factor, specialist_widen_factor, specialist_contract_factor):
    outputs = []
    previous = []
    for step_index in range(TICKS):
        current_row = []
        for segment_ordinal in range(SECTIONS):
            if step_index == 0:
                inner_response = opening_residual[segment_ordinal]
            elif segment_ordinal == 0:
                inner_response = incoming_residual[step_index - 1]
            else:
                inner_response = previous[segment_ordinal - 1]
            micro_index = step_index - segment_ordinal + SECTIONS - 1
            result_rows = run_layer(inner_response, stored_summaries[step_index, segment_ordinal], stored_counts[micro_index], picked_specialists[step_index, segment_ordinal], chooser_mixing_share[step_index, segment_ordinal], segment_ordinal, mixing_scale_factor, asking_projection, summary_lookup_factor, summary_content_factor, merging_projection, compress_projection, summary_scale_factor, specialist_scale_factor, specialist_switch_factor, specialist_widen_factor, specialist_contract_factor)
            current_row.append(result_rows)
        previous = current_row
        outputs.append(jnp.stack(current_row))
    return jnp.stack(outputs)
```

```python
import jax
import jax.numpy as jnp
from jax import lax
from jax.experimental import pallas as pl
from jax.experimental.pallas import tpu as pltpu
from jax.sharding import PartitionSpec as P


epsilon = 1e-06


MESH = pl.DeviceIdType.MESH
PIECES = 4
RETURN_PIECES = 4
NT = (((1,), (1,)), ((), ()))


def place_on_line():
    count = lax.axis_size("expert")
    pair = 2 if count % 2 == 0 else 1
    mine = lax.axis_index("expert")
    return count // pair, pair, mine, mine // pair, lax.rem(mine, pair)


def greet(chips, pair, mine, spot, side):
    barrier = pltpu.get_barrier_semaphore()

    def hello(other):
        pl.semaphore_signal(barrier, inc=1, device_id={"expert": other}, device_id_type=MESH)

    @pl.when(spot > 0)
    def _():
        hello(mine - pair)

    @pl.when(spot < chips - 1)
    def _():
        hello(mine + pair)

    if pair == 2:
        hello(mine + 1 - 2 * side)
    inner = (spot > 0) & (spot < chips - 1)

    @pl.when(inner)
    def _():
        pl.semaphore_wait(barrier, pair + 1)

    @pl.when(jnp.logical_not(inner))
    def _():
        pl.semaphore_wait(barrier, pair)


def remote(src, dst, send, recv, other):
    return pltpu.make_async_remote_copy(
        src_ref=src,
        dst_ref=dst,
        send_sem=send,
        recv_sem=recv,
        device_id={"expert": other},
        device_id_type=MESH,
    )


def visiting_order(k, spot, chips):
    low = jnp.minimum(spot, chips - 1 - spot)
    near = (k + 1) // 2
    around = spot + jnp.where(lax.rem(k, 2) == 0, near, -near)
    rest = jnp.where(spot < chips - 1 - spot, k, chips - 1 - k)
    return jnp.where(k <= 2 * low, around, rest)


def experts_kernel(
    own_ref,
    small_ref,
    gate_hbm,
    up_hbm,
    down_hbm,
    sum_ref,
    gate,
    up,
    down,
    rows_all,
    small_all,
    hidden,
    part,
    side_in,
    line_in,
    own_sem,
    weight_sem,
    line_send,
    line_recv,
    side_send,
    side_recv,
    give_send,
    give_recv,
    back_send,
    back_recv,
):
    chips, pair, mine, spot, side = place_on_line()
    height, width = own_ref.shape
    local = gate.shape[0]
    step = height // PIECES
    chunk = width // RETURN_PIECES
    sibling = mine + 1 - 2 * side
    at_end = (spot == 0) | (spot == chips - 1)

    loads = []
    for index, (source, target) in enumerate(((gate_hbm, gate), (up_hbm, up), (down_hbm, down))):
        for e in range(local):
            loads.append(
                pltpu.make_async_copy(source.at[e], target.at[e], weight_sem.at[index, e])
            )

    def rows(block, core, piece):
        if piece == PIECES:
            return small_all.at[block, core]
        first = pl.multiple_of(core * height + piece * step, step)
        return rows_all.at[block, pl.ds(first, step)]

    def origin(block, piece):
        if block is not None:
            return rows(block, side, piece)
        return small_ref if piece == PIECES else own_ref.at[pl.ds(piece * step, step)]

    def line_copy(block, piece, way):
        where = spot if block is None else block
        direction = 0 if way > 0 else 1
        return remote(
            origin(block, piece),
            rows(where, side, piece),
            line_send.at[direction, where, piece],
            line_recv.at[where, piece],
            mine + way * pair,
        )

    def side_copy(block, piece):
        where = spot if block is None else block
        return remote(
            origin(block, piece),
            rows(where, side, piece),
            side_send.at[where, piece],
            side_recv.at[where, piece],
            sibling,
        )

    def onward(block, piece, way, act):
        @pl.when((spot < chips - 1) if way > 0 else (spot > 0))
        def _():
            act(line_copy(block, piece, way))

    def passing(far, act):
        for piece in range(PIECES + 1):
            for way in (1, -1):
                block = spot - way * far

                @pl.when((block >= 0) if way > 0 else (block < chips))
                def _():
                    act(block, piece, way)

    def give_copy(block, piece):
        return remote(
            part.at[block, 1 - side, piece],
            side_in.at[block, piece],
            give_send.at[block, piece],
            give_recv.at[block, piece],
            sibling,
        )

    def back_copy(block, piece, way):
        direction = (1 - way) // 2
        return remote(
            part.at[block, side, piece],
            line_in.at[direction, block, piece],
            back_send.at[block, piece],
            back_recv.at[direction, block, piece],
            mine + way * pair,
        )

    def wide(value):
        return value.astype(jnp.float32)

    def combine(block, piece, way, from_line):
        give_copy(block, piece).wait_recv()
        value = wide(part[block, side, piece]) + wide(side_in[block, piece])
        if from_line:
            back_copy(block, piece, way).wait_recv()
            value = value + wide(line_in[(1 - way) // 2, block, piece])
        part[block, side, piece] = value.astype(part.dtype)
        back_copy(block, piece, way).start()

    greet(chips, pair, mine, spot, side)
    for piece in (PIECES, *range(PIECES)):
        for way in (1, -1):
            onward(None, piece, way, lambda copy: copy.start())
        side_copy(None, piece).start()
    keep = pltpu.make_async_copy(
        own_ref, rows_all.at[spot, pl.ds(pl.multiple_of(side * height, height), height)], own_sem.at[0]
    )
    keep.start()
    keep_small = pltpu.make_async_copy(small_ref, small_all.at[spot, side], own_sem.at[1])
    keep_small.start()
    for load in loads:
        load.start()
    keep.wait()
    keep_small.wait()
    for load in loads:
        load.wait()

    def visit(k, carry):
        block = visiting_order(k, spot, chips)
        way = jnp.where(block > spot, 1, -1)
        outward = at_end & (k > 0)
        for piece in range(PIECES + 1):
            side_copy(block, piece).wait_recv()
        values = rows_all[block]
        for e in range(local):
            chosen_expert = mine * local + e
            columns = []
            for core in range(pair):
                table = small_all[block, core]
                here = lax.broadcasted_iota(jnp.int32, table.shape, 0) == chosen_expert
                row = jnp.sum(jnp.where(here, table, 0.0), axis=0, keepdims=True)
                columns.append(jnp.broadcast_to(row, (height, height)).T[:, :1])
            share = jnp.concatenate(columns, axis=0)
            gated = lax.dot_general(values, gate[e], NT, preferred_element_type=jnp.float32)
            upped = lax.dot_general(values, up[e], NT, preferred_element_type=jnp.float32)
            hidden[e] = (gated * jax.nn.sigmoid(gated) * upped * share).astype(hidden.dtype)
        for piece in range(RETURN_PIECES):
            total = None
            for e in range(local):
                term = jnp.dot(
                    hidden[e],
                    down[e, :, piece * chunk : (piece + 1) * chunk],
                    preferred_element_type=jnp.float32,
                )
                total = term if total is None else total + term
            total = total.astype(part.dtype)
            for core in range(pair):
                part[block, core, piece] = total[core * height : (core + 1) * height]
            give_copy(block, piece).start()
            if piece > 0:

                @pl.when(outward)
                def _():
                    combine(block, piece - 1, way, False)

        @pl.when(outward)
        def _():
            combine(block, RETURN_PIECES - 1, way, False)

        @pl.when(k < chips - 1)
        def _():
            def receive(block, piece, way):
                line_copy(block, piece, way).wait_recv()
                onward(block, piece, way, lambda copy: copy.start())
                side_copy(block, piece).start()

            passing(k + 1, receive)

        return carry

    lax.fori_loop(0, chips, visit, 0)

    left_first = 2 * spot <= chips - 1

    def relay(a, carry):
        for piece in range(RETURN_PIECES):
            for turn in range(2):
                way = jnp.where(left_first, 1 - 2 * turn, 2 * turn - 1)
                block = jnp.where(way > 0, a, chips - 1 - a)
                valid = jnp.where(way > 0, block > spot, block < spot) & jnp.logical_not(at_end)

                @pl.when(valid)
                def _():
                    combine(block, piece, way, True)

        return carry

    lax.fori_loop(1, chips, relay, 0)
    for piece in range(RETURN_PIECES):
        give_copy(spot, piece).wait_recv()
        columns = pl.ds(piece * chunk, chunk)
        sum_ref[:, columns] = wide(part[spot, side, piece]) + wide(side_in[spot, piece])
        for way in (1, -1):

            @pl.when((spot > 0) if way > 0 else (spot < chips - 1))
            def _():
                back_copy(spot, piece, way).wait_recv()
                sum_ref[:, columns] += wide(line_in[(1 - way) // 2, spot, piece])

    for piece in range(PIECES + 1):
        for way in (1, -1):
            onward(None, piece, way, lambda copy: copy.wait_send())
        side_copy(None, piece).wait_send()

    def settle(far, carry):
        def sent(block, piece, way):
            onward(block, piece, way, lambda copy: copy.wait_send())
            side_copy(block, piece).wait_send()

        passing(far, sent)
        return carry

    lax.fori_loop(1, chips, settle, 0)

    def settle_back(block, carry):
        for piece in range(RETURN_PIECES):
            give_copy(block, piece).wait_send()

            @pl.when(block != spot)
            def _():
                back_copy(block, piece, jnp.where(block > spot, 1, -1)).wait_send()

        return carry

    lax.fori_loop(0, chips, settle_back, 0)


def experts(own, small, gate, up, down):
    count = lax.axis_size("expert")
    pair = 2
    chips = count // pair
    height, width = own.shape
    local, inner = down.shape[:2]
    kind = own.dtype
    chunk = width // RETURN_PIECES
    blocks = chips * pair * height * width * 2
    weights = 3 * local * inner * width * 2
    dma = pltpu.SemaphoreType.DMA
    hbm = pl.BlockSpec(memory_space=pl.ANY)
    vmem = pl.BlockSpec(memory_space=pltpu.VMEM)
    return pl.pallas_call(
        experts_kernel,
        out_shape=jax.ShapeDtypeStruct((height, width), jnp.float32),
        in_specs=[vmem, vmem, hbm, hbm, hbm],
        out_specs=vmem,
        scratch_shapes=[
            pltpu.VMEM((local, inner, width), kind),
            pltpu.VMEM((local, inner, width), kind),
            pltpu.VMEM((local, inner, width), kind),
            pltpu.VMEM((chips, pair * height, width), kind),
            pltpu.VMEM((chips, pair) + small.shape, small.dtype),
            pltpu.VMEM((local, pair * height, inner), kind),
            pltpu.VMEM((chips, pair, RETURN_PIECES, height, chunk), kind),
            pltpu.VMEM((chips, RETURN_PIECES, height, chunk), kind),
            pltpu.VMEM((2, chips, RETURN_PIECES, height, chunk), kind),
            dma((2,)),
            dma((3, local)),
            dma((2, chips, PIECES + 1)),
            dma((chips, PIECES + 1)),
            dma((chips, PIECES + 1)),
            dma((chips, PIECES + 1)),
            dma((chips, RETURN_PIECES)),
            dma((chips, RETURN_PIECES)),
            dma((chips, RETURN_PIECES)),
            dma((2, chips, RETURN_PIECES)),
        ],
        compiler_params=pltpu.CompilerParams(
            collective_id=0, has_side_effects=True, vmem_limit_bytes=4 * blocks + weights + 12 * 2**20
        ),
        cost_estimate=pl.CostEstimate(
            flops=2 * weights * blocks // (width * 4), bytes_accessed=32 * blocks, transcendentals=0
        ),
    )(own, small, gate, up, down)


def shifted(value, axis, steps):
    count = lax.axis_size(axis)
    initial, last = (max(0, -steps), min(count, count - steps))
    return lax.ppermute(value, axis, [(source, source + steps) for source in range(initial, last)])


def row_norm(values, gain_row):
    return (
        values * lax.rsqrt(jnp.mean(values * values, axis=-1, keepdims=True) + epsilon) * gain_row
    )


def attend(q_lat, cache_rows, new_rows, length, score_scale):
    piece_list = q_lat.shape[0]
    context = cache_rows.shape[0]
    key_rows = jnp.concatenate([cache_rows, new_rows], axis=0)
    scores = (
        jnp.einsum("thl,kl->thk", q_lat, key_rows, preferred_element_type=jnp.float32) * score_scale
    )
    position = lax.broadcasted_iota(jnp.int32, (piece_list, context + piece_list), 1)
    query_pos = lax.broadcasted_iota(jnp.int32, (piece_list, context + piece_list), 0)
    visible = jnp.where(position < context, position < length, position - context <= query_pos)
    scores = jnp.where(visible[:, None, :], scores, -jnp.inf)
    row_max = jnp.max(scores, axis=-1, keepdims=True)
    expd = jnp.where(visible[:, None, :], jnp.exp(scores - row_max), 0.0)
    attention = (expd / jnp.sum(expd, axis=-1, keepdims=True)).astype(jnp.bfloat16)
    return jnp.einsum(
        "thk,kl->thl", attention, key_rows, preferred_element_type=jnp.float32
    ).astype(jnp.bfloat16)


def shards(
    opening_residual,
    incoming_residual,
    stored_summaries,
    stored_counts,
    picked_specialists,
    chooser_mixing_share,
    mixing_scale_factor,
    asking_projection,
    summary_lookup_factor,
    summary_content_factor,
    merging_projection,
    compress_projection,
    summary_scale_factor,
    specialist_scale_factor,
    specialist_switch_factor,
    specialist_widen_factor,
    specialist_contract_factor,
):
    segment_ordinal = lax.axis_index("section")
    section_count = lax.axis_size("section")
    sources = lax.axis_size("expert")
    tick_count = stored_summaries.shape[0]
    piece_list = opening_residual.shape[1]
    inner_feature_midcount = opening_residual.shape[2]
    full_width = mixing_scale_factor.shape[1]
    local_heads = summary_lookup_factor.shape[1]
    head_size = summary_lookup_factor.shape[2]
    top_count = picked_specialists.shape[3]
    expert_local = specialist_switch_factor.shape[1]
    score_scale = head_size ** (-0.5)
    expert_ids = lax.broadcasted_iota(jnp.int32, (1, 1, 1, expert_local * sources), 3)
    shares_dense = jnp.sum(
        jnp.where(
            picked_specialists[:, 0][..., None] == expert_ids,
            chooser_mixing_share[:, 0][..., None],
            0.0,
        ),
        axis=2,
    )
    shares_dense = jnp.swapaxes(shares_dense, 1, 2)
    outputs = []
    present_carry = opening_residual[0]
    section_out = present_carry
    for step_index in range(tick_count):
        if step_index > 0:
            handed = shifted(section_out, "section", 1)
            present_carry = jnp.where(
                segment_ordinal == 0, incoming_residual[step_index - 1], handed
            )
        micro_index = step_index - segment_ordinal + section_count - 1
        length = lax.dynamic_index_in_dim(stored_counts[:, 0], micro_index, 0, keepdims=False)
        full_rows = lax.all_gather(present_carry, "tensor", axis=1, tiled=True)
        normed = row_norm(full_rows.astype(jnp.float32), mixing_scale_factor[0]).astype(
            jnp.bfloat16
        )
        queries = jnp.dot(normed, asking_projection[0], preferred_element_type=jnp.float32).astype(
            jnp.bfloat16
        )
        queries = queries.reshape(piece_list, local_heads, head_size)
        q_lat = jnp.einsum(
            "thd,hdl->thl", queries, summary_lookup_factor[0], preferred_element_type=jnp.float32
        ).astype(jnp.bfloat16)
        latent_part = jnp.dot(normed, compress_projection[0], preferred_element_type=jnp.float32)
        latent_raw = lax.all_gather(
            latent_part.astype(jnp.bfloat16), "tensor", axis=1, tiled=True
        ).astype(latent_part.dtype)
        new_latent = row_norm(latent_raw, summary_scale_factor[0]).astype(jnp.bfloat16)
        o_lat = attend(q_lat, stored_summaries[step_index, 0, 0], new_latent, length, score_scale)
        heads_out = jnp.einsum(
            "thl,hld->thd", o_lat, summary_content_factor[0], preferred_element_type=jnp.float32
        ).astype(jnp.bfloat16)
        heads_out = heads_out.reshape(piece_list, local_heads * head_size)
        head_terms = jnp.dot(heads_out, merging_projection[0], preferred_element_type=jnp.float32)
        residual = present_carry.astype(jnp.float32) + lax.psum_scatter(
            head_terms.astype(jnp.bfloat16), "tensor", scatter_dimension=1, tiled=True
        ).astype(jnp.float32)
        squares = lax.psum(jnp.sum(residual * residual, axis=1), "tensor")
        moe_input = (
            residual
            * lax.rsqrt(squares / full_width + epsilon)[:, None]
            * specialist_scale_factor[0]
        ).astype(jnp.bfloat16)
        whole_rows = lax.all_gather(moe_input, "tensor", axis=1, tiled=True)
        routed = experts(
            whole_rows,
            shares_dense[step_index],
            jnp.swapaxes(specialist_switch_factor[0], 1, 2),
            jnp.swapaxes(specialist_widen_factor[0], 1, 2),
            specialist_contract_factor[0],
        )
        if lax.axis_size("tensor") > 1:
            routed = lax.psum_scatter(
                routed.astype(jnp.bfloat16), "tensor", scatter_dimension=1, tiled=True
            ).astype(jnp.float32)
        section_out = (residual + routed).astype(jnp.bfloat16)
        outputs.append(section_out)
    return jnp.stack(outputs)[:, None]


def solution(mesh):
    in_specs = (
        P("section", ("groups", "expert"), "tensor"),
        P(None, ("groups", "expert"), "tensor"),
        P(None, "section", ("groups", "expert"), None, None),
        P(None, ("groups", "expert")),
        P(None, "section", ("groups", "expert"), None),
        P(None, "section", ("groups", "expert"), None),
        P("section", None),
        P("section", None, "tensor"),
        P("section", "tensor", None, None),
        P("section", "tensor", None, None),
        P("section", "tensor", None),
        P("section", None, "tensor"),
        P("section", None),
        P("section", "tensor"),
        P("section", "expert", None, "tensor"),
        P("section", "expert", None, "tensor"),
        P("section", "expert", "tensor", None),
    )
    out_specs = P(None, "section", ("groups", "expert"), "tensor")
    return jax.shard_map(shards, mesh=mesh, in_specs=in_specs, out_specs=out_specs, check_vma=False)
```

```python
import jax
import jax.numpy as jnp
from jax import lax
from jax.experimental import pallas as pl
from jax.experimental.pallas import tpu as pltpu
from jax.sharding import PartitionSpec as P


epsilon = 1e-06


MESH = pl.DeviceIdType.MESH
PIECES = 4
RETURN_PIECES = 4
NT = (((1,), (1,)), ((), ()))


def place_on_line():
    count = lax.axis_size("expert")
    pair = 2 if count % 2 == 0 else 1
    mine = lax.axis_index("expert")
    return count // pair, pair, mine, mine // pair, lax.rem(mine, pair)


def greet(chips, pair, mine, spot, side):
    barrier = pltpu.get_barrier_semaphore()

    def hello(other):
        pl.semaphore_signal(barrier, inc=1, device_id={"expert": other}, device_id_type=MESH)

    @pl.when(spot > 0)
    def _():
        hello(mine - pair)

    @pl.when(spot < chips - 1)
    def _():
        hello(mine + pair)

    if pair == 2:
        hello(mine + 1 - 2 * side)
    inner = (spot > 0) & (spot < chips - 1)

    @pl.when(inner)
    def _():
        pl.semaphore_wait(barrier, pair + 1)

    @pl.when(jnp.logical_not(inner))
    def _():
        pl.semaphore_wait(barrier, pair)


def remote(src, dst, send, recv, other):
    return pltpu.make_async_remote_copy(
        src_ref=src,
        dst_ref=dst,
        send_sem=send,
        recv_sem=recv,
        device_id={"expert": other},
        device_id_type=MESH,
    )


def visiting_order(k, spot, chips):
    low = jnp.minimum(spot, chips - 1 - spot)
    near = (k + 1) // 2
    around = spot + jnp.where(lax.rem(k, 2) == 0, near, -near)
    rest = jnp.where(spot < chips - 1 - spot, k, chips - 1 - k)
    return jnp.where(k <= 2 * low, around, rest)


def experts_kernel(
    own_ref,
    small_ref,
    gate_hbm,
    up_hbm,
    down_hbm,
    sum_ref,
    gate,
    up,
    down,
    rows_all,
    small_all,
    hidden,
    part,
    side_in,
    line_in,
    own_sem,
    weight_sem,
    line_send,
    line_recv,
    side_send,
    side_recv,
    give_send,
    give_recv,
    back_send,
    back_recv,
):
    chips, pair, mine, spot, side = place_on_line()
    height, width = own_ref.shape
    local = gate.shape[0]
    step = height // PIECES
    chunk = width // RETURN_PIECES
    sibling = mine + 1 - 2 * side
    at_end = (spot == 0) | (spot == chips - 1)

    loads = []
    for index, (source, target) in enumerate(((gate_hbm, gate), (up_hbm, up), (down_hbm, down))):
        for e in range(local):
            loads.append(
                pltpu.make_async_copy(source.at[e], target.at[e], weight_sem.at[index, e])
            )

    def rows(block, core, piece):
        if piece == PIECES:
            return small_all.at[block, core]
        first = pl.multiple_of(core * height + piece * step, step)
        return rows_all.at[block, pl.ds(first, step)]

    def origin(block, piece):
        if block is not None:
            return rows(block, side, piece)
        return small_ref if piece == PIECES else own_ref.at[pl.ds(piece * step, step)]

    def line_copy(block, piece, way):
        where = spot if block is None else block
        direction = 0 if way > 0 else 1
        return remote(
            origin(block, piece),
            rows(where, side, piece),
            line_send.at[direction, where, piece],
            line_recv.at[where, piece],
            mine + way * pair,
        )

    def side_copy(block, piece):
        where = spot if block is None else block
        return remote(
            origin(block, piece),
            rows(where, side, piece),
            side_send.at[where, piece],
            side_recv.at[where, piece],
            sibling,
        )

    def onward(block, piece, way, act):
        @pl.when((spot < chips - 1) if way > 0 else (spot > 0))
        def _():
            act(line_copy(block, piece, way))

    def passing(far, act):
        for piece in range(PIECES + 1):
            for way in (1, -1):
                block = spot - way * far

                @pl.when((block >= 0) if way > 0 else (block < chips))
                def _():
                    act(block, piece, way)

    def give_copy(block, piece):
        return remote(
            part.at[block, 1 - side, piece],
            side_in.at[block, piece],
            give_send.at[block, piece],
            give_recv.at[block, piece],
            sibling,
        )

    def back_copy(block, piece, way):
        direction = (1 - way) // 2
        return remote(
            part.at[block, side, piece],
            line_in.at[direction, block, piece],
            back_send.at[block, piece],
            back_recv.at[direction, block, piece],
            mine + way * pair,
        )

    def wide(value):
        return value.astype(jnp.float32)

    def combine(block, piece, way, from_line):
        give_copy(block, piece).wait_recv()
        value = wide(part[block, side, piece]) + wide(side_in[block, piece])
        if from_line:
            back_copy(block, piece, way).wait_recv()
            value = value + wide(line_in[(1 - way) // 2, block, piece])
        part[block, side, piece] = value.astype(part.dtype)
        back_copy(block, piece, way).start()

    greet(chips, pair, mine, spot, side)
    for piece in (PIECES, *range(PIECES)):
        for way in (1, -1):
            onward(None, piece, way, lambda copy: copy.start())
        side_copy(None, piece).start()
    keep = pltpu.make_async_copy(
        own_ref, rows_all.at[spot, pl.ds(pl.multiple_of(side * height, height), height)], own_sem.at[0]
    )
    keep.start()
    keep_small = pltpu.make_async_copy(small_ref, small_all.at[spot, side], own_sem.at[1])
    keep_small.start()
    for load in loads:
        load.start()
    keep.wait()
    keep_small.wait()
    for load in loads:
        load.wait()

    def visit(k, carry):
        block = visiting_order(k, spot, chips)
        way = jnp.where(block > spot, 1, -1)
        outward = at_end & (k > 0)
        for piece in range(PIECES + 1):
            side_copy(block, piece).wait_recv()
        values = rows_all[block]
        for e in range(local):
            chosen_expert = mine * local + e
            columns = []
            for core in range(pair):
                table = small_all[block, core]
                here = lax.broadcasted_iota(jnp.int32, table.shape, 0) == chosen_expert
                row = jnp.sum(jnp.where(here, table, 0.0), axis=0, keepdims=True)
                columns.append(jnp.broadcast_to(row, (height, height)).T[:, :1])
            share = jnp.concatenate(columns, axis=0)
            gated = lax.dot_general(values, gate[e], NT, preferred_element_type=jnp.float32)
            upped = lax.dot_general(values, up[e], NT, preferred_element_type=jnp.float32)
            hidden[e] = (gated * jax.nn.sigmoid(gated) * upped * share).astype(hidden.dtype)
        for piece in range(RETURN_PIECES):
            total = None
            for e in range(local):
                term = jnp.dot(
                    hidden[e],
                    down[e, :, piece * chunk : (piece + 1) * chunk],
                    preferred_element_type=jnp.float32,
                )
                total = term if total is None else total + term
            total = total.astype(part.dtype)
            for core in range(pair):
                part[block, core, piece] = total[core * height : (core + 1) * height]
            give_copy(block, piece).start()
            if piece > 0:

                @pl.when(outward)
                def _():
                    combine(block, piece - 1, way, False)

        @pl.when(outward)
        def _():
            combine(block, RETURN_PIECES - 1, way, False)

        @pl.when(k < chips - 1)
        def _():
            def receive(block, piece, way):
                line_copy(block, piece, way).wait_recv()
                onward(block, piece, way, lambda copy: copy.start())
                side_copy(block, piece).start()

            passing(k + 1, receive)

        return carry

    lax.fori_loop(0, chips, visit, 0)

    left_first = 2 * spot <= chips - 1

    def relay(a, carry):
        for piece in range(RETURN_PIECES):
            for turn in range(2):
                way = jnp.where(left_first, 1 - 2 * turn, 2 * turn - 1)
                block = jnp.where(way > 0, a, chips - 1 - a)
                valid = jnp.where(way > 0, block > spot, block < spot) & jnp.logical_not(at_end)

                @pl.when(valid)
                def _():
                    combine(block, piece, way, True)

        return carry

    lax.fori_loop(1, chips, relay, 0)
    for piece in range(RETURN_PIECES):
        give_copy(spot, piece).wait_recv()
        columns = pl.ds(piece * chunk, chunk)
        sum_ref[:, columns] = wide(part[spot, side, piece]) + wide(side_in[spot, piece])
        for way in (1, -1):

            @pl.when((spot > 0) if way > 0 else (spot < chips - 1))
            def _():
                back_copy(spot, piece, way).wait_recv()
                sum_ref[:, columns] += wide(line_in[(1 - way) // 2, spot, piece])

    for piece in range(PIECES + 1):
        for way in (1, -1):
            onward(None, piece, way, lambda copy: copy.wait_send())
        side_copy(None, piece).wait_send()

    def settle(far, carry):
        def sent(block, piece, way):
            onward(block, piece, way, lambda copy: copy.wait_send())
            side_copy(block, piece).wait_send()

        passing(far, sent)
        return carry

    lax.fori_loop(1, chips, settle, 0)

    def settle_back(block, carry):
        for piece in range(RETURN_PIECES):
            give_copy(block, piece).wait_send()

            @pl.when(block != spot)
            def _():
                back_copy(block, piece, jnp.where(block > spot, 1, -1)).wait_send()

        return carry

    lax.fori_loop(0, chips, settle_back, 0)


def experts(own, small, gate, up, down):
    count = lax.axis_size("expert")
    pair = 2
    chips = count // pair
    height, width = own.shape
    local, inner = down.shape[:2]
    kind = own.dtype
    chunk = width // RETURN_PIECES
    blocks = chips * pair * height * width * 2
    weights = 3 * local * inner * width * 2
    dma = pltpu.SemaphoreType.DMA
    hbm = pl.BlockSpec(memory_space=pl.ANY)
    vmem = pl.BlockSpec(memory_space=pltpu.VMEM)
    return pl.pallas_call(
        experts_kernel,
        out_shape=jax.ShapeDtypeStruct((height, width), jnp.float32),
        in_specs=[vmem, vmem, hbm, hbm, hbm],
        out_specs=vmem,
        scratch_shapes=[
            pltpu.VMEM((local, inner, width), kind),
            pltpu.VMEM((local, inner, width), kind),
            pltpu.VMEM((local, inner, width), kind),
            pltpu.VMEM((chips, pair * height, width), kind),
            pltpu.VMEM((chips, pair) + small.shape, small.dtype),
            pltpu.VMEM((local, pair * height, inner), kind),
            pltpu.VMEM((chips, pair, RETURN_PIECES, height, chunk), kind),
            pltpu.VMEM((chips, RETURN_PIECES, height, chunk), kind),
            pltpu.VMEM((2, chips, RETURN_PIECES, height, chunk), kind),
            dma((2,)),
            dma((3, local)),
            dma((2, chips, PIECES + 1)),
            dma((chips, PIECES + 1)),
            dma((chips, PIECES + 1)),
            dma((chips, PIECES + 1)),
            dma((chips, RETURN_PIECES)),
            dma((chips, RETURN_PIECES)),
            dma((chips, RETURN_PIECES)),
            dma((2, chips, RETURN_PIECES)),
        ],
        compiler_params=pltpu.CompilerParams(
            collective_id=0, has_side_effects=True, vmem_limit_bytes=4 * blocks + weights + 12 * 2**20
        ),
        cost_estimate=pl.CostEstimate(
            flops=2 * weights * blocks // (width * 4), bytes_accessed=32 * blocks, transcendentals=0
        ),
    )(own, small, gate, up, down)


HALVES = 2


def relay_kernel(
    lengths,
    shares_ref,
    mixing_gain,
    latent_gain,
    expert_gain,
    opening_hbm,
    incoming_hbm,
    stored_hbm,
    asking_hbm,
    compress_hbm,
    lookup_hbm,
    content_hbm,
    merging_hbm,
    gate_hbm,
    up_hbm,
    down_hbm,
    out_hbm,
    asking,
    compress,
    lookup,
    content,
    merging,
    gate,
    up,
    down,
    keys,
    inputs,
    residual,
    q_lat,
    rows_all,
    small_all,
    hidden,
    part,
    side_in,
    line_in,
    results,
    input_sem,
    load_sem,
    gate_sem,
    key_sem,
    out_sem,
    small_sem,
    line_send,
    line_recv,
    side_send,
    side_recv,
    small_line_send,
    small_line_recv,
    small_side_send,
    small_side_recv,
    give_send,
    give_recv,
    back_send,
    back_recv,
    hop_send,
    hop_recv,
):
    chips, pair, mine, spot, side = place_on_line()
    section = lax.axis_index("section")
    sections = lax.axis_size("section")
    ticks, _, height, width = inputs.shape
    local = gate.shape[0]
    heads, head_size, latent = lookup.shape
    context = keys.shape[1] - HALVES * height
    chunk = width // RETURN_PIECES
    step = height // PIECES
    sibling = mine + 1 - 2 * side
    at_end = (spot == 0) | (spot == chips - 1)
    kind = rows_all.dtype

    def wide(value):
        return value.astype(jnp.float32)

    def local_copy(source, target, sem):
        return pltpu.make_async_copy(source, target, sem)

    def input_copy(t, half):
        source = opening_hbm.at[half] if t == 0 else incoming_hbm.at[t - 1, half]
        return local_copy(source, inputs.at[t, half], input_sem.at[t, half])

    def key_copy(t):
        return local_copy(stored_hbm.at[t], keys.at[t, pl.ds(0, context)], key_sem.at[t])

    attention_loads = [
        local_copy(source, target, load_sem.at[index])
        for index, (source, target) in enumerate(
            (
                (asking_hbm, asking),
                (compress_hbm, compress),
                (lookup_hbm, lookup),
                (content_hbm, content),
                (merging_hbm, merging),
            )
        )
    ]
    expert_loads = [
        local_copy(source.at[e], target.at[e], gate_sem.at[index, e])
        for e in range(local)
        for index, (source, target) in enumerate(((gate_hbm, gate), (up_hbm, up), (down_hbm, down)))
    ]

    def reach(way):
        return (spot < chips - 1) if way > 0 else (spot > 0)

    def rows(t, block, half, piece):
        first = pl.multiple_of(side * height + piece * step, step)
        return rows_all.at[t, block, half, pl.ds(first, step)]

    def line_copy(t, block, half, piece, way):
        direction = 0 if way > 0 else 1
        place = rows(t, block, half, piece)
        return remote(
            place,
            place,
            line_send.at[direction, block, half, piece],
            line_recv.at[t, block, half, piece],
            mine + way * pair,
        )

    def side_copy(t, block, half, piece):
        place = rows(t, block, half, piece)
        return remote(
            place,
            place,
            side_send.at[block, half, piece],
            side_recv.at[t, block, half, piece],
            sibling,
        )

    def small_line_copy(block, way):
        direction = 0 if way > 0 else 1
        source = shares_ref if block is None else small_all.at[block, side]
        where = spot if block is None else block
        return remote(
            source,
            small_all.at[where, side],
            small_line_send.at[direction, where],
            small_line_recv.at[where],
            mine + way * pair,
        )

    def small_side_copy(block):
        source = shares_ref if block is None else small_all.at[block, side]
        where = spot if block is None else block
        return remote(
            source,
            small_all.at[where, side],
            small_side_send.at[where],
            small_side_recv.at[where],
            sibling,
        )

    def give_copy(block, half, piece):
        return remote(
            part.at[block, half, 1 - side, piece],
            side_in.at[block, half, piece],
            give_send.at[block, half, piece],
            give_recv.at[block, half, piece],
            sibling,
        )

    def back_copy(block, half, piece, way, sender):
        slot = jnp.where((block == sender + way) & (way < 0), chips, block)
        return remote(
            part.at[block, half, side, piece],
            line_in.at[slot, half, piece],
            back_send.at[block, half, piece],
            back_recv.at[slot, half, piece],
            mine + way * pair,
        )

    def combine(block, half, piece, way, from_line):
        give_copy(block, half, piece).wait_recv()
        value = wide(part[block, half, side, piece]) + wide(side_in[block, half, piece])
        if from_line:
            back_copy(block, half, piece, way, spot - way).wait_recv()
            value = value + wide(line_in[block, half, piece])
        part[block, half, side, piece] = value.astype(part.dtype)
        back_copy(block, half, piece, way, spot).start()

    def hop_copy(t, half, piece):
        columns = pl.ds(piece * chunk, chunk)
        return pltpu.make_async_remote_copy(
            src_ref=results.at[t, half, :, columns],
            dst_ref=inputs.at[t + 1, half, :, columns],
            send_sem=hop_send.at[half, piece],
            recv_sem=hop_recv.at[t + 1, half, piece],
            device_id={"section": section + 1},
            device_id_type=MESH,
        )

    def stream(way, unit, blocks):
        first = unit < blocks
        near = spot - way * (1 + unit)
        back = unit - blocks
        far = back if way > 0 else chips - 1 - back
        return jnp.where(first, near, far), jnp.where(first, 0, 1)

    def upstream(way):
        return spot if way > 0 else chips - 1 - spot

    def send_own(t, half, way):
        for piece in range(PIECES):

            @pl.when(reach(way))
            def _():
                line_copy(t, spot, half, piece, way).start()

    def arrive(t, way, j):
        blocks = upstream(way)
        block, half = stream(way, lax.div(j, PIECES), blocks)
        piece = lax.rem(j, PIECES)
        line_copy(t, block, half, piece, way).wait_recv()

        @pl.when(reach(way))
        def _():
            line_copy(t, block, half, piece, way).start()

        side_copy(t, block, half, piece).start()

        @pl.when(j == 2 * blocks * PIECES - 1)
        def _():
            send_own(t, 1, way)

    def send_back(way, v):
        ahead = upstream(-way)
        block, half = stream(-way, lax.div(v, RETURN_PIECES), ahead)
        combine(block, half, lax.rem(v, RETURN_PIECES), way, True)

    def normed(values, gain):
        mean = jnp.mean(values * values, axis=-1, keepdims=True)
        return (values * lax.rsqrt(mean + epsilon) * gain).astype(kind)

    def project(t):
        values = inputs[t].reshape(HALVES * height, width)
        rows_in = normed(wide(values), mixing_gain[...])
        queries = jnp.dot(rows_in, asking[...], preferred_element_type=jnp.float32).astype(kind)
        raw = jnp.dot(rows_in, compress[...], preferred_element_type=jnp.float32)
        keys[t, context:] = normed(raw, latent_gain[...])
        for head in range(heads):
            part_of = queries[:, head * head_size : (head + 1) * head_size]
            lat = jnp.dot(part_of, lookup[head], preferred_element_type=jnp.float32).astype(kind)
            for half in range(HALVES):
                q_lat[half, head * height : (head + 1) * height] = lat[
                    half * height : (half + 1) * height
                ]

    def attend_half(t, half):
        table = keys[t]
        scores = lax.dot_general(q_lat[half], table, NT, preferred_element_type=jnp.float32)
        scores = scores * head_size ** (-0.5)
        position = lax.broadcasted_iota(jnp.int32, (height, table.shape[0]), 1)
        query = lax.broadcasted_iota(jnp.int32, (height, table.shape[0]), 0) + half * height
        limit = jnp.where(position < context, lengths[t], query + (context + 1))
        visible = (position < limit)[None]
        scores = scores.reshape((heads,) + position.shape)
        scores = jnp.where(visible, scores, -jnp.inf).reshape(heads * height, -1)
        expd = jnp.exp(scores - jnp.max(scores, axis=-1, keepdims=True))
        weight = (expd * (1.0 / jnp.sum(expd, axis=-1, keepdims=True))).astype(kind)
        o_lat = jnp.dot(weight, table, preferred_element_type=jnp.float32).astype(kind)
        outs = []
        for head in range(heads):
            outs.append(
                jnp.dot(
                    o_lat[head * height : (head + 1) * height],
                    content[head],
                    preferred_element_type=jnp.float32,
                ).astype(kind)
            )
        heads_out = jnp.concatenate(outs, axis=1)
        total = wide(inputs[t, half]) + jnp.dot(
            heads_out, merging[...], preferred_element_type=jnp.float32
        )
        residual[half] = total
        first = pl.multiple_of(side * height, height)
        rows_all[t, spot, half, pl.ds(first, height)] = normed(total, expert_gain[...])

    def pass_small(far):
        for way in (1, -1):
            block = spot - way * far

            @pl.when((block >= 0) if way > 0 else (block < chips))
            def _():
                small_line_copy(block, way).wait_recv()

                @pl.when(reach(way))
                def _():
                    small_line_copy(block, way).start()

                small_side_copy(block).start()

    def poll(t, counts):
        after = []
        for way, count in zip((1, -1), counts):
            total = 2 * upstream(way) * PIECES

            @pl.when(count < total)
            def _():
                arrive(t, way, count)

            after.append(jnp.minimum(count + 1, total))
        return tuple(after)

    def catch_up(t, way, count, goal):
        def one(j, carry):
            arrive(t, way, j)
            return carry

        lax.fori_loop(count, goal, one, 0)

    units = 2 * chips
    short = 2 * jnp.minimum(spot, chips - 1 - spot)
    leftward = spot > chips - 1 - spot

    def unit_of(k):
        paired = k < 2 * short
        unit = jnp.where(paired, lax.div(k, 2), k - short)
        from_left = jnp.where(paired, lax.rem(k, 2) == 0, leftward)
        left_block, left_half = stream(1, unit, upstream(1))
        right_block, right_half = stream(-1, unit, upstream(-1))
        own = k >= units - 2
        block = jnp.where(own, spot, jnp.where(from_left, left_block, right_block))
        half = jnp.where(own, k - units + 2, jnp.where(from_left, left_half, right_half))
        need = jnp.where(own, 0, (unit + 1) * PIECES)
        return block, half, jnp.where(from_left, need, 0), jnp.where(from_left, 0, need)

    def visit(t, k, carry):
        counts, sent = carry[:2], carry[2:]
        block, half, _, _ = unit_of(k)
        way = jnp.where(block > spot, 1, -1)
        outward = at_end & (block != spot)
        for piece in range(PIECES):
            side_copy(t, block, half, piece).wait_recv()
        values = rows_all[t, block, half]
        for e in range(local):
            line = mine * local + e + t * (small_all.shape[2] // ticks)
            columns = []
            for core in range(pair):
                table = small_all[block, core]
                here = lax.broadcasted_iota(jnp.int32, table.shape, 0) == line
                row = jnp.sum(jnp.where(here, table, 0.0), axis=0, keepdims=True)
                column = jnp.broadcast_to(row, (row.shape[1], row.shape[1])).T[:, :1]
                columns.append(jnp.where(half == 0, column[:height], column[height:]))
            share = jnp.concatenate(columns, axis=0)
            gated = lax.dot_general(values, gate[e], NT, preferred_element_type=jnp.float32)
            upped = lax.dot_general(values, up[e], NT, preferred_element_type=jnp.float32)
            hidden[e] = (gated * jax.nn.sigmoid(gated) * upped * share).astype(kind)
            counts = poll(t, counts)
        for piece in range(RETURN_PIECES):
            total = None
            for e in range(local):
                term = jnp.dot(
                    hidden[e],
                    down[e, :, piece * chunk : (piece + 1) * chunk],
                    preferred_element_type=jnp.float32,
                )
                total = term if total is None else total + term
            total = total.astype(part.dtype)
            for core in range(pair):
                part[block, half, core, piece] = total[core * height : (core + 1) * height]
            give_copy(block, half, piece).start()
            if piece > 0:

                @pl.when(outward)
                def _():
                    combine(block, half, piece - 1, way, False)

        @pl.when(outward)
        def _():
            combine(block, half, RETURN_PIECES - 1, way, False)

        counts = poll(t, counts)
        after = []
        for direction, count in zip((1, -1), sent):
            done = back_goal(direction, k)
            goal = jnp.maximum(count, done)
            return_up(direction, count, goal)
            after.append(goal)
        needs = unit_of(jnp.minimum(k + 1, units - 1))[2:]
        ready = []
        for direction, count, need in zip((1, -1), counts, needs):
            goal = jnp.maximum(count, need)
            catch_up(t, direction, count, goal)
            ready.append(goal)
        return (*ready, *after)

    def back_total(way):
        ahead = jnp.where(at_end, 0, upstream(-way))
        return 2 * ahead * RETURN_PIECES

    def back_goal(way, k):
        due = lax.div(jnp.maximum(14 * k - 29 * upstream(way), 0), 5)
        return jnp.minimum(due, back_total(way))

    def return_up(way, count, goal):
        def one(v, carry):
            send_back(way, v)
            return carry

        lax.fori_loop(count, goal, one, 0)

    def finish(t, half):
        for piece in range(RETURN_PIECES):
            columns = pl.ds(piece * chunk, chunk)
            give_copy(spot, half, piece).wait_recv()
            residual[half, :, columns] += wide(part[spot, half, side, piece]) + wide(
                side_in[spot, half, piece]
            )
            for way in (1, -1):

                @pl.when(reach(-way))
                def _():
                    back_copy(spot, half, piece, way, spot - way).wait_recv()
                    slot = spot if way > 0 else chips
                    residual[half, :, columns] += wide(line_in[slot, half, piece])

            results[t, half, :, columns] = residual[half, :, columns].astype(kind)

            @pl.when((section < sections - 1) & (t < ticks - 1))
            def _():
                hop_copy(t, half, piece).start()

        local_copy(results.at[t, half], out_hbm.at[t, half], out_sem.at[t, half]).start()

    barrier = pltpu.get_barrier_semaphore()

    def hello(condition, device):
        @pl.when(condition)
        def _():
            pl.semaphore_signal(barrier, inc=1, device_id=device, device_id_type=MESH)

    for half in range(HALVES):
        input_copy(0, half).start()
    for load in attention_loads[:3]:
        load.start()
    key_copy(0).start()
    for load in attention_loads[3:]:
        load.start()
    for load in expert_loads:
        load.start()
    keep_small = local_copy(shares_ref, small_all.at[spot, side], small_sem.at[0])
    keep_small.start()
    for t in range(1, ticks):
        key_copy(t).start()

        @pl.when(section == 0)
        def _():
            for half in range(HALVES):
                input_copy(t, half).start()

    line_neighbours = jnp.where(at_end, 1, 2)
    section_neighbours = jnp.where((section == 0) | (section == sections - 1), 1, 2)
    hello(spot > 0, {"expert": mine - pair})
    hello(spot < chips - 1, {"expert": mine + pair})
    hello(section > 0, {"section": section - 1})
    hello(section < sections - 1, {"section": section + 1})
    pl.semaphore_signal(barrier, inc=1, device_id={"expert": sibling}, device_id_type=MESH)
    pl.semaphore_wait(barrier, 1 + line_neighbours + section_neighbours)

    for way in (1, -1):

        @pl.when(reach(way))
        def _():
            small_line_copy(None, way).start()

    small_side_copy(None).start()
    keep_small.wait()

    def tick(t, carry):
        for half in range(HALVES):

            @pl.when((t == 0) | (section == 0))
            def _():
                local_copy(opening_hbm.at[half], inputs.at[t, half], input_sem.at[t, half]).wait()

            @pl.when((t > 0) & (section > 0))
            def _():
                for piece in range(RETURN_PIECES):
                    hop_copy(t - 1, half, piece).wait_recv()

        @pl.when(t == 0)
        def _():
            for load in attention_loads[:3]:
                load.wait()

        project(t)
        key_copy(t).wait()

        @pl.when(t == 0)
        def _():
            for load in attention_loads[3:]:
                load.wait()
            if chips > 1:
                pass_small(1)

        for half in range(HALVES):
            attend_half(t, half)
            for piece in range(PIECES):
                side_copy(t, spot, half, piece).start()
            for way in (1, -1):
                if half == 0:
                    send_own(t, half, way)
                else:

                    @pl.when(upstream(way) == 0)
                    def _():
                        send_own(t, half, way)

            if half == 0:

                @pl.when(t == 0)
                def _():
                    for far in range(2, chips):
                        pass_small(far)

        @pl.when(t == 0)
        def _():
            for load in expert_loads:
                load.wait()
            small_side_copy(None).wait_recv()
            for far in range(1, chips):
                for way in (1, -1):
                    block = spot - way * far

                    @pl.when((block >= 0) if way > 0 else (block < chips))
                    def _():
                        small_side_copy(block).wait_recv()

        start = []
        for way in (1, -1):
            goal = jnp.minimum(2 * upstream(way) * PIECES, PIECES)
            catch_up(t, way, 0, goal)
            start.append(goal)
        none = jnp.int32(0)
        state = lax.fori_loop(
            0, units, lambda k, state: visit(t, k, state), (*start, none, none)
        )
        finish(t, 0)

        def rest(v, carry):
            for way, done in zip((1, -1), state[2:]):

                @pl.when(done + v < back_total(way))
                def _():
                    send_back(way, done + v)

            return carry

        left_over = [back_total(way) - done for way, done in zip((1, -1), state[2:])]
        lax.fori_loop(0, jnp.maximum(left_over[0], left_over[1]), rest, 0)
        finish(t, 1)

        def settle(block, inner):
            for half in range(HALVES):
                for piece in range(PIECES):
                    for way in (1, -1):
                        passes = (block <= spot) if way > 0 else (block >= spot)

                        @pl.when(passes & reach(way))
                        def _():
                            line_copy(t, block, half, piece, way).wait_send()

                    side_copy(t, block, half, piece).wait_send()
                for piece in range(RETURN_PIECES):
                    give_copy(block, half, piece).wait_send()

                    @pl.when(block != spot)
                    def _():
                        back_copy(
                            block, half, piece, jnp.where(block > spot, 1, -1), spot
                        ).wait_send()

            return inner

        lax.fori_loop(0, chips, settle, 0)

        @pl.when((section < sections - 1) & (t < ticks - 1))
        def _():
            for half in range(HALVES):
                for piece in range(RETURN_PIECES):
                    hop_copy(t, half, piece).wait_send()

        return carry

    lax.fori_loop(0, ticks, tick, 0)

    def settle_small(block, carry):
        for way in (1, -1):
            passes = (block <= spot) if way > 0 else (block >= spot)

            @pl.when(passes & reach(way))
            def _():
                small_line_copy(block, way).wait_send()

        small_side_copy(block).wait_send()
        return carry

    lax.fori_loop(0, chips, settle_small, 0)
    for t in range(ticks):
        for half in range(HALVES):
            local_copy(results.at[t, half], out_hbm.at[t, half], out_sem.at[t, half]).wait()


def relay(
    lengths,
    shares,
    mixing_gain,
    latent_gain,
    expert_gain,
    opening,
    incoming,
    stored,
    asking,
    compress,
    lookup,
    content,
    merging,
    gate,
    up,
    down,
):
    count = lax.axis_size("expert")
    pair = 2
    chips = count // pair
    ticks, context, latent = stored.shape
    kind = opening.dtype
    height = opening.shape[0] // HALVES
    width = opening.shape[1]
    local, inner = down.shape[:2]
    heads = lookup.shape[0]
    chunk = width // RETURN_PIECES
    dma = pltpu.SemaphoreType.DMA
    hbm = pl.BlockSpec(memory_space=pl.ANY)
    vmem = pl.BlockSpec(memory_space=pltpu.VMEM)
    smem = pl.BlockSpec(memory_space=pltpu.SMEM)
    cut = (HALVES, height, width)
    out = pl.pallas_call(
        relay_kernel,
        out_shape=jax.ShapeDtypeStruct((ticks,) + cut, kind),
        in_specs=[smem] + [vmem] * 4 + [hbm] * 11,
        out_specs=hbm,
        scratch_shapes=[
            *[pltpu.VMEM(w.shape, kind) for w in (asking, compress, lookup, content, merging)],
            *[pltpu.VMEM((local, inner, width), kind) for _ in range(3)],
            pltpu.VMEM((ticks, context + HALVES * height, latent), kind),
            pltpu.VMEM((ticks,) + cut, kind),
            pltpu.VMEM(cut, jnp.float32),
            pltpu.VMEM((HALVES, heads * height, latent), kind),
            pltpu.VMEM((ticks, chips, HALVES, pair * height, width), kind),
            pltpu.VMEM((chips, pair) + shares.shape, shares.dtype),
            pltpu.VMEM((local, pair * height, inner), kind),
            pltpu.VMEM((chips, HALVES, pair, RETURN_PIECES, height, chunk), kind),
            pltpu.VMEM((chips, HALVES, RETURN_PIECES, height, chunk), kind),
            pltpu.VMEM((chips + 1, HALVES, RETURN_PIECES, height, chunk), kind),
            pltpu.VMEM((ticks,) + cut, kind),
            dma((ticks, HALVES)),
            dma((5,)),
            dma((3, local)),
            dma((ticks,)),
            dma((ticks, HALVES)),
            dma((1,)),
            dma((2, chips, HALVES, PIECES)),
            dma((ticks, chips, HALVES, PIECES)),
            dma((chips, HALVES, PIECES)),
            dma((ticks, chips, HALVES, PIECES)),
            dma((2, chips)),
            dma((chips,)),
            dma((chips,)),
            dma((chips,)),
            dma((chips, HALVES, RETURN_PIECES)),
            dma((chips, HALVES, RETURN_PIECES)),
            dma((chips, HALVES, RETURN_PIECES)),
            dma((chips + 1, HALVES, RETURN_PIECES)),
            dma((HALVES, RETURN_PIECES)),
            dma((ticks, HALVES, RETURN_PIECES)),
        ],
        compiler_params=pltpu.CompilerParams(
            collective_id=0, has_side_effects=True, vmem_limit_bytes=63 * 2**20
        ),
    )(
        lengths,
        shares,
        mixing_gain,
        latent_gain,
        expert_gain,
        opening.reshape(cut),
        incoming.reshape((ticks - 1,) + cut),
        stored,
        asking,
        compress,
        lookup,
        content,
        merging,
        gate,
        up,
        down,
    )
    return out.reshape(ticks, HALVES * height, width)


def shifted(value, axis, steps):
    count = lax.axis_size(axis)
    initial, last = (max(0, -steps), min(count, count - steps))
    return lax.ppermute(value, axis, [(source, source + steps) for source in range(initial, last)])


def row_norm(values, gain_row):
    return (
        values * lax.rsqrt(jnp.mean(values * values, axis=-1, keepdims=True) + epsilon) * gain_row
    )


def attend(q_lat, cache_rows, new_rows, length, score_scale):
    piece_list = q_lat.shape[0]
    context = cache_rows.shape[0]
    key_rows = jnp.concatenate([cache_rows, new_rows], axis=0)
    scores = (
        jnp.einsum("thl,kl->thk", q_lat, key_rows, preferred_element_type=jnp.float32) * score_scale
    )
    position = lax.broadcasted_iota(jnp.int32, (piece_list, context + piece_list), 1)
    query_pos = lax.broadcasted_iota(jnp.int32, (piece_list, context + piece_list), 0)
    visible = jnp.where(position < context, position < length, position - context <= query_pos)
    scores = jnp.where(visible[:, None, :], scores, -jnp.inf)
    row_max = jnp.max(scores, axis=-1, keepdims=True)
    expd = jnp.where(visible[:, None, :], jnp.exp(scores - row_max), 0.0)
    attention = (expd / jnp.sum(expd, axis=-1, keepdims=True)).astype(jnp.bfloat16)
    return jnp.einsum(
        "thk,kl->thl", attention, key_rows, preferred_element_type=jnp.float32
    ).astype(jnp.bfloat16)


def shards(
    opening_residual,
    incoming_residual,
    stored_summaries,
    stored_counts,
    picked_specialists,
    chooser_mixing_share,
    mixing_scale_factor,
    asking_projection,
    summary_lookup_factor,
    summary_content_factor,
    merging_projection,
    compress_projection,
    summary_scale_factor,
    specialist_scale_factor,
    specialist_switch_factor,
    specialist_widen_factor,
    specialist_contract_factor,
):
    segment_ordinal = lax.axis_index("section")
    section_count = lax.axis_size("section")
    sources = lax.axis_size("expert")
    tick_count = stored_summaries.shape[0]
    piece_list = opening_residual.shape[1]
    inner_feature_midcount = opening_residual.shape[2]
    full_width = mixing_scale_factor.shape[1]
    local_heads = summary_lookup_factor.shape[1]
    head_size = summary_lookup_factor.shape[2]
    top_count = picked_specialists.shape[3]
    expert_local = specialist_switch_factor.shape[1]
    score_scale = head_size ** (-0.5)
    expert_ids = lax.broadcasted_iota(jnp.int32, (1, 1, 1, expert_local * sources), 3)
    shares_dense = jnp.sum(
        jnp.where(
            picked_specialists[:, 0][..., None] == expert_ids,
            chooser_mixing_share[:, 0][..., None],
            0.0,
        ),
        axis=2,
    )
    shares_dense = jnp.swapaxes(shares_dense, 1, 2)
    if lax.axis_size("tensor") == 1 and sources % 2 == 0 and section_count > 1 and tick_count > 1:
        turns = jnp.arange(tick_count) - segment_ordinal + section_count - 1
        routed_results = relay(
            stored_counts[:, 0][turns],
            shares_dense.reshape(tick_count * shares_dense.shape[1], piece_list),
            mixing_scale_factor,
            summary_scale_factor,
            specialist_scale_factor,
            opening_residual[0],
            incoming_residual,
            stored_summaries[:, 0, 0],
            asking_projection[0],
            compress_projection[0],
            summary_lookup_factor[0],
            summary_content_factor[0],
            merging_projection[0],
            jnp.swapaxes(specialist_switch_factor[0], 1, 2),
            jnp.swapaxes(specialist_widen_factor[0], 1, 2),
            specialist_contract_factor[0],
        )
        return routed_results[:, None]
    outputs = []
    present_carry = opening_residual[0]
    section_out = present_carry
    for step_index in range(tick_count):
        if step_index > 0:
            handed = shifted(section_out, "section", 1)
            present_carry = jnp.where(
                segment_ordinal == 0, incoming_residual[step_index - 1], handed
            )
        micro_index = step_index - segment_ordinal + section_count - 1
        length = lax.dynamic_index_in_dim(stored_counts[:, 0], micro_index, 0, keepdims=False)
        full_rows = lax.all_gather(present_carry, "tensor", axis=1, tiled=True)
        normed = row_norm(full_rows.astype(jnp.float32), mixing_scale_factor[0]).astype(
            jnp.bfloat16
        )
        queries = jnp.dot(normed, asking_projection[0], preferred_element_type=jnp.float32).astype(
            jnp.bfloat16
        )
        queries = queries.reshape(piece_list, local_heads, head_size)
        q_lat = jnp.einsum(
            "thd,hdl->thl", queries, summary_lookup_factor[0], preferred_element_type=jnp.float32
        ).astype(jnp.bfloat16)
        latent_part = jnp.dot(normed, compress_projection[0], preferred_element_type=jnp.float32)
        latent_raw = lax.all_gather(
            latent_part.astype(jnp.bfloat16), "tensor", axis=1, tiled=True
        ).astype(latent_part.dtype)
        new_latent = row_norm(latent_raw, summary_scale_factor[0]).astype(jnp.bfloat16)
        o_lat = attend(q_lat, stored_summaries[step_index, 0, 0], new_latent, length, score_scale)
        heads_out = jnp.einsum(
            "thl,hld->thd", o_lat, summary_content_factor[0], preferred_element_type=jnp.float32
        ).astype(jnp.bfloat16)
        heads_out = heads_out.reshape(piece_list, local_heads * head_size)
        head_terms = jnp.dot(heads_out, merging_projection[0], preferred_element_type=jnp.float32)
        residual = present_carry.astype(jnp.float32) + lax.psum_scatter(
            head_terms.astype(jnp.bfloat16), "tensor", scatter_dimension=1, tiled=True
        ).astype(jnp.float32)
        squares = lax.psum(jnp.sum(residual * residual, axis=1), "tensor")
        moe_input = (
            residual
            * lax.rsqrt(squares / full_width + epsilon)[:, None]
            * specialist_scale_factor[0]
        ).astype(jnp.bfloat16)
        whole_rows = lax.all_gather(moe_input, "tensor", axis=1, tiled=True)
        routed = experts(
            whole_rows,
            shares_dense[step_index],
            jnp.swapaxes(specialist_switch_factor[0], 1, 2),
            jnp.swapaxes(specialist_widen_factor[0], 1, 2),
            specialist_contract_factor[0],
        )
        if lax.axis_size("tensor") > 1:
            routed = lax.psum_scatter(
                routed.astype(jnp.bfloat16), "tensor", scatter_dimension=1, tiled=True
            ).astype(jnp.float32)
        section_out = (residual + routed).astype(jnp.bfloat16)
        outputs.append(section_out)
    return jnp.stack(outputs)[:, None]


def solution(mesh):
    in_specs = (
        P("section", ("groups", "expert"), "tensor"),
        P(None, ("groups", "expert"), "tensor"),
        P(None, "section", ("groups", "expert"), None, None),
        P(None, ("groups", "expert")),
        P(None, "section", ("groups", "expert"), None),
        P(None, "section", ("groups", "expert"), None),
        P("section", None),
        P("section", None, "tensor"),
        P("section", "tensor", None, None),
        P("section", "tensor", None, None),
        P("section", "tensor", None),
        P("section", None, "tensor"),
        P("section", None),
        P("section", "tensor"),
        P("section", "expert", None, "tensor"),
        P("section", "expert", None, "tensor"),
        P("section", "expert", "tensor", None),
    )
    out_specs = P(None, "section", ("groups", "expert"), "tensor")
    return jax.shard_map(shards, mesh=mesh, in_specs=in_specs, out_specs=out_specs, check_vma=False)
```

```python
import functools

import jax
import jax.numpy as jnp
from jax import lax
from jax.experimental import pallas as pl
from jax.experimental.pallas import tpu as pltpu
from jax.sharding import PartitionSpec as P


epsilon = 1e-06


MESH = pl.DeviceIdType.MESH
PIECES = 4
RETURN_PIECES = 4
NT = (((1,), (1,)), ((), ()))


def place_on_line():
    count = lax.axis_size("expert")
    pair = 2 if count % 2 == 0 else 1
    mine = lax.axis_index("expert")
    return count // pair, pair, mine, mine // pair, lax.rem(mine, pair)


def greet(chips, pair, mine, spot, side):
    barrier = pltpu.get_barrier_semaphore()

    def hello(other):
        pl.semaphore_signal(barrier, inc=1, device_id={"expert": other}, device_id_type=MESH)

    @pl.when(spot > 0)
    def _():
        hello(mine - pair)

    @pl.when(spot < chips - 1)
    def _():
        hello(mine + pair)

    if pair == 2:
        hello(mine + 1 - 2 * side)
    inner = (spot > 0) & (spot < chips - 1)

    @pl.when(inner)
    def _():
        pl.semaphore_wait(barrier, pair + 1)

    @pl.when(jnp.logical_not(inner))
    def _():
        pl.semaphore_wait(barrier, pair)


def remote(src, dst, send, recv, other):
    return pltpu.make_async_remote_copy(
        src_ref=src,
        dst_ref=dst,
        send_sem=send,
        recv_sem=recv,
        device_id={"expert": other},
        device_id_type=MESH,
    )


def visiting_order(k, spot, chips):
    low = jnp.minimum(spot, chips - 1 - spot)
    near = (k + 1) // 2
    around = spot + jnp.where(lax.rem(k, 2) == 0, near, -near)
    rest = jnp.where(spot < chips - 1 - spot, k, chips - 1 - k)
    return jnp.where(k <= 2 * low, around, rest)


def experts_kernel(
    own_ref,
    small_ref,
    gate_hbm,
    up_hbm,
    down_hbm,
    sum_ref,
    gate,
    up,
    down,
    rows_all,
    small_all,
    hidden,
    part,
    side_in,
    line_in,
    own_sem,
    weight_sem,
    line_send,
    line_recv,
    side_send,
    side_recv,
    give_send,
    give_recv,
    back_send,
    back_recv,
):
    chips, pair, mine, spot, side = place_on_line()
    height, width = own_ref.shape
    local = gate.shape[0]
    step = height // PIECES
    chunk = width // RETURN_PIECES
    sibling = mine + 1 - 2 * side
    at_end = (spot == 0) | (spot == chips - 1)

    loads = []
    for index, (source, target) in enumerate(((gate_hbm, gate), (up_hbm, up), (down_hbm, down))):
        for e in range(local):
            loads.append(
                pltpu.make_async_copy(source.at[e], target.at[e], weight_sem.at[index, e])
            )

    def rows(block, core, piece):
        if piece == PIECES:
            return small_all.at[block, core]
        first = pl.multiple_of(core * height + piece * step, step)
        return rows_all.at[block, pl.ds(first, step)]

    def origin(block, piece):
        if block is not None:
            return rows(block, side, piece)
        return small_ref if piece == PIECES else own_ref.at[pl.ds(piece * step, step)]

    def line_copy(block, piece, way):
        where = spot if block is None else block
        direction = 0 if way > 0 else 1
        return remote(
            origin(block, piece),
            rows(where, side, piece),
            line_send.at[direction, where, piece],
            line_recv.at[where, piece],
            mine + way * pair,
        )

    def side_copy(block, piece):
        where = spot if block is None else block
        return remote(
            origin(block, piece),
            rows(where, side, piece),
            side_send.at[where, piece],
            side_recv.at[where, piece],
            sibling,
        )

    def onward(block, piece, way, act):
        @pl.when((spot < chips - 1) if way > 0 else (spot > 0))
        def _():
            act(line_copy(block, piece, way))

    def passing(far, act):
        for piece in range(PIECES + 1):
            for way in (1, -1):
                block = spot - way * far

                @pl.when((block >= 0) if way > 0 else (block < chips))
                def _():
                    act(block, piece, way)

    def give_copy(block, piece):
        return remote(
            part.at[block, 1 - side, piece],
            side_in.at[block, piece],
            give_send.at[block, piece],
            give_recv.at[block, piece],
            sibling,
        )

    def back_copy(block, piece, way):
        direction = (1 - way) // 2
        return remote(
            part.at[block, side, piece],
            line_in.at[direction, block, piece],
            back_send.at[block, piece],
            back_recv.at[direction, block, piece],
            mine + way * pair,
        )

    def wide(value):
        return value.astype(jnp.float32)

    def combine(block, piece, way, from_line):
        give_copy(block, piece).wait_recv()
        value = wide(part[block, side, piece]) + wide(side_in[block, piece])
        if from_line:
            back_copy(block, piece, way).wait_recv()
            value = value + wide(line_in[(1 - way) // 2, block, piece])
        part[block, side, piece] = value.astype(part.dtype)
        back_copy(block, piece, way).start()

    greet(chips, pair, mine, spot, side)
    for piece in (PIECES, *range(PIECES)):
        for way in (1, -1):
            onward(None, piece, way, lambda copy: copy.start())
        side_copy(None, piece).start()
    keep = pltpu.make_async_copy(
        own_ref, rows_all.at[spot, pl.ds(pl.multiple_of(side * height, height), height)], own_sem.at[0]
    )
    keep.start()
    keep_small = pltpu.make_async_copy(small_ref, small_all.at[spot, side], own_sem.at[1])
    keep_small.start()
    for load in loads:
        load.start()
    keep.wait()
    keep_small.wait()
    for load in loads:
        load.wait()

    def visit(k, carry):
        block = visiting_order(k, spot, chips)
        way = jnp.where(block > spot, 1, -1)
        outward = at_end & (k > 0)
        for piece in range(PIECES + 1):
            side_copy(block, piece).wait_recv()
        values = rows_all[block]
        for e in range(local):
            chosen_expert = mine * local + e
            columns = []
            for core in range(pair):
                table = small_all[block, core]
                here = lax.broadcasted_iota(jnp.int32, table.shape, 0) == chosen_expert
                row = jnp.sum(jnp.where(here, table, 0.0), axis=0, keepdims=True)
                columns.append(jnp.broadcast_to(row, (height, height)).T[:, :1])
            share = jnp.concatenate(columns, axis=0)
            gated = lax.dot_general(values, gate[e], NT, preferred_element_type=jnp.float32)
            upped = lax.dot_general(values, up[e], NT, preferred_element_type=jnp.float32)
            hidden[e] = (gated * jax.nn.sigmoid(gated) * upped * share).astype(hidden.dtype)
        for piece in range(RETURN_PIECES):
            total = None
            for e in range(local):
                term = jnp.dot(
                    hidden[e],
                    down[e, :, piece * chunk : (piece + 1) * chunk],
                    preferred_element_type=jnp.float32,
                )
                total = term if total is None else total + term
            total = total.astype(part.dtype)
            for core in range(pair):
                part[block, core, piece] = total[core * height : (core + 1) * height]
            give_copy(block, piece).start()
            if piece > 0:

                @pl.when(outward)
                def _():
                    combine(block, piece - 1, way, False)

        @pl.when(outward)
        def _():
            combine(block, RETURN_PIECES - 1, way, False)

        @pl.when(k < chips - 1)
        def _():
            def receive(block, piece, way):
                line_copy(block, piece, way).wait_recv()
                onward(block, piece, way, lambda copy: copy.start())
                side_copy(block, piece).start()

            passing(k + 1, receive)

        return carry

    lax.fori_loop(0, chips, visit, 0)

    left_first = 2 * spot <= chips - 1

    def relay(a, carry):
        for piece in range(RETURN_PIECES):
            for turn in range(2):
                way = jnp.where(left_first, 1 - 2 * turn, 2 * turn - 1)
                block = jnp.where(way > 0, a, chips - 1 - a)
                valid = jnp.where(way > 0, block > spot, block < spot) & jnp.logical_not(at_end)

                @pl.when(valid)
                def _():
                    combine(block, piece, way, True)

        return carry

    lax.fori_loop(1, chips, relay, 0)
    for piece in range(RETURN_PIECES):
        give_copy(spot, piece).wait_recv()
        columns = pl.ds(piece * chunk, chunk)
        sum_ref[:, columns] = wide(part[spot, side, piece]) + wide(side_in[spot, piece])
        for way in (1, -1):

            @pl.when((spot > 0) if way > 0 else (spot < chips - 1))
            def _():
                back_copy(spot, piece, way).wait_recv()
                sum_ref[:, columns] += wide(line_in[(1 - way) // 2, spot, piece])

    for piece in range(PIECES + 1):
        for way in (1, -1):
            onward(None, piece, way, lambda copy: copy.wait_send())
        side_copy(None, piece).wait_send()

    def settle(far, carry):
        def sent(block, piece, way):
            onward(block, piece, way, lambda copy: copy.wait_send())
            side_copy(block, piece).wait_send()

        passing(far, sent)
        return carry

    lax.fori_loop(1, chips, settle, 0)

    def settle_back(block, carry):
        for piece in range(RETURN_PIECES):
            give_copy(block, piece).wait_send()

            @pl.when(block != spot)
            def _():
                back_copy(block, piece, jnp.where(block > spot, 1, -1)).wait_send()

        return carry

    lax.fori_loop(0, chips, settle_back, 0)


def experts(own, small, gate, up, down):
    count = lax.axis_size("expert")
    pair = 2
    chips = count // pair
    height, width = own.shape
    local, inner = down.shape[:2]
    kind = own.dtype
    chunk = width // RETURN_PIECES
    blocks = chips * pair * height * width * 2
    weights = 3 * local * inner * width * 2
    dma = pltpu.SemaphoreType.DMA
    hbm = pl.BlockSpec(memory_space=pl.ANY)
    vmem = pl.BlockSpec(memory_space=pltpu.VMEM)
    return pl.pallas_call(
        experts_kernel,
        out_shape=jax.ShapeDtypeStruct((height, width), jnp.float32),
        in_specs=[vmem, vmem, hbm, hbm, hbm],
        out_specs=vmem,
        scratch_shapes=[
            pltpu.VMEM((local, inner, width), kind),
            pltpu.VMEM((local, inner, width), kind),
            pltpu.VMEM((local, inner, width), kind),
            pltpu.VMEM((chips, pair * height, width), kind),
            pltpu.VMEM((chips, pair) + small.shape, small.dtype),
            pltpu.VMEM((local, pair * height, inner), kind),
            pltpu.VMEM((chips, pair, RETURN_PIECES, height, chunk), kind),
            pltpu.VMEM((chips, RETURN_PIECES, height, chunk), kind),
            pltpu.VMEM((2, chips, RETURN_PIECES, height, chunk), kind),
            dma((2,)),
            dma((3, local)),
            dma((2, chips, PIECES + 1)),
            dma((chips, PIECES + 1)),
            dma((chips, PIECES + 1)),
            dma((chips, PIECES + 1)),
            dma((chips, RETURN_PIECES)),
            dma((chips, RETURN_PIECES)),
            dma((chips, RETURN_PIECES)),
            dma((2, chips, RETURN_PIECES)),
        ],
        compiler_params=pltpu.CompilerParams(
            collective_id=0, has_side_effects=True, vmem_limit_bytes=4 * blocks + weights + 12 * 2**20
        ),
        cost_estimate=pl.CostEstimate(
            flops=2 * weights * blocks // (width * 4), bytes_accessed=32 * blocks, transcendentals=0
        ),
    )(own, small, gate, up, down)


HALVES = 2


def relay_kernel(ticks, *refs):
    (
        lengths,
        picks_ref,
        shares_ref,
        mixing_gain,
        latent_gain,
        expert_gain,
        opening_hbm,
        incoming_hbm,
        stored_hbm,
        asking_hbm,
        compress_hbm,
        lookup_hbm,
        content_hbm,
        merging_hbm,
        gate_hbm,
        up_hbm,
        down_hbm,
    ) = refs[:17]
    outs = refs[17 : 17 + ticks]
    (
        asking,
        compress,
        lookup,
        content,
        merging,
        gate,
        up,
        down,
        stage,
        keys,
        inputs,
        residual,
        q_lat,
        rows_all,
        small_all,
        hidden,
        part,
        side_in,
        line_in,
        results,
        input_sem,
        load_sem,
        down_sem,
        stage_sem,
        key_sem,
        out_sem,
        line_send,
        line_recv,
        side_send,
        side_recv,
        small_send,
        small_recv,
        give_send,
        give_recv,
        back_send,
        back_recv,
        hop_send,
        hop_recv,
    ) = refs[17 + ticks :]
    chips, pair, mine, spot, side = place_on_line()
    section = lax.axis_index("section")
    sections = lax.axis_size("section")
    _, _, height, width = inputs.shape
    count = chips * pair
    inner = down.shape[1]
    local = gate.shape[0]
    heads, head_size, latent = lookup.shape
    context = keys.shape[1] - HALVES * height
    chunk = width // RETURN_PIECES
    step = height // PIECES
    sibling = mine + 1 - 2 * side
    at_end = (spot == 0) | (spot == chips - 1)
    kind = rows_all.dtype

    def wide(value):
        return value.astype(jnp.float32)

    def local_copy(source, target, sem):
        return pltpu.make_async_copy(source, target, sem)

    def input_copy(t, half):
        source = opening_hbm.at[half] if t == 0 else incoming_hbm.at[t - 1, half]
        return local_copy(source, inputs.at[t, half], input_sem.at[t, half])

    def key_copy(t):
        return local_copy(stored_hbm.at[t], keys.at[t, pl.ds(0, context)], key_sem.at[t])

    attention_loads = [
        local_copy(source, target, load_sem.at[index])
        for index, (source, target) in enumerate(
            (
                (asking_hbm, asking),
                (compress_hbm, compress),
                (lookup_hbm, lookup),
                (content_hbm, content),
                (merging_hbm, merging),
            )
        )
    ]
    down_loads = [local_copy(down_hbm.at[e], down.at[e], down_sem.at[e]) for e in range(local)]
    raw = [(source, target, e) for e in range(local) for source, target in ((gate_hbm, gate), (up_hbm, up))]
    block_rows = stage.shape[1]
    full = inner // block_rows
    tail = inner - full * block_rows

    def stage_copy(matrix, c, size):
        source, _, e = raw[matrix]
        first = pl.multiple_of(c * block_rows, block_rows)
        return local_copy(
            source.at[e, pl.ds(first, size)], stage.at[c, pl.ds(0, size)], stage_sem.at[c]
        )

    def stage_start(matrix):
        for c in range(full):
            stage_copy(matrix, c, block_rows).start()
        if tail:
            stage_copy(matrix, full, tail).start()

    def turn_weights(counts):
        for matrix in range(len(raw)):
            _, target, e = raw[matrix]

            def turn(c, carry):
                stage_copy(matrix, c, block_rows).wait()
                first = pl.multiple_of(c * block_rows, block_rows)
                target[e, :, pl.ds(first, block_rows)] = stage[c].T
                if matrix + 1 < len(raw):
                    stage_copy(matrix + 1, c, block_rows).start()
                return carry

            lax.fori_loop(0, full, turn, 0)
            if tail:
                stage_copy(matrix, full, tail).wait()
                target[e, :, full * block_rows :] = stage[full, :tail].T
                if matrix + 1 < len(raw):
                    stage_copy(matrix + 1, full, tail).start()

            counts = poll(0, counts)
        return counts

    def reach(way):
        return (spot < chips - 1) if way > 0 else (spot > 0)

    def rows(t, block, half, piece):
        first = pl.multiple_of(side * height + piece * step, step)
        return rows_all.at[t, block, half, pl.ds(first, step)]

    def line_copy(t, block, half, piece, way):
        direction = 0 if way > 0 else 1
        place = rows(t, block, half, piece)
        return remote(
            place,
            place,
            line_send.at[direction, block, half, piece],
            line_recv.at[t, block, half, piece],
            mine + way * pair,
        )

    def side_copy(t, block, half, piece):
        place = rows(t, block, half, piece)
        return remote(
            place,
            place,
            side_send.at[block, half, piece],
            side_recv.at[t, block, half, piece],
            sibling,
        )

    def small_copy(distance):
        place = small_all.at[spot, side]
        return remote(
            place,
            place,
            small_send.at[distance],
            small_recv.at[distance],
            lax.rem(mine + distance, count),
        )

    def give_copy(block, half, piece):
        return remote(
            part.at[block, half, 1 - side, piece],
            side_in.at[block, half, piece],
            give_send.at[block, half, piece],
            give_recv.at[block, half, piece],
            sibling,
        )

    def back_copy(block, half, piece, way, sender):
        slot = jnp.where((block == sender + way) & (way < 0), chips, block)
        return remote(
            part.at[block, half, side, piece],
            line_in.at[slot, half, piece],
            back_send.at[block, half, piece],
            back_recv.at[slot, half, piece],
            mine + way * pair,
        )

    def combine(block, half, piece, way, from_line):
        give_copy(block, half, piece).wait_recv()
        value = wide(part[block, half, side, piece]) + wide(side_in[block, half, piece])
        if from_line:
            back_copy(block, half, piece, way, spot - way).wait_recv()
            value = value + wide(line_in[block, half, piece])
        part[block, half, side, piece] = value.astype(part.dtype)
        back_copy(block, half, piece, way, spot).start()

    def hop_copy(t, half, piece):
        columns = pl.ds(piece * chunk, chunk)
        return pltpu.make_async_remote_copy(
            src_ref=results.at[t, half, :, columns],
            dst_ref=inputs.at[t + 1, half, :, columns],
            send_sem=hop_send.at[half, piece],
            recv_sem=hop_recv.at[t + 1, half, piece],
            device_id={"section": section + 1},
            device_id_type=MESH,
        )

    def stream(way, unit, blocks):
        first = unit < blocks
        near = spot - way * (1 + unit)
        back = unit - blocks
        far = jnp.where(way > 0, back, chips - 1 - back)
        return jnp.where(first, near, far), jnp.where(first, 0, 1)

    def upstream(way):
        return jnp.where(way > 0, spot, chips - 1 - spot)

    def send_own(t, half, way):
        for piece in range(PIECES):

            @pl.when(reach(way))
            def _():
                line_copy(t, spot, half, piece, way).start()

    def arrive(t, way, j):
        blocks = upstream(way)
        block, half = stream(way, lax.div(j, PIECES), blocks)
        piece = lax.rem(j, PIECES)
        line_copy(t, block, half, piece, way).wait_recv()

        @pl.when(reach(way))
        def _():
            line_copy(t, block, half, piece, way).start()

        side_copy(t, block, half, piece).start()

        @pl.when(j == 2 * blocks * PIECES - 1)
        def _():
            send_own(t, 1, way)

    def send_back(way, v):
        ahead = upstream(-way)
        block, half = stream(-way, lax.div(v, RETURN_PIECES), ahead)
        combine(block, half, lax.rem(v, RETURN_PIECES), way, True)

    def normed(values, gain):
        mean = jnp.mean(values * values, axis=-1, keepdims=True)
        return (values * lax.rsqrt(mean + epsilon) * gain).astype(kind)

    def project(t):
        values = inputs[t].reshape(HALVES * height, width)
        rows_in = normed(wide(values), mixing_gain[...])
        queries = jnp.dot(rows_in, asking[...], preferred_element_type=jnp.float32).astype(kind)
        raw = jnp.dot(rows_in, compress[...], preferred_element_type=jnp.float32)
        keys[t, context:] = normed(raw, latent_gain[...])
        for head in range(heads):
            part_of = queries[:, head * head_size : (head + 1) * head_size]
            lat = jnp.dot(part_of, lookup[head], preferred_element_type=jnp.float32).astype(kind)
            for half in range(HALVES):
                q_lat[half, head * height : (head + 1) * height] = lat[
                    half * height : (half + 1) * height
                ]

    def attend_half(t, half):
        table = keys[t]
        scores = lax.dot_general(q_lat[half], table, NT, preferred_element_type=jnp.float32)
        scores = scores * head_size ** (-0.5)
        position = lax.broadcasted_iota(jnp.int32, (height, table.shape[0]), 1)
        query = lax.broadcasted_iota(jnp.int32, (height, table.shape[0]), 0) + half * height
        limit = jnp.where(position < context, lengths[t - section + sections - 1], query + (context + 1))
        visible = (position < limit)[None]
        scores = scores.reshape((heads,) + position.shape)
        scores = jnp.where(visible, scores, -jnp.inf).reshape(heads * height, -1)
        expd = jnp.exp(scores - jnp.max(scores, axis=-1, keepdims=True))
        weight = (expd * (1.0 / jnp.sum(expd, axis=-1, keepdims=True))).astype(kind)
        o_lat = jnp.dot(weight, table, preferred_element_type=jnp.float32).astype(kind)
        outs = []
        for head in range(heads):
            outs.append(
                jnp.dot(
                    o_lat[head * height : (head + 1) * height],
                    content[head],
                    preferred_element_type=jnp.float32,
                ).astype(kind)
            )
        heads_out = jnp.concatenate(outs, axis=1)
        total = wide(inputs[t, half]) + jnp.dot(
            heads_out, merging[...], preferred_element_type=jnp.float32
        )
        residual[half] = total
        first = pl.multiple_of(side * height, height)
        rows_all[t, spot, half, pl.ds(first, height)] = normed(total, expert_gain[...])

    def poll(t, counts):
        after = []
        for way, count in zip((1, -1), counts):
            total = 2 * upstream(way) * PIECES

            @pl.when(count < total)
            def _():
                arrive(t, way, count)

            after.append(jnp.minimum(count + 1, total))
        return tuple(after)

    def catch_up(t, way, count, goal):
        def one(j, carry):
            arrive(t, way, j)
            return carry

        lax.fori_loop(count, goal, one, 0)

    units = 2 * chips
    short = 2 * jnp.minimum(spot, chips - 1 - spot)
    leftward = spot > chips - 1 - spot
    near_way = jnp.where(leftward, -1, 1)

    def unit_of(k, lead):
        own = (k < lead) | (k >= units - 2 + lead)
        v = jnp.maximum(k - lead, 0)
        paired = v < 2 * short
        unit = jnp.where(paired, lax.div(v, 2), v - short)
        from_left = jnp.where(paired, lax.rem(v, 2) == 0, leftward)
        left_block, left_half = stream(1, unit, upstream(1))
        right_block, right_half = stream(-1, unit, upstream(-1))
        block = jnp.where(own, spot, jnp.where(from_left, left_block, right_block))
        half = jnp.where(own, jnp.where(k < units - 1, 0, 1), jnp.where(from_left, left_half, right_half))
        need = jnp.where(own, 0, (unit + 1) * PIECES)
        return block, half, jnp.where(from_left, need, 0), jnp.where(from_left, 0, need)

    def visit(t, k, carry):
        counts, sent = carry[:2], carry[2:]
        lead = jnp.where(t > 0, 1, 0)
        block, half, _, _ = unit_of(k, lead)
        done_block, done_half, _, _ = unit_of(jnp.maximum(k - 1, 0), lead)
        outward = at_end & (done_block != spot) & (k > 0)
        for piece in range(PIECES):
            side_copy(t, block, half, piece).wait_recv()
        values = rows_all[t, block, half]
        for e in range(local):
            line = mine * local + e + t * (small_all.shape[2] // ticks)
            columns = []
            for core in range(pair):
                table = small_all[block, core]
                here = lax.broadcasted_iota(jnp.int32, table.shape, 0) == line
                row = jnp.sum(jnp.where(here, table, 0.0), axis=0, keepdims=True)
                column = jnp.broadcast_to(row, (row.shape[1], row.shape[1])).T[:, :1]
                columns.append(jnp.where(half == 0, column[:height], column[height:]))
            share = jnp.concatenate(columns, axis=0)
            gated = jnp.dot(values, gate[e], preferred_element_type=jnp.float32)
            upped = jnp.dot(values, up[e], preferred_element_type=jnp.float32)
            hidden[e] = (gated * jax.nn.sigmoid(gated) * upped * share).astype(kind)
            counts = poll(t, counts)
            if e == 0:

                @pl.when(outward)
                def _():
                    way = jnp.where(done_block > spot, 1, -1)
                    for piece in range(RETURN_PIECES):
                        combine(done_block, done_half, piece, way, False)

        for piece in range(RETURN_PIECES):
            total = None
            for e in range(local):
                term = jnp.dot(
                    hidden[e],
                    down[e, :, piece * chunk : (piece + 1) * chunk],
                    preferred_element_type=jnp.float32,
                )
                total = term if total is None else total + term
            total = total.astype(part.dtype)
            for core in range(pair):
                part[block, half, core, piece] = total[core * height : (core + 1) * height]
            give_copy(block, half, piece).start()
            if piece == RETURN_PIECES // 2 - 1:
                counts = poll(t, counts)

        counts = poll(t, counts)
        after = []
        for direction, count in zip((near_way, -near_way), sent):
            done = back_goal(direction, k + 1 - lead)
            goal = jnp.maximum(count, done)
            return_up(direction, count, goal)
            after.append(goal)
        needs = unit_of(jnp.minimum(k + 1, units - 1), lead)[2:]
        ready = []
        for direction, count, need in zip((1, -1), counts, needs):
            goal = jnp.maximum(count, need)
            catch_up(t, direction, count, goal)
            ready.append(goal)
        return (*ready, *after)

    def back_total(way):
        ahead = jnp.where(at_end, 0, upstream(-way))
        return 2 * ahead * RETURN_PIECES

    def back_goal(way, k):
        due = lax.div(jnp.maximum(11 * k - 42 * upstream(way) + 12, 0), 4)
        return jnp.minimum(due, back_total(way))

    def return_up(way, count, goal):
        def one(v, carry):
            send_back(way, v)
            return carry

        lax.fori_loop(count, goal, one, 0)

    def finish(t, half):
        for piece in range(RETURN_PIECES):
            columns = pl.ds(piece * chunk, chunk)
            give_copy(spot, half, piece).wait_recv()
            residual[half, :, columns] += wide(part[spot, half, side, piece]) + wide(
                side_in[spot, half, piece]
            )
            for way in (1, -1):

                @pl.when(reach(-way))
                def _():
                    back_copy(spot, half, piece, way, spot - way).wait_recv()
                    slot = spot if way > 0 else chips
                    residual[half, :, columns] += wide(line_in[slot, half, piece])

            results[t, half, :, columns] = residual[half, :, columns].astype(kind)

            @pl.when((section < sections - 1) & (t < ticks - 1))
            def _():
                hop_copy(t, half, piece).start()

        for i, out in enumerate(outs):

            @pl.when(t == i)
            def _():
                local_copy(results.at[i, half], out.at[half], out_sem.at[i, half]).start()

    barrier = pltpu.get_barrier_semaphore()

    def hello(condition, device):
        @pl.when(condition)
        def _():
            pl.semaphore_signal(barrier, inc=1, device_id=device, device_id_type=MESH)

    for half in range(HALVES):
        input_copy(0, half).start()
    for load in attention_loads[:3]:
        load.start()
    key_copy(0).start()
    experts_all = local * count
    tokens = HALVES * height
    for t in range(ticks):
        table = jnp.zeros((experts_all, tokens), jnp.float32)
        expert = lax.broadcasted_iota(jnp.int32, table.shape, 0)
        for choice in range(picks_ref.shape[1]):
            named = picks_ref[t, choice : choice + 1] == expert
            table = table + jnp.where(named, shares_ref[t, choice : choice + 1], 0.0)
        small_all[spot, side, t * experts_all : (t + 1) * experts_all] = table
    for distance in range(1, count):
        other = lax.rem(mine + distance, count)
        pl.semaphore_signal(barrier, inc=1, device_id={"expert": other}, device_id_type=MESH)
    section_neighbours = jnp.where((section == 0) | (section == sections - 1), 1, 2)
    hello(section > 0, {"section": section - 1})
    hello(section < sections - 1, {"section": section + 1})
    pl.semaphore_wait(barrier, count - 1 + section_neighbours)
    for distance in range(1, count):
        small_copy(distance).start()

    def tick(t, carry):
        for half in range(HALVES):

            @pl.when((t == 0) | (section == 0))
            def _():
                local_copy(opening_hbm.at[half], inputs.at[t, half], input_sem.at[t, half]).wait()

            @pl.when((t > 0) & (section > 0))
            def _():
                for piece in range(RETURN_PIECES):
                    hop_copy(t - 1, half, piece).wait_recv()

        @pl.when(t == 0)
        def _():
            for load in attention_loads[:3]:
                load.wait()
            for load in attention_loads[3:]:
                load.start()

        project(t)
        key_copy(t).wait()

        @pl.when(t == 0)
        def _():
            for load in attention_loads[3:]:
                load.wait()
            stage_start(0)
            for load in down_loads:
                load.start()
            for later in range(1, ticks):
                key_copy(later).start()

                @pl.when(section == 0)
                def _():
                    for half in range(HALVES):
                        input_copy(later, half).start()

        for half in range(HALVES):
            attend_half(t, half)
            for piece in range(PIECES):
                side_copy(t, spot, half, piece).start()
            for way in (1, -1):
                if half == 0:
                    send_own(t, half, way)
                else:

                    @pl.when(upstream(way) == 0)
                    def _():
                        send_own(t, half, way)

        none = jnp.int32(0)

        def first_tick():
            counts = turn_weights((none, none))
            for load in down_loads:
                load.wait()
            for distance in range(1, count):
                small_copy(distance).wait_recv()
            ready = []
            for way, start, need in zip((1, -1), counts, unit_of(none, none)[2:]):
                goal = jnp.maximum(start, need)
                catch_up(0, way, start, goal)
                ready.append(goal)
            return tuple(ready)

        counts = lax.cond(t == 0, first_tick, lambda: (none, none))
        state = lax.fori_loop(
            0, units, lambda k, state: visit(t, k, state), (*counts, none, none)
        )
        finish(t, 0)

        def rest(v, carry):
            for way, done in zip((near_way, -near_way), state[2:]):

                @pl.when(done + v < back_total(way))
                def _():
                    send_back(way, done + v)

            return carry

        left_over = [back_total(way) - done for way, done in zip((near_way, -near_way), state[2:])]
        lax.fori_loop(0, jnp.maximum(left_over[0], left_over[1]), rest, 0)
        finish(t, 1)

        def settle(block, inner):
            for half in range(HALVES):
                for piece in range(PIECES):
                    for way in (1, -1):
                        passes = (block <= spot) if way > 0 else (block >= spot)

                        @pl.when(passes & reach(way))
                        def _():
                            line_copy(t, block, half, piece, way).wait_send()

                    side_copy(t, block, half, piece).wait_send()
                for piece in range(RETURN_PIECES):
                    give_copy(block, half, piece).wait_send()

                    @pl.when(block != spot)
                    def _():
                        back_copy(
                            block, half, piece, jnp.where(block > spot, 1, -1), spot
                        ).wait_send()

            return inner

        lax.fori_loop(0, chips, settle, 0)

        @pl.when((section < sections - 1) & (t < ticks - 1))
        def _():
            for half in range(HALVES):
                for piece in range(RETURN_PIECES):
                    hop_copy(t, half, piece).wait_send()

        return carry

    lax.fori_loop(0, ticks, tick, 0)

    for distance in range(1, count):
        small_copy(distance).wait_send()
    for t in range(ticks):
        for half in range(HALVES):
            local_copy(results.at[t, half], outs[t].at[half], out_sem.at[t, half]).wait()


def relay(
    lengths,
    picks,
    shares,
    mixing_gain,
    latent_gain,
    expert_gain,
    opening,
    incoming,
    stored,
    asking,
    compress,
    lookup,
    content,
    merging,
    gate,
    up,
    down,
):
    count = lax.axis_size("expert")
    pair = 2
    chips = count // pair
    ticks, context, latent = stored.shape
    kind = opening.dtype
    height = opening.shape[0] // HALVES
    width = opening.shape[1]
    local, inner = down.shape[:2]
    heads = lookup.shape[0]
    chunk = width // RETURN_PIECES
    dma = pltpu.SemaphoreType.DMA
    hbm = pl.BlockSpec(memory_space=pl.ANY)
    vmem = pl.BlockSpec(memory_space=pltpu.VMEM)
    smem = pl.BlockSpec(memory_space=pltpu.SMEM)
    cut = (HALVES, height, width)
    results = pl.pallas_call(
        functools.partial(relay_kernel, ticks),
        out_shape=[jax.ShapeDtypeStruct(cut, kind)] * ticks,
        in_specs=[smem] + [vmem] * 5 + [hbm] * 11,
        out_specs=[hbm] * ticks,
        scratch_shapes=[
            *[pltpu.VMEM(w.shape, kind) for w in (asking, compress, lookup, content, merging)],
            *[pltpu.VMEM((local, width, inner), kind) for _ in range(2)],
            pltpu.VMEM((local, inner, width), kind),
            pltpu.VMEM((pl.cdiv(inner, 128), 128, width), kind),
            pltpu.VMEM((ticks, context + HALVES * height, latent), kind),
            pltpu.VMEM((ticks,) + cut, kind),
            pltpu.VMEM(cut, jnp.float32),
            pltpu.VMEM((HALVES, heads * height, latent), kind),
            pltpu.VMEM((ticks, chips, HALVES, pair * height, width), kind),
            pltpu.VMEM((chips, pair, ticks * local * count, HALVES * height), shares.dtype),
            pltpu.VMEM((local, pair * height, inner), kind),
            pltpu.VMEM((chips, HALVES, pair, RETURN_PIECES, height, chunk), kind),
            pltpu.VMEM((chips, HALVES, RETURN_PIECES, height, chunk), kind),
            pltpu.VMEM((chips + 1, HALVES, RETURN_PIECES, height, chunk), kind),
            pltpu.VMEM((ticks,) + cut, kind),
            dma((ticks, HALVES)),
            dma((5,)),
            dma((local,)),
            dma((pl.cdiv(inner, 128),)),
            dma((ticks,)),
            dma((ticks, HALVES)),
            dma((2, chips, HALVES, PIECES)),
            dma((ticks, chips, HALVES, PIECES)),
            dma((chips, HALVES, PIECES)),
            dma((ticks, chips, HALVES, PIECES)),
            dma((count,)),
            dma((count,)),
            dma((chips, HALVES, RETURN_PIECES)),
            dma((chips, HALVES, RETURN_PIECES)),
            dma((chips, HALVES, RETURN_PIECES)),
            dma((chips + 1, HALVES, RETURN_PIECES)),
            dma((HALVES, RETURN_PIECES)),
            dma((ticks, HALVES, RETURN_PIECES)),
        ],
        compiler_params=pltpu.CompilerParams(
            collective_id=0, has_side_effects=True, vmem_limit_bytes=63 * 2**20
        ),
    )(
        lengths,
        picks,
        shares,
        mixing_gain,
        latent_gain,
        expert_gain,
        opening.reshape(cut),
        incoming.reshape((ticks - 1,) + cut),
        stored,
        asking,
        compress,
        lookup,
        content,
        merging,
        gate,
        up,
        down,
    )
    return jnp.stack([result.reshape(HALVES * height, width) for result in results])


def shifted(value, axis, steps):
    count = lax.axis_size(axis)
    initial, last = (max(0, -steps), min(count, count - steps))
    return lax.ppermute(value, axis, [(source, source + steps) for source in range(initial, last)])


def row_norm(values, gain_row):
    return (
        values * lax.rsqrt(jnp.mean(values * values, axis=-1, keepdims=True) + epsilon) * gain_row
    )


def attend(q_lat, cache_rows, new_rows, length, score_scale):
    piece_list = q_lat.shape[0]
    context = cache_rows.shape[0]
    key_rows = jnp.concatenate([cache_rows, new_rows], axis=0)
    scores = (
        jnp.einsum("thl,kl->thk", q_lat, key_rows, preferred_element_type=jnp.float32) * score_scale
    )
    position = lax.broadcasted_iota(jnp.int32, (piece_list, context + piece_list), 1)
    query_pos = lax.broadcasted_iota(jnp.int32, (piece_list, context + piece_list), 0)
    visible = jnp.where(position < context, position < length, position - context <= query_pos)
    scores = jnp.where(visible[:, None, :], scores, -jnp.inf)
    row_max = jnp.max(scores, axis=-1, keepdims=True)
    expd = jnp.where(visible[:, None, :], jnp.exp(scores - row_max), 0.0)
    attention = (expd / jnp.sum(expd, axis=-1, keepdims=True)).astype(jnp.bfloat16)
    return jnp.einsum(
        "thk,kl->thl", attention, key_rows, preferred_element_type=jnp.float32
    ).astype(jnp.bfloat16)


def shards(
    opening_residual,
    incoming_residual,
    stored_summaries,
    stored_counts,
    picked_specialists,
    chooser_mixing_share,
    mixing_scale_factor,
    asking_projection,
    summary_lookup_factor,
    summary_content_factor,
    merging_projection,
    compress_projection,
    summary_scale_factor,
    specialist_scale_factor,
    specialist_switch_factor,
    specialist_widen_factor,
    specialist_contract_factor,
):
    segment_ordinal = lax.axis_index("section")
    section_count = lax.axis_size("section")
    sources = lax.axis_size("expert")
    tick_count = stored_summaries.shape[0]
    piece_list = opening_residual.shape[1]
    inner_feature_midcount = opening_residual.shape[2]
    full_width = mixing_scale_factor.shape[1]
    local_heads = summary_lookup_factor.shape[1]
    head_size = summary_lookup_factor.shape[2]
    top_count = picked_specialists.shape[3]
    expert_local = specialist_switch_factor.shape[1]
    score_scale = head_size ** (-0.5)
    if lax.axis_size("tensor") == 1 and sources % 2 == 0 and section_count > 1 and tick_count > 1:
        results = relay(
            stored_counts[:, 0],
            jnp.swapaxes(picked_specialists[:, 0], 1, 2),
            jnp.swapaxes(chooser_mixing_share[:, 0], 1, 2),
            mixing_scale_factor,
            summary_scale_factor,
            specialist_scale_factor,
            opening_residual[0],
            incoming_residual,
            stored_summaries[:, 0, 0],
            asking_projection[0],
            compress_projection[0],
            summary_lookup_factor[0],
            summary_content_factor[0],
            merging_projection[0],
            jnp.swapaxes(specialist_switch_factor[0], 1, 2),
            jnp.swapaxes(specialist_widen_factor[0], 1, 2),
            specialist_contract_factor[0],
        )
        return results[:, None]
    expert_ids = lax.broadcasted_iota(jnp.int32, (1, 1, 1, expert_local * sources), 3)
    shares_dense = jnp.sum(
        jnp.where(
            picked_specialists[:, 0][..., None] == expert_ids,
            chooser_mixing_share[:, 0][..., None],
            0.0,
        ),
        axis=2,
    )
    shares_dense = jnp.swapaxes(shares_dense, 1, 2)
    outputs = []
    present_carry = opening_residual[0]
    section_out = present_carry
    for step_index in range(tick_count):
        if step_index > 0:
            handed = shifted(section_out, "section", 1)
            present_carry = jnp.where(
                segment_ordinal == 0, incoming_residual[step_index - 1], handed
            )
        micro_index = step_index - segment_ordinal + section_count - 1
        length = lax.dynamic_index_in_dim(stored_counts[:, 0], micro_index, 0, keepdims=False)
        full_rows = lax.all_gather(present_carry, "tensor", axis=1, tiled=True)
        normed = row_norm(full_rows.astype(jnp.float32), mixing_scale_factor[0]).astype(
            jnp.bfloat16
        )
        queries = jnp.dot(normed, asking_projection[0], preferred_element_type=jnp.float32).astype(
            jnp.bfloat16
        )
        queries = queries.reshape(piece_list, local_heads, head_size)
        q_lat = jnp.einsum(
            "thd,hdl->thl", queries, summary_lookup_factor[0], preferred_element_type=jnp.float32
        ).astype(jnp.bfloat16)
        latent_part = jnp.dot(normed, compress_projection[0], preferred_element_type=jnp.float32)
        latent_raw = lax.all_gather(
            latent_part.astype(jnp.bfloat16), "tensor", axis=1, tiled=True
        ).astype(latent_part.dtype)
        new_latent = row_norm(latent_raw, summary_scale_factor[0]).astype(jnp.bfloat16)
        o_lat = attend(q_lat, stored_summaries[step_index, 0, 0], new_latent, length, score_scale)
        heads_out = jnp.einsum(
            "thl,hld->thd", o_lat, summary_content_factor[0], preferred_element_type=jnp.float32
        ).astype(jnp.bfloat16)
        heads_out = heads_out.reshape(piece_list, local_heads * head_size)
        head_terms = jnp.dot(heads_out, merging_projection[0], preferred_element_type=jnp.float32)
        residual = present_carry.astype(jnp.float32) + lax.psum_scatter(
            head_terms.astype(jnp.bfloat16), "tensor", scatter_dimension=1, tiled=True
        ).astype(jnp.float32)
        squares = lax.psum(jnp.sum(residual * residual, axis=1), "tensor")
        moe_input = (
            residual
            * lax.rsqrt(squares / full_width + epsilon)[:, None]
            * specialist_scale_factor[0]
        ).astype(jnp.bfloat16)
        whole_rows = lax.all_gather(moe_input, "tensor", axis=1, tiled=True)
        routed = experts(
            whole_rows,
            shares_dense[step_index],
            jnp.swapaxes(specialist_switch_factor[0], 1, 2),
            jnp.swapaxes(specialist_widen_factor[0], 1, 2),
            specialist_contract_factor[0],
        )
        if lax.axis_size("tensor") > 1:
            routed = lax.psum_scatter(
                routed.astype(jnp.bfloat16), "tensor", scatter_dimension=1, tiled=True
            ).astype(jnp.float32)
        section_out = (residual + routed).astype(jnp.bfloat16)
        outputs.append(section_out)
    return jnp.stack(outputs)[:, None]


def solution(mesh):
    in_specs = (
        P("section", ("groups", "expert"), "tensor"),
        P(None, ("groups", "expert"), "tensor"),
        P(None, "section", ("groups", "expert"), None, None),
        P(None, ("groups", "expert")),
        P(None, "section", ("groups", "expert"), None),
        P(None, "section", ("groups", "expert"), None),
        P("section", None),
        P("section", None, "tensor"),
        P("section", "tensor", None, None),
        P("section", "tensor", None, None),
        P("section", "tensor", None),
        P("section", None, "tensor"),
        P("section", None),
        P("section", "tensor"),
        P("section", "expert", None, "tensor"),
        P("section", "expert", None, "tensor"),
        P("section", "expert", "tensor", None),
    )
    out_specs = P(None, "section", ("groups", "expert"), "tensor")
    return jax.shard_map(shards, mesh=mesh, in_specs=in_specs, out_specs=out_specs, check_vma=False)
```

```python
import functools

import jax
import jax.numpy as jnp
from jax import lax
from jax.experimental import pallas as pl
from jax.experimental.pallas import tpu as pltpu
from jax.sharding import PartitionSpec as P


epsilon = 1e-06


MESH = pl.DeviceIdType.MESH
PIECES = 4
RETURN_PIECES = 4
NT = (((1,), (1,)), ((), ()))


def place_on_line():
    count = lax.axis_size("expert")
    pair = 2 if count % 2 == 0 else 1
    mine = lax.axis_index("expert")
    return count // pair, pair, mine, mine // pair, lax.rem(mine, pair)


def greet(chips, pair, mine, spot, side):
    barrier = pltpu.get_barrier_semaphore()

    def hello(other):
        pl.semaphore_signal(barrier, inc=1, device_id={"expert": other}, device_id_type=MESH)

    @pl.when(spot > 0)
    def _():
        hello(mine - pair)

    @pl.when(spot < chips - 1)
    def _():
        hello(mine + pair)

    if pair == 2:
        hello(mine + 1 - 2 * side)
    inner = (spot > 0) & (spot < chips - 1)

    @pl.when(inner)
    def _():
        pl.semaphore_wait(barrier, pair + 1)

    @pl.when(jnp.logical_not(inner))
    def _():
        pl.semaphore_wait(barrier, pair)


def remote(src, dst, send, recv, other):
    return pltpu.make_async_remote_copy(
        src_ref=src,
        dst_ref=dst,
        send_sem=send,
        recv_sem=recv,
        device_id={"expert": other},
        device_id_type=MESH,
    )


def visiting_order(k, spot, chips):
    low = jnp.minimum(spot, chips - 1 - spot)
    near = (k + 1) // 2
    around = spot + jnp.where(lax.rem(k, 2) == 0, near, -near)
    rest = jnp.where(spot < chips - 1 - spot, k, chips - 1 - k)
    return jnp.where(k <= 2 * low, around, rest)


def experts_kernel(
    own_ref,
    small_ref,
    gate_hbm,
    up_hbm,
    down_hbm,
    sum_ref,
    gate,
    up,
    down,
    rows_all,
    small_all,
    hidden,
    part,
    side_in,
    line_in,
    own_sem,
    weight_sem,
    line_send,
    line_recv,
    side_send,
    side_recv,
    give_send,
    give_recv,
    back_send,
    back_recv,
):
    chips, pair, mine, spot, side = place_on_line()
    height, width = own_ref.shape
    local = gate.shape[0]
    step = height // PIECES
    chunk = width // RETURN_PIECES
    sibling = mine + 1 - 2 * side
    at_end = (spot == 0) | (spot == chips - 1)

    loads = []
    for index, (source, target) in enumerate(((gate_hbm, gate), (up_hbm, up), (down_hbm, down))):
        for e in range(local):
            loads.append(
                pltpu.make_async_copy(source.at[e], target.at[e], weight_sem.at[index, e])
            )

    def rows(block, core, piece):
        if piece == PIECES:
            return small_all.at[block, core]
        first = pl.multiple_of(core * height + piece * step, step)
        return rows_all.at[block, pl.ds(first, step)]

    def origin(block, piece):
        if block is not None:
            return rows(block, side, piece)
        return small_ref if piece == PIECES else own_ref.at[pl.ds(piece * step, step)]

    def line_copy(block, piece, way):
        where = spot if block is None else block
        direction = 0 if way > 0 else 1
        return remote(
            origin(block, piece),
            rows(where, side, piece),
            line_send.at[direction, where, piece],
            line_recv.at[where, piece],
            mine + way * pair,
        )

    def side_copy(block, piece):
        where = spot if block is None else block
        return remote(
            origin(block, piece),
            rows(where, side, piece),
            side_send.at[where, piece],
            side_recv.at[where, piece],
            sibling,
        )

    def onward(block, piece, way, act):
        @pl.when((spot < chips - 1) if way > 0 else (spot > 0))
        def _():
            act(line_copy(block, piece, way))

    def passing(far, act):
        for piece in range(PIECES + 1):
            for way in (1, -1):
                block = spot - way * far

                @pl.when((block >= 0) if way > 0 else (block < chips))
                def _():
                    act(block, piece, way)

    def give_copy(block, piece):
        return remote(
            part.at[block, 1 - side, piece],
            side_in.at[block, piece],
            give_send.at[block, piece],
            give_recv.at[block, piece],
            sibling,
        )

    def back_copy(block, piece, way):
        direction = (1 - way) // 2
        return remote(
            part.at[block, side, piece],
            line_in.at[direction, block, piece],
            back_send.at[block, piece],
            back_recv.at[direction, block, piece],
            mine + way * pair,
        )

    def wide(value):
        return value.astype(jnp.float32)

    def combine(block, piece, way, from_line):
        give_copy(block, piece).wait_recv()
        value = wide(part[block, side, piece]) + wide(side_in[block, piece])
        if from_line:
            back_copy(block, piece, way).wait_recv()
            value = value + wide(line_in[(1 - way) // 2, block, piece])
        part[block, side, piece] = value.astype(part.dtype)
        back_copy(block, piece, way).start()

    greet(chips, pair, mine, spot, side)
    for piece in (PIECES, *range(PIECES)):
        for way in (1, -1):
            onward(None, piece, way, lambda copy: copy.start())
        side_copy(None, piece).start()
    keep = pltpu.make_async_copy(
        own_ref, rows_all.at[spot, pl.ds(pl.multiple_of(side * height, height), height)], own_sem.at[0]
    )
    keep.start()
    keep_small = pltpu.make_async_copy(small_ref, small_all.at[spot, side], own_sem.at[1])
    keep_small.start()
    for load in loads:
        load.start()
    keep.wait()
    keep_small.wait()
    for load in loads:
        load.wait()

    def visit(k, carry):
        block = visiting_order(k, spot, chips)
        way = jnp.where(block > spot, 1, -1)
        outward = at_end & (k > 0)
        for piece in range(PIECES + 1):
            side_copy(block, piece).wait_recv()
        values = rows_all[block]
        for e in range(local):
            chosen_expert = mine * local + e
            columns = []
            for core in range(pair):
                table = small_all[block, core]
                here = lax.broadcasted_iota(jnp.int32, table.shape, 0) == chosen_expert
                row = jnp.sum(jnp.where(here, table, 0.0), axis=0, keepdims=True)
                columns.append(jnp.broadcast_to(row, (height, height)).T[:, :1])
            share = jnp.concatenate(columns, axis=0)
            gated = lax.dot_general(values, gate[e], NT, preferred_element_type=jnp.float32)
            upped = lax.dot_general(values, up[e], NT, preferred_element_type=jnp.float32)
            hidden[e] = (gated * jax.nn.sigmoid(gated) * upped * share).astype(hidden.dtype)
        for piece in range(RETURN_PIECES):
            total = None
            for e in range(local):
                term = jnp.dot(
                    hidden[e],
                    down[e, :, piece * chunk : (piece + 1) * chunk],
                    preferred_element_type=jnp.float32,
                )
                total = term if total is None else total + term
            total = total.astype(part.dtype)
            for core in range(pair):
                part[block, core, piece] = total[core * height : (core + 1) * height]
            give_copy(block, piece).start()
            if piece > 0:

                @pl.when(outward)
                def _():
                    combine(block, piece - 1, way, False)

        @pl.when(outward)
        def _():
            combine(block, RETURN_PIECES - 1, way, False)

        @pl.when(k < chips - 1)
        def _():
            def receive(block, piece, way):
                line_copy(block, piece, way).wait_recv()
                onward(block, piece, way, lambda copy: copy.start())
                side_copy(block, piece).start()

            passing(k + 1, receive)

        return carry

    lax.fori_loop(0, chips, visit, 0)

    left_first = 2 * spot <= chips - 1

    def relay(a, carry):
        for piece in range(RETURN_PIECES):
            for turn in range(2):
                way = jnp.where(left_first, 1 - 2 * turn, 2 * turn - 1)
                block = jnp.where(way > 0, a, chips - 1 - a)
                valid = jnp.where(way > 0, block > spot, block < spot) & jnp.logical_not(at_end)

                @pl.when(valid)
                def _():
                    combine(block, piece, way, True)

        return carry

    lax.fori_loop(1, chips, relay, 0)
    for piece in range(RETURN_PIECES):
        give_copy(spot, piece).wait_recv()
        columns = pl.ds(piece * chunk, chunk)
        sum_ref[:, columns] = wide(part[spot, side, piece]) + wide(side_in[spot, piece])
        for way in (1, -1):

            @pl.when((spot > 0) if way > 0 else (spot < chips - 1))
            def _():
                back_copy(spot, piece, way).wait_recv()
                sum_ref[:, columns] += wide(line_in[(1 - way) // 2, spot, piece])

    for piece in range(PIECES + 1):
        for way in (1, -1):
            onward(None, piece, way, lambda copy: copy.wait_send())
        side_copy(None, piece).wait_send()

    def settle(far, carry):
        def sent(block, piece, way):
            onward(block, piece, way, lambda copy: copy.wait_send())
            side_copy(block, piece).wait_send()

        passing(far, sent)
        return carry

    lax.fori_loop(1, chips, settle, 0)

    def settle_back(block, carry):
        for piece in range(RETURN_PIECES):
            give_copy(block, piece).wait_send()

            @pl.when(block != spot)
            def _():
                back_copy(block, piece, jnp.where(block > spot, 1, -1)).wait_send()

        return carry

    lax.fori_loop(0, chips, settle_back, 0)


def experts(own, small, gate, up, down):
    count = lax.axis_size("expert")
    pair = 2
    chips = count // pair
    height, width = own.shape
    local, inner = down.shape[:2]
    kind = own.dtype
    chunk = width // RETURN_PIECES
    blocks = chips * pair * height * width * 2
    weights = 3 * local * inner * width * 2
    dma = pltpu.SemaphoreType.DMA
    hbm = pl.BlockSpec(memory_space=pl.ANY)
    vmem = pl.BlockSpec(memory_space=pltpu.VMEM)
    return pl.pallas_call(
        experts_kernel,
        out_shape=jax.ShapeDtypeStruct((height, width), jnp.float32),
        in_specs=[vmem, vmem, hbm, hbm, hbm],
        out_specs=vmem,
        scratch_shapes=[
            pltpu.VMEM((local, inner, width), kind),
            pltpu.VMEM((local, inner, width), kind),
            pltpu.VMEM((local, inner, width), kind),
            pltpu.VMEM((chips, pair * height, width), kind),
            pltpu.VMEM((chips, pair) + small.shape, small.dtype),
            pltpu.VMEM((local, pair * height, inner), kind),
            pltpu.VMEM((chips, pair, RETURN_PIECES, height, chunk), kind),
            pltpu.VMEM((chips, RETURN_PIECES, height, chunk), kind),
            pltpu.VMEM((2, chips, RETURN_PIECES, height, chunk), kind),
            dma((2,)),
            dma((3, local)),
            dma((2, chips, PIECES + 1)),
            dma((chips, PIECES + 1)),
            dma((chips, PIECES + 1)),
            dma((chips, PIECES + 1)),
            dma((chips, RETURN_PIECES)),
            dma((chips, RETURN_PIECES)),
            dma((chips, RETURN_PIECES)),
            dma((2, chips, RETURN_PIECES)),
        ],
        compiler_params=pltpu.CompilerParams(
            collective_id=0, has_side_effects=True, vmem_limit_bytes=4 * blocks + weights + 12 * 2**20
        ),
        cost_estimate=pl.CostEstimate(
            flops=2 * weights * blocks // (width * 4), bytes_accessed=32 * blocks, transcendentals=0
        ),
    )(own, small, gate, up, down)


HALVES = 2


def relay_kernel(ticks, *refs):
    (
        lengths,
        picks_ref,
        shares_ref,
        mixing_gain,
        latent_gain,
        expert_gain,
        opening_hbm,
        incoming_hbm,
        stored_hbm,
        asking_hbm,
        compress_hbm,
        lookup_hbm,
        content_hbm,
        merging_hbm,
        gate_hbm,
        up_hbm,
        down_hbm,
    ) = refs[:17]
    results = refs[17]
    (
        asking,
        compress,
        lookup,
        content,
        merging,
        gate,
        up,
        down,
        stage,
        keys,
        inputs,
        residual,
        q_lat,
        rows_all,
        small_all,
        hidden,
        part,
        side_in,
        line_in,
        input_sem,
        load_sem,
        down_sem,
        stage_sem,
        key_sem,
        line_send,
        line_recv,
        side_send,
        side_recv,
        small_send,
        small_recv,
        give_send,
        give_recv,
        back_send,
        back_recv,
        hop_send,
        hop_recv,
    ) = refs[18:]
    chips, pair, mine, spot, side = place_on_line()
    section = lax.axis_index("section")
    sections = lax.axis_size("section")
    _, _, height, width = inputs.shape
    count = chips * pair
    inner = down.shape[1]
    local = gate.shape[0]
    heads, head_size, latent = lookup.shape
    context = keys.shape[1] - HALVES * height
    chunk = width // RETURN_PIECES
    step = height // PIECES
    sibling = mine + 1 - 2 * side
    at_end = (spot == 0) | (spot == chips - 1)
    kind = rows_all.dtype

    def wide(value):
        return value.astype(jnp.float32)

    def local_copy(source, target, sem):
        return pltpu.make_async_copy(source, target, sem)

    def input_copy(t, half):
        source = opening_hbm.at[half] if t == 0 else incoming_hbm.at[t - 1, half]
        return local_copy(source, inputs.at[t, half], input_sem.at[t, half])

    def key_copy(t):
        return local_copy(stored_hbm.at[t], keys.at[t, pl.ds(0, context)], key_sem.at[t])

    attention_loads = [
        local_copy(source, target, load_sem.at[index])
        for index, (source, target) in enumerate(
            (
                (asking_hbm, asking),
                (compress_hbm, compress),
                (lookup_hbm, lookup),
                (content_hbm, content),
                (merging_hbm, merging),
            )
        )
    ]
    down_loads = [local_copy(down_hbm.at[e], down.at[e], down_sem.at[e]) for e in range(local)]
    raw = [(source, target, e) for e in range(local) for source, target in ((gate_hbm, gate), (up_hbm, up))]
    block_rows = stage.shape[1]
    full = inner // block_rows
    tail = inner - full * block_rows

    def stage_copy(matrix, c, size):
        source, _, e = raw[matrix]
        first = pl.multiple_of(c * block_rows, block_rows)
        return local_copy(
            source.at[e, pl.ds(first, size)], stage.at[c, pl.ds(0, size)], stage_sem.at[c]
        )

    def stage_start(matrix):
        for c in range(full):
            stage_copy(matrix, c, block_rows).start()
        if tail:
            stage_copy(matrix, full, tail).start()

    def turn_weights(counts):
        for matrix in range(len(raw)):
            _, target, e = raw[matrix]

            def turn(c, carry):
                stage_copy(matrix, c, block_rows).wait()
                first = pl.multiple_of(c * block_rows, block_rows)
                target[e, :, pl.ds(first, block_rows)] = stage[c].T
                if matrix + 1 < len(raw):
                    stage_copy(matrix + 1, c, block_rows).start()
                return carry

            lax.fori_loop(0, full, turn, 0)
            if tail:
                stage_copy(matrix, full, tail).wait()
                target[e, :, full * block_rows :] = stage[full, :tail].T
                if matrix + 1 < len(raw):
                    stage_copy(matrix + 1, full, tail).start()

            counts = poll(0, counts)
        return counts

    def reach(way):
        return (spot < chips - 1) if way > 0 else (spot > 0)

    def rows(t, block, half, piece):
        first = pl.multiple_of(side * height + piece * step, step)
        return rows_all.at[t, block, half, pl.ds(first, step)]

    def line_copy(t, block, half, piece, way):
        direction = 0 if way > 0 else 1
        place = rows(t, block, half, piece)
        return remote(
            place,
            place,
            line_send.at[direction, block],
            line_recv.at[t, block, half, piece],
            mine + way * pair,
        )

    def side_copy(t, block, half, piece):
        place = rows(t, block, half, piece)
        return remote(
            place,
            place,
            side_send.at[block],
            side_recv.at[t, block, half],
            sibling,
        )

    def whole_rows(t, block, half, other, send, recv):
        place = rows_all.at[t, block, half, pl.ds(pl.multiple_of(side * height, height), height)]
        return remote(place, place, send, recv, other)

    def side_half(t, block, half):
        return whole_rows(t, block, half, sibling, side_send.at[block], side_recv.at[t, block, half])

    def all_sent(target, send):
        remote(target, target, send, side_recv.at[0, 0, 0], sibling).wait_send()

    def small_copy(distance):
        place = small_all.at[spot, side]
        return remote(
            place,
            place,
            small_send.at[distance],
            small_recv.at[distance],
            lax.rem(mine + distance, count),
        )

    def give_copy(block, half, piece):
        return remote(
            part.at[block, half, 1 - side, piece],
            side_in.at[block, half, piece],
            give_send.at[block],
            give_recv.at[block, half, piece],
            sibling,
        )

    def back_copy(block, half, piece, way, sender):
        slot = jnp.where((block == sender + way) & (way < 0), chips, block)
        return remote(
            part.at[block, half, side, piece],
            line_in.at[slot, half, piece],
            back_send.at[block],
            back_recv.at[slot, half, piece],
            mine + way * pair,
        )

    def combine(block, half, piece, way, from_line):
        give_copy(block, half, piece).wait_recv()
        value = wide(part[block, half, side, piece]) + wide(side_in[block, half, piece])
        if from_line:
            back_copy(block, half, piece, way, spot - way).wait_recv()
            value = value + wide(line_in[block, half, piece])
        part[block, half, side, piece] = value.astype(part.dtype)
        back_copy(block, half, piece, way, spot).start()

    def hop_copy(t, half, piece):
        columns = pl.ds(piece * chunk, chunk)
        return pltpu.make_async_remote_copy(
            src_ref=results.at[t, half, :, columns],
            dst_ref=inputs.at[t + 1, half, :, columns],
            send_sem=hop_send.at[t],
            recv_sem=hop_recv.at[t + 1, half],
            device_id={"section": section + 1},
            device_id_type=MESH,
        )

    def stream(way, unit, blocks):
        first = unit < blocks
        near = spot - way * (1 + unit)
        back = unit - blocks
        far = jnp.where(way > 0, back, chips - 1 - back)
        return jnp.where(first, near, far), jnp.where(first, 0, 1)

    def upstream(way):
        return jnp.where(way > 0, spot, chips - 1 - spot)

    def send_own(t, half, way):
        for piece in range(PIECES):

            @pl.when(reach(way))
            def _():
                line_copy(t, spot, half, piece, way).start()

    def arrive(t, way, j):
        blocks = upstream(way)
        block, half = stream(way, lax.div(j, PIECES), blocks)
        piece = lax.rem(j, PIECES)
        line_copy(t, block, half, piece, way).wait_recv()

        @pl.when(reach(way))
        def _():
            line_copy(t, block, half, piece, way).start()

        side_copy(t, block, half, piece).start()

        @pl.when(j == 2 * blocks * PIECES - 1)
        def _():
            send_own(t, 1, way)

    def send_back(way, v):
        ahead = upstream(-way)
        block, half = stream(-way, lax.div(v, RETURN_PIECES), ahead)
        combine(block, half, lax.rem(v, RETURN_PIECES), way, True)

    def normed(values, gain):
        mean = jnp.mean(values * values, axis=-1, keepdims=True)
        return (values * lax.rsqrt(mean + epsilon) * gain).astype(kind)

    def first_only(t, act):
        @pl.when(t == 0)
        def _():
            act()

    def project(t, halves):
        values = jnp.concatenate([inputs[t, half] for half in halves], axis=0)
        rows_in = normed(wide(values), mixing_gain[...])
        queries = jnp.dot(rows_in, asking[...], preferred_element_type=jnp.float32).astype(kind)
        raw = jnp.dot(rows_in, compress[...], preferred_element_type=jnp.float32)
        first = context + halves[0] * height
        keys[t, first : first + len(halves) * height] = normed(raw, latent_gain[...])
        for head in range(heads):
            part_of = queries[:, head * head_size : (head + 1) * head_size]
            lat = jnp.dot(part_of, lookup[head], preferred_element_type=jnp.float32).astype(kind)
            for i, half in enumerate(halves):
                q_lat[half, head * height : (head + 1) * height] = lat[i * height : (i + 1) * height]

    def attend_half(t, half):
        table = keys[t, : context + (half + 1) * height]
        scores = lax.dot_general(q_lat[half], table, NT, preferred_element_type=jnp.float32)
        scores = scores * head_size ** (-0.5)
        position = lax.broadcasted_iota(jnp.int32, (height, table.shape[0]), 1)
        query = lax.broadcasted_iota(jnp.int32, (height, table.shape[0]), 0) + half * height
        limit = jnp.where(position < context, lengths[t - section + sections - 1], query + (context + 1))
        visible = (position < limit)[None]
        scores = scores.reshape((heads,) + position.shape)
        scores = jnp.where(visible, scores, -jnp.inf).reshape(heads * height, -1)
        expd = jnp.exp(scores - jnp.max(scores, axis=-1, keepdims=True))
        weight = (expd * (1.0 / jnp.sum(expd, axis=-1, keepdims=True))).astype(kind)
        o_lat = jnp.dot(weight, table, preferred_element_type=jnp.float32).astype(kind)
        outs = []
        for head in range(heads):
            outs.append(
                jnp.dot(
                    o_lat[head * height : (head + 1) * height],
                    content[head],
                    preferred_element_type=jnp.float32,
                ).astype(kind)
            )
        heads_out = jnp.concatenate(outs, axis=1)
        total = wide(inputs[t, half]) + jnp.dot(
            heads_out, merging[...], preferred_element_type=jnp.float32
        )
        residual[half] = total
        first = pl.multiple_of(side * height, height)
        rows_all[t, spot, half, pl.ds(first, height)] = normed(total, expert_gain[...])

    def poll(t, counts):
        after = []
        for way, count in zip((1, -1), counts):
            total = 2 * upstream(way) * PIECES

            @pl.when(count < total)
            def _():
                arrive(t, way, count)

            after.append(jnp.minimum(count + 1, total))
        return tuple(after)

    def catch_up(t, way, count, goal):
        def one(j, carry):
            arrive(t, way, j)
            return carry

        lax.fori_loop(count, goal, one, 0)

    units = 2 * chips
    short = 2 * jnp.minimum(spot, chips - 1 - spot)
    leftward = spot > chips - 1 - spot
    near_way = jnp.where(leftward, -1, 1)

    def unit_of(k, lead):
        own = (k < lead) | (k >= units - 2 + lead)
        v = jnp.maximum(k - lead, 0)
        paired = v < 2 * short
        unit = jnp.where(paired, lax.div(v, 2), v - short)
        from_left = jnp.where(paired, lax.rem(v, 2) == 0, leftward)
        left_block, left_half = stream(1, unit, upstream(1))
        right_block, right_half = stream(-1, unit, upstream(-1))
        block = jnp.where(own, spot, jnp.where(from_left, left_block, right_block))
        half = jnp.where(own, jnp.where(k < units - 1, 0, 1), jnp.where(from_left, left_half, right_half))
        need = jnp.where(own, 0, (unit + 1) * PIECES)
        return block, half, jnp.where(from_left, need, 0), jnp.where(from_left, 0, need)

    def visit(t, k, carry):
        counts, sent = carry[:2], carry[2:]
        lead = jnp.where(t > 0, 1, 0)
        block, half, _, _ = unit_of(k, lead)
        done_block, done_half, _, _ = unit_of(jnp.maximum(k - 1, 0), lead)
        outward = at_end & (done_block != spot) & (k > 0)
        side_half(t, block, half).wait_recv()

        @pl.when(outward)
        def _():
            way = jnp.where(done_block > spot, 1, -1)
            for piece in range(RETURN_PIECES):
                combine(done_block, done_half, piece, way, False)

        @pl.when((k == units - 1) & (lead == 0))
        def _():
            finish(t, 0)

        values = rows_all[t, block, half]
        for e in range(local):
            line = mine * local + e + t * (small_all.shape[2] // ticks)
            columns = []
            for core in range(pair):
                table = small_all[block, core]
                here = lax.broadcasted_iota(jnp.int32, table.shape, 0) == line
                row = jnp.sum(jnp.where(here, table, 0.0), axis=0, keepdims=True)
                column = jnp.broadcast_to(row, (row.shape[1], row.shape[1])).T[:, :1]
                columns.append(jnp.where(half == 0, column[:height], column[height:]))
            share = jnp.concatenate(columns, axis=0)
            gated = jnp.dot(values, gate[e], preferred_element_type=jnp.float32)
            upped = jnp.dot(values, up[e], preferred_element_type=jnp.float32)
            hidden[e] = (gated * jax.nn.sigmoid(gated) * upped * share).astype(kind)
            counts = poll(t, counts)
            if e == 0:
                sent = send_due(sent, 2 * k - 1, k - lead)
        for piece in range(RETURN_PIECES):
            total = None
            for e in range(local):
                term = jnp.dot(
                    hidden[e],
                    down[e, :, piece * chunk : (piece + 1) * chunk],
                    preferred_element_type=jnp.float32,
                )
                total = term if total is None else total + term
            total = total.astype(part.dtype)
            for core in range(pair):
                part[block, half, core, piece] = total[core * height : (core + 1) * height]
            give_copy(block, half, piece).start()
            if piece == RETURN_PIECES // 2 - 1:
                counts = poll(t, counts)

        counts = poll(t, counts)
        after = send_due(sent, 2 * k, k - lead + 1)
        needs = unit_of(jnp.minimum(k + 1, units - 1), lead)[2:]
        ready = []
        for direction, count, need in zip((1, -1), counts, needs):
            goal = jnp.maximum(count, need)
            catch_up(t, direction, count, goal)
            ready.append(goal)
        return (*ready, *after)

    def back_total(way):
        ahead = jnp.where(at_end, 0, upstream(-way))
        return 2 * ahead * RETURN_PIECES

    def back_goal(way, moment, seen):
        beyond = upstream(way) - 1
        due = lax.div(jnp.maximum(11 * moment - 32 - beyond * (moment + 50), 0), 8)
        seen = jnp.clip(seen, 0, units - 2)
        longer = jnp.where(leftward, way < 0, way > 0)
        paired = lax.div(seen + jnp.where(way < 0, 1, 0), 2)
        held = jnp.where(seen <= 2 * short, paired, jnp.where(longer, seen - short, short))
        return jnp.minimum(jnp.minimum(due, held * RETURN_PIECES), back_total(way))

    def send_due(sent, moment, seen):
        after = []
        for direction, count in zip((near_way, -near_way), sent):
            goal = jnp.maximum(count, back_goal(direction, moment, seen))
            return_up(direction, count, goal)
            after.append(goal)
        return tuple(after)

    def return_up(way, count, goal):
        def one(v, carry):
            send_back(way, v)
            return carry

        lax.fori_loop(count, goal, one, 0)

    def finish(t, half):
        for piece in range(RETURN_PIECES):
            columns = pl.ds(piece * chunk, chunk)
            give_copy(spot, half, piece).wait_recv()
            residual[half, :, columns] += wide(part[spot, half, side, piece]) + wide(
                side_in[spot, half, piece]
            )
            for way in (1, -1):

                @pl.when(reach(-way))
                def _():
                    back_copy(spot, half, piece, way, spot - way).wait_recv()
                    slot = spot if way > 0 else chips
                    residual[half, :, columns] += wide(line_in[slot, half, piece])

            results[t, half, :, columns] = residual[half, :, columns].astype(kind)

            @pl.when((section < sections - 1) & (t < ticks - 1))
            def _():
                hop_copy(t, half, piece).start()

    barrier = pltpu.get_barrier_semaphore()

    def hello(condition, device):
        @pl.when(condition)
        def _():
            pl.semaphore_signal(barrier, inc=1, device_id=device, device_id_type=MESH)

    for half in range(HALVES):
        input_copy(0, half).start()
    for load in attention_loads[:3]:
        load.start()
    key_copy(0).start()
    experts_all = local * count
    tokens = HALVES * height
    for t in range(ticks):
        table = jnp.zeros((experts_all, tokens), jnp.float32)
        expert = lax.broadcasted_iota(jnp.int32, table.shape, 0)
        for choice in range(picks_ref.shape[1]):
            named = picks_ref[t, choice] == expert
            table = table + jnp.where(named, shares_ref[t, choice], 0.0)
        small_all[spot, side, t * experts_all : (t + 1) * experts_all] = table
    for distance in range(1, count):
        other = lax.rem(mine + distance, count)
        pl.semaphore_signal(barrier, inc=1, device_id={"expert": other}, device_id_type=MESH)
    section_neighbours = jnp.where((section == 0) | (section == sections - 1), 1, 2)
    hello(section > 0, {"section": section - 1})
    hello(section < sections - 1, {"section": section + 1})
    pl.semaphore_wait(barrier, count - 1 + section_neighbours)
    for distance in range(1, count):
        small_copy(distance).start()

    def tick(t, carry):
        @pl.when(t == 0)
        def _():
            for half in range(HALVES):
                input_copy(0, half).wait()
            for load in attention_loads[:3]:
                load.wait()
            for load in attention_loads[3:]:
                load.start()
            project(0, tuple(range(HALVES)))
            key_copy(0).wait()
            for load in attention_loads[3:]:
                load.wait()
            stage_start(0)
            for load in down_loads:
                load.start()
            for later in range(1, ticks):
                key_copy(later).start()

                @pl.when(section == 0)
                def _():
                    for half in range(HALVES):
                        input_copy(later, half).start()

        for half in range(HALVES):

            @pl.when(t > 0)
            def _():
                @pl.when(section == 0)
                def _():
                    local_copy(opening_hbm.at[half], inputs.at[t, half], input_sem.at[t, half]).wait()

                @pl.when(section > 0)
                def _():
                    place = inputs.at[t, half]
                    remote(place, place, hop_send.at[0], hop_recv.at[t, half], sibling).wait_recv()

                project(t, (half,))
                if half == 0:
                    key_copy(t).wait()

            attend_half(t, half)
            for piece in range(PIECES):
                side_copy(t, spot, half, piece).start()
            for way in (1, -1):
                if half == 0:
                    send_own(t, half, way)
                else:

                    @pl.when(upstream(way) == 0)
                    def _():
                        send_own(t, half, way)

        none = jnp.int32(0)

        def first_tick():
            counts = turn_weights((none, none))
            for load in down_loads:
                load.wait()
            for distance in range(1, count):
                small_copy(distance).wait_recv()
            ready = []
            for way, start, need in zip((1, -1), counts, unit_of(none, none)[2:]):
                goal = jnp.maximum(start, need)
                catch_up(0, way, start, goal)
                ready.append(goal)
            return tuple(ready)

        counts = lax.cond(t == 0, first_tick, lambda: (none, none))
        state = lax.fori_loop(
            0, units, lambda k, state: visit(t, k, state), (*counts, none, none)
        )
        @pl.when(t > 0)
        def _():
            finish(t, 0)

        def rest(v, carry):
            for way, done in zip((near_way, -near_way), state[2:]):

                @pl.when(done + v < back_total(way))
                def _():
                    send_back(way, done + v)

            return carry

        left_over = [back_total(way) - done for way, done in zip((near_way, -near_way), state[2:])]
        lax.fori_loop(0, jnp.maximum(left_over[0], left_over[1]), rest, 0)
        finish(t, 1)

        def settle(block, inner):
            owned = pl.ds(pl.multiple_of(side * height, height), height)
            for way in (1, -1):
                passes = (block <= spot) if way > 0 else (block >= spot)

                @pl.when(passes & reach(way))
                def _():
                    direction = 0 if way > 0 else 1
                    all_sent(rows_all.at[t, block, :, owned], line_send.at[direction, block])

            all_sent(rows_all.at[t, block, :, owned], side_send.at[block])
            all_sent(part.at[block, :, 1 - side], give_send.at[block])

            @pl.when(block != spot)
            def _():
                all_sent(part.at[block, :, side], back_send.at[block])

            return inner

        lax.fori_loop(0, chips, settle, 0)
        return carry

    lax.fori_loop(0, ticks, tick, 0)

    for distance in range(1, count):
        small_copy(distance).wait_send()
    for t in range(ticks - 1):

        @pl.when(section < sections - 1)
        def _():
            all_sent(results.at[t], hop_send.at[t])


def relay(
    lengths,
    picks,
    shares,
    mixing_gain,
    latent_gain,
    expert_gain,
    opening,
    incoming,
    stored,
    asking,
    compress,
    lookup,
    content,
    merging,
    gate,
    up,
    down,
):
    count = lax.axis_size("expert")
    pair = 2
    chips = count // pair
    ticks, context, latent = stored.shape
    kind = opening.dtype
    height = opening.shape[0] // HALVES
    width = opening.shape[1]
    local, inner = down.shape[:2]
    heads = lookup.shape[0]
    chunk = width // RETURN_PIECES
    dma = pltpu.SemaphoreType.DMA
    hbm = pl.BlockSpec(memory_space=pl.ANY)
    vmem = pl.BlockSpec(memory_space=pltpu.VMEM)
    smem = pl.BlockSpec(memory_space=pltpu.SMEM)
    cut = (HALVES, height, width)
    return pl.pallas_call(
        functools.partial(relay_kernel, ticks),
        out_shape=jax.ShapeDtypeStruct((ticks,) + cut, kind),
        in_specs=[smem] + [vmem] * 5 + [hbm] * 11,
        out_specs=vmem,
        scratch_shapes=[
            *[pltpu.VMEM(w.shape, kind) for w in (asking, compress, lookup, content, merging)],
            *[pltpu.VMEM((local, width, inner), kind) for _ in range(2)],
            pltpu.VMEM((local, inner, width), kind),
            pltpu.VMEM((pl.cdiv(inner, 128), 128, width), kind),
            pltpu.VMEM((ticks, context + HALVES * height, latent), kind),
            pltpu.VMEM((ticks,) + cut, kind),
            pltpu.VMEM(cut, jnp.float32),
            pltpu.VMEM((HALVES, heads * height, latent), kind),
            pltpu.VMEM((ticks, chips, HALVES, pair * height, width), kind),
            pltpu.VMEM((chips, pair, ticks * local * count, HALVES * height), shares.dtype),
            pltpu.VMEM((local, pair * height, inner), kind),
            pltpu.VMEM((chips, HALVES, pair, RETURN_PIECES, height, chunk), kind),
            pltpu.VMEM((chips, HALVES, RETURN_PIECES, height, chunk), kind),
            pltpu.VMEM((chips + 1, HALVES, RETURN_PIECES, height, chunk), kind),
            dma((ticks, HALVES)),
            dma((5,)),
            dma((local,)),
            dma((pl.cdiv(inner, 128),)),
            dma((ticks,)),
            dma((2, chips)),
            dma((ticks, chips, HALVES, PIECES)),
            dma((chips,)),
            dma((ticks, chips, HALVES)),
            dma((count,)),
            dma((count,)),
            dma((chips,)),
            dma((chips, HALVES, RETURN_PIECES)),
            dma((chips,)),
            dma((chips + 1, HALVES, RETURN_PIECES)),
            dma((ticks,)),
            dma((ticks, HALVES)),
        ],
        compiler_params=pltpu.CompilerParams(
            collective_id=0, has_side_effects=True, vmem_limit_bytes=58 * 2**20
        ),
    )(
        lengths,
        picks,
        shares,
        mixing_gain,
        latent_gain,
        expert_gain,
        opening.reshape(cut),
        incoming.reshape((ticks - 1,) + cut),
        stored,
        asking,
        compress,
        lookup,
        content,
        merging,
        gate,
        up,
        down,
    ).reshape(ticks, HALVES * height, width)


def shifted(value, axis, steps):
    count = lax.axis_size(axis)
    initial, last = (max(0, -steps), min(count, count - steps))
    return lax.ppermute(value, axis, [(source, source + steps) for source in range(initial, last)])


def row_norm(values, gain_row):
    return (
        values * lax.rsqrt(jnp.mean(values * values, axis=-1, keepdims=True) + epsilon) * gain_row
    )


def attend(q_lat, cache_rows, new_rows, length, score_scale):
    piece_list = q_lat.shape[0]
    context = cache_rows.shape[0]
    key_rows = jnp.concatenate([cache_rows, new_rows], axis=0)
    scores = (
        jnp.einsum("thl,kl->thk", q_lat, key_rows, preferred_element_type=jnp.float32) * score_scale
    )
    position = lax.broadcasted_iota(jnp.int32, (piece_list, context + piece_list), 1)
    query_pos = lax.broadcasted_iota(jnp.int32, (piece_list, context + piece_list), 0)
    visible = jnp.where(position < context, position < length, position - context <= query_pos)
    scores = jnp.where(visible[:, None, :], scores, -jnp.inf)
    row_max = jnp.max(scores, axis=-1, keepdims=True)
    expd = jnp.where(visible[:, None, :], jnp.exp(scores - row_max), 0.0)
    attention = (expd / jnp.sum(expd, axis=-1, keepdims=True)).astype(jnp.bfloat16)
    return jnp.einsum(
        "thk,kl->thl", attention, key_rows, preferred_element_type=jnp.float32
    ).astype(jnp.bfloat16)


def shards(
    opening_residual,
    incoming_residual,
    stored_summaries,
    stored_counts,
    picked_specialists,
    chooser_mixing_share,
    mixing_scale_factor,
    asking_projection,
    summary_lookup_factor,
    summary_content_factor,
    merging_projection,
    compress_projection,
    summary_scale_factor,
    specialist_scale_factor,
    specialist_switch_factor,
    specialist_widen_factor,
    specialist_contract_factor,
):
    segment_ordinal = lax.axis_index("section")
    section_count = lax.axis_size("section")
    sources = lax.axis_size("expert")
    tick_count = stored_summaries.shape[0]
    piece_list = opening_residual.shape[1]
    inner_feature_midcount = opening_residual.shape[2]
    full_width = mixing_scale_factor.shape[1]
    local_heads = summary_lookup_factor.shape[1]
    head_size = summary_lookup_factor.shape[2]
    top_count = picked_specialists.shape[3]
    expert_local = specialist_switch_factor.shape[1]
    score_scale = head_size ** (-0.5)
    if lax.axis_size("tensor") == 1 and sources % 2 == 0 and section_count > 1 and tick_count > 1:
        results = relay(
            stored_counts[:, 0],
            jnp.transpose(picked_specialists, (0, 3, 1, 2)),
            jnp.transpose(chooser_mixing_share, (0, 3, 1, 2)),
            mixing_scale_factor,
            summary_scale_factor,
            specialist_scale_factor,
            opening_residual[0],
            incoming_residual,
            stored_summaries[:, 0, 0],
            asking_projection[0],
            compress_projection[0],
            summary_lookup_factor[0],
            summary_content_factor[0],
            merging_projection[0],
            jnp.swapaxes(specialist_switch_factor[0], 1, 2),
            jnp.swapaxes(specialist_widen_factor[0], 1, 2),
            specialist_contract_factor[0],
        )
        return results[:, None]
    expert_ids = lax.broadcasted_iota(jnp.int32, (1, 1, 1, expert_local * sources), 3)
    shares_dense = jnp.sum(
        jnp.where(
            picked_specialists[:, 0][..., None] == expert_ids,
            chooser_mixing_share[:, 0][..., None],
            0.0,
        ),
        axis=2,
    )
    shares_dense = jnp.swapaxes(shares_dense, 1, 2)
    outputs = []
    present_carry = opening_residual[0]
    section_out = present_carry
    for step_index in range(tick_count):
        if step_index > 0:
            handed = shifted(section_out, "section", 1)
            present_carry = jnp.where(
                segment_ordinal == 0, incoming_residual[step_index - 1], handed
            )
        micro_index = step_index - segment_ordinal + section_count - 1
        length = lax.dynamic_index_in_dim(stored_counts[:, 0], micro_index, 0, keepdims=False)
        full_rows = lax.all_gather(present_carry, "tensor", axis=1, tiled=True)
        normed = row_norm(full_rows.astype(jnp.float32), mixing_scale_factor[0]).astype(
            jnp.bfloat16
        )
        queries = jnp.dot(normed, asking_projection[0], preferred_element_type=jnp.float32).astype(
            jnp.bfloat16
        )
        queries = queries.reshape(piece_list, local_heads, head_size)
        q_lat = jnp.einsum(
            "thd,hdl->thl", queries, summary_lookup_factor[0], preferred_element_type=jnp.float32
        ).astype(jnp.bfloat16)
        latent_part = jnp.dot(normed, compress_projection[0], preferred_element_type=jnp.float32)
        latent_raw = lax.all_gather(
            latent_part.astype(jnp.bfloat16), "tensor", axis=1, tiled=True
        ).astype(latent_part.dtype)
        new_latent = row_norm(latent_raw, summary_scale_factor[0]).astype(jnp.bfloat16)
        o_lat = attend(q_lat, stored_summaries[step_index, 0, 0], new_latent, length, score_scale)
        heads_out = jnp.einsum(
            "thl,hld->thd", o_lat, summary_content_factor[0], preferred_element_type=jnp.float32
        ).astype(jnp.bfloat16)
        heads_out = heads_out.reshape(piece_list, local_heads * head_size)
        head_terms = jnp.dot(heads_out, merging_projection[0], preferred_element_type=jnp.float32)
        residual = present_carry.astype(jnp.float32) + lax.psum_scatter(
            head_terms.astype(jnp.bfloat16), "tensor", scatter_dimension=1, tiled=True
        ).astype(jnp.float32)
        squares = lax.psum(jnp.sum(residual * residual, axis=1), "tensor")
        moe_input = (
            residual
            * lax.rsqrt(squares / full_width + epsilon)[:, None]
            * specialist_scale_factor[0]
        ).astype(jnp.bfloat16)
        whole_rows = lax.all_gather(moe_input, "tensor", axis=1, tiled=True)
        routed = experts(
            whole_rows,
            shares_dense[step_index],
            jnp.swapaxes(specialist_switch_factor[0], 1, 2),
            jnp.swapaxes(specialist_widen_factor[0], 1, 2),
            specialist_contract_factor[0],
        )
        if lax.axis_size("tensor") > 1:
            routed = lax.psum_scatter(
                routed.astype(jnp.bfloat16), "tensor", scatter_dimension=1, tiled=True
            ).astype(jnp.float32)
        section_out = (residual + routed).astype(jnp.bfloat16)
        outputs.append(section_out)
    return jnp.stack(outputs)[:, None]


def solution(mesh):
    in_specs = (
        P("section", ("groups", "expert"), "tensor"),
        P(None, ("groups", "expert"), "tensor"),
        P(None, "section", ("groups", "expert"), None, None),
        P(None, ("groups", "expert")),
        P(None, "section", ("groups", "expert"), None),
        P(None, "section", ("groups", "expert"), None),
        P("section", None),
        P("section", None, "tensor"),
        P("section", "tensor", None, None),
        P("section", "tensor", None, None),
        P("section", "tensor", None),
        P("section", None, "tensor"),
        P("section", None),
        P("section", "tensor"),
        P("section", "expert", None, "tensor"),
        P("section", "expert", None, "tensor"),
        P("section", "expert", "tensor", None),
    )
    out_specs = P(None, "section", ("groups", "expert"), "tensor")
    return jax.shard_map(shards, mesh=mesh, in_specs=in_specs, out_specs=out_specs, check_vma=False)
```

```python
import functools

import jax
import jax.numpy as jnp
from jax import lax
from jax.experimental import pallas as pl
from jax.experimental.pallas import tpu as pltpu
from jax.sharding import PartitionSpec as P


epsilon = 1e-06


MESH = pl.DeviceIdType.MESH
PIECES = 4
RETURN_PIECES = 4
NT = (((1,), (1,)), ((), ()))


def place_on_line():
    count = lax.axis_size("expert")
    pair = 2 if count % 2 == 0 else 1
    mine = lax.axis_index("expert")
    return count // pair, pair, mine, mine // pair, lax.rem(mine, pair)


def greet(chips, pair, mine, spot, side):
    barrier = pltpu.get_barrier_semaphore()

    def hello(other):
        pl.semaphore_signal(barrier, inc=1, device_id={"expert": other}, device_id_type=MESH)

    @pl.when(spot > 0)
    def _():
        hello(mine - pair)

    @pl.when(spot < chips - 1)
    def _():
        hello(mine + pair)

    if pair == 2:
        hello(mine + 1 - 2 * side)
    inner = (spot > 0) & (spot < chips - 1)

    @pl.when(inner)
    def _():
        pl.semaphore_wait(barrier, pair + 1)

    @pl.when(jnp.logical_not(inner))
    def _():
        pl.semaphore_wait(barrier, pair)


def remote(src, dst, send, recv, other):
    return pltpu.make_async_remote_copy(
        src_ref=src,
        dst_ref=dst,
        send_sem=send,
        recv_sem=recv,
        device_id={"expert": other},
        device_id_type=MESH,
    )


def visiting_order(k, spot, chips):
    low = jnp.minimum(spot, chips - 1 - spot)
    near = (k + 1) // 2
    around = spot + jnp.where(lax.rem(k, 2) == 0, near, -near)
    rest = jnp.where(spot < chips - 1 - spot, k, chips - 1 - k)
    return jnp.where(k <= 2 * low, around, rest)


def experts_kernel(
    own_ref,
    small_ref,
    gate_hbm,
    up_hbm,
    down_hbm,
    sum_ref,
    gate,
    up,
    down,
    rows_all,
    small_all,
    hidden,
    part,
    side_in,
    line_in,
    own_sem,
    weight_sem,
    line_send,
    line_recv,
    side_send,
    side_recv,
    give_send,
    give_recv,
    back_send,
    back_recv,
):
    chips, pair, mine, spot, side = place_on_line()
    height, width = own_ref.shape
    local = gate.shape[0]
    step = height // PIECES
    chunk = width // RETURN_PIECES
    sibling = mine + 1 - 2 * side
    at_end = (spot == 0) | (spot == chips - 1)

    loads = []
    for index, (source, target) in enumerate(((gate_hbm, gate), (up_hbm, up), (down_hbm, down))):
        for e in range(local):
            loads.append(
                pltpu.make_async_copy(source.at[e], target.at[e], weight_sem.at[index, e])
            )

    def rows(block, core, piece):
        if piece == PIECES:
            return small_all.at[block, core]
        first = pl.multiple_of(core * height + piece * step, step)
        return rows_all.at[block, pl.ds(first, step)]

    def origin(block, piece):
        if block is not None:
            return rows(block, side, piece)
        return small_ref if piece == PIECES else own_ref.at[pl.ds(piece * step, step)]

    def line_copy(block, piece, way):
        where = spot if block is None else block
        direction = 0 if way > 0 else 1
        return remote(
            origin(block, piece),
            rows(where, side, piece),
            line_send.at[direction, where, piece],
            line_recv.at[where, piece],
            mine + way * pair,
        )

    def side_copy(block, piece):
        where = spot if block is None else block
        return remote(
            origin(block, piece),
            rows(where, side, piece),
            side_send.at[where, piece],
            side_recv.at[where, piece],
            sibling,
        )

    def onward(block, piece, way, act):
        @pl.when((spot < chips - 1) if way > 0 else (spot > 0))
        def _():
            act(line_copy(block, piece, way))

    def passing(far, act):
        for piece in range(PIECES + 1):
            for way in (1, -1):
                block = spot - way * far

                @pl.when((block >= 0) if way > 0 else (block < chips))
                def _():
                    act(block, piece, way)

    def give_copy(block, piece):
        return remote(
            part.at[block, 1 - side, piece],
            side_in.at[block, piece],
            give_send.at[block, piece],
            give_recv.at[block, piece],
            sibling,
        )

    def back_copy(block, piece, way):
        direction = (1 - way) // 2
        return remote(
            part.at[block, side, piece],
            line_in.at[direction, block, piece],
            back_send.at[block, piece],
            back_recv.at[direction, block, piece],
            mine + way * pair,
        )

    def wide(value):
        return value.astype(jnp.float32)

    def combine(block, piece, way, from_line):
        give_copy(block, piece).wait_recv()
        value = wide(part[block, side, piece]) + wide(side_in[block, piece])
        if from_line:
            back_copy(block, piece, way).wait_recv()
            value = value + wide(line_in[(1 - way) // 2, block, piece])
        part[block, side, piece] = value.astype(part.dtype)
        back_copy(block, piece, way).start()

    greet(chips, pair, mine, spot, side)
    for piece in (PIECES, *range(PIECES)):
        for way in (1, -1):
            onward(None, piece, way, lambda copy: copy.start())
        side_copy(None, piece).start()
    keep = pltpu.make_async_copy(
        own_ref, rows_all.at[spot, pl.ds(pl.multiple_of(side * height, height), height)], own_sem.at[0]
    )
    keep.start()
    keep_small = pltpu.make_async_copy(small_ref, small_all.at[spot, side], own_sem.at[1])
    keep_small.start()
    for load in loads:
        load.start()
    keep.wait()
    keep_small.wait()
    for load in loads:
        load.wait()

    def visit(k, carry):
        block = visiting_order(k, spot, chips)
        way = jnp.where(block > spot, 1, -1)
        outward = at_end & (k > 0)
        for piece in range(PIECES + 1):
            side_copy(block, piece).wait_recv()
        values = rows_all[block]
        for e in range(local):
            chosen_expert = mine * local + e
            columns = []
            for core in range(pair):
                table = small_all[block, core]
                here = lax.broadcasted_iota(jnp.int32, table.shape, 0) == chosen_expert
                row = jnp.sum(jnp.where(here, table, 0.0), axis=0, keepdims=True)
                columns.append(jnp.broadcast_to(row, (height, height)).T[:, :1])
            share = jnp.concatenate(columns, axis=0)
            gated = lax.dot_general(values, gate[e], NT, preferred_element_type=jnp.float32)
            upped = lax.dot_general(values, up[e], NT, preferred_element_type=jnp.float32)
            hidden[e] = (gated * jax.nn.sigmoid(gated) * upped * share).astype(hidden.dtype)
        for piece in range(RETURN_PIECES):
            total = None
            for e in range(local):
                term = jnp.dot(
                    hidden[e],
                    down[e, :, piece * chunk : (piece + 1) * chunk],
                    preferred_element_type=jnp.float32,
                )
                total = term if total is None else total + term
            total = total.astype(part.dtype)
            for core in range(pair):
                part[block, core, piece] = total[core * height : (core + 1) * height]
            give_copy(block, piece).start()
            if piece > 0:

                @pl.when(outward)
                def _():
                    combine(block, piece - 1, way, False)

        @pl.when(outward)
        def _():
            combine(block, RETURN_PIECES - 1, way, False)

        @pl.when(k < chips - 1)
        def _():
            def receive(block, piece, way):
                line_copy(block, piece, way).wait_recv()
                onward(block, piece, way, lambda copy: copy.start())
                side_copy(block, piece).start()

            passing(k + 1, receive)

        return carry

    lax.fori_loop(0, chips, visit, 0)

    left_first = 2 * spot <= chips - 1

    def relay(a, carry):
        for piece in range(RETURN_PIECES):
            for turn in range(2):
                way = jnp.where(left_first, 1 - 2 * turn, 2 * turn - 1)
                block = jnp.where(way > 0, a, chips - 1 - a)
                valid = jnp.where(way > 0, block > spot, block < spot) & jnp.logical_not(at_end)

                @pl.when(valid)
                def _():
                    combine(block, piece, way, True)

        return carry

    lax.fori_loop(1, chips, relay, 0)
    for piece in range(RETURN_PIECES):
        give_copy(spot, piece).wait_recv()
        columns = pl.ds(piece * chunk, chunk)
        sum_ref[:, columns] = wide(part[spot, side, piece]) + wide(side_in[spot, piece])
        for way in (1, -1):

            @pl.when((spot > 0) if way > 0 else (spot < chips - 1))
            def _():
                back_copy(spot, piece, way).wait_recv()
                sum_ref[:, columns] += wide(line_in[(1 - way) // 2, spot, piece])

    for piece in range(PIECES + 1):
        for way in (1, -1):
            onward(None, piece, way, lambda copy: copy.wait_send())
        side_copy(None, piece).wait_send()

    def settle(far, carry):
        def sent(block, piece, way):
            onward(block, piece, way, lambda copy: copy.wait_send())
            side_copy(block, piece).wait_send()

        passing(far, sent)
        return carry

    lax.fori_loop(1, chips, settle, 0)

    def settle_back(block, carry):
        for piece in range(RETURN_PIECES):
            give_copy(block, piece).wait_send()

            @pl.when(block != spot)
            def _():
                back_copy(block, piece, jnp.where(block > spot, 1, -1)).wait_send()

        return carry

    lax.fori_loop(0, chips, settle_back, 0)


def experts(own, small, gate, up, down):
    count = lax.axis_size("expert")
    pair = 2
    chips = count // pair
    height, width = own.shape
    local, inner = down.shape[:2]
    kind = own.dtype
    chunk = width // RETURN_PIECES
    blocks = chips * pair * height * width * 2
    weights = 3 * local * inner * width * 2
    dma = pltpu.SemaphoreType.DMA
    hbm = pl.BlockSpec(memory_space=pl.ANY)
    vmem = pl.BlockSpec(memory_space=pltpu.VMEM)
    return pl.pallas_call(
        experts_kernel,
        out_shape=jax.ShapeDtypeStruct((height, width), jnp.float32),
        in_specs=[vmem, vmem, hbm, hbm, hbm],
        out_specs=vmem,
        scratch_shapes=[
            pltpu.VMEM((local, inner, width), kind),
            pltpu.VMEM((local, inner, width), kind),
            pltpu.VMEM((local, inner, width), kind),
            pltpu.VMEM((chips, pair * height, width), kind),
            pltpu.VMEM((chips, pair) + small.shape, small.dtype),
            pltpu.VMEM((local, pair * height, inner), kind),
            pltpu.VMEM((chips, pair, RETURN_PIECES, height, chunk), kind),
            pltpu.VMEM((chips, RETURN_PIECES, height, chunk), kind),
            pltpu.VMEM((2, chips, RETURN_PIECES, height, chunk), kind),
            dma((2,)),
            dma((3, local)),
            dma((2, chips, PIECES + 1)),
            dma((chips, PIECES + 1)),
            dma((chips, PIECES + 1)),
            dma((chips, PIECES + 1)),
            dma((chips, RETURN_PIECES)),
            dma((chips, RETURN_PIECES)),
            dma((chips, RETURN_PIECES)),
            dma((2, chips, RETURN_PIECES)),
        ],
        compiler_params=pltpu.CompilerParams(
            collective_id=0, has_side_effects=True, vmem_limit_bytes=4 * blocks + weights + 12 * 2**20
        ),
        cost_estimate=pl.CostEstimate(
            flops=2 * weights * blocks // (width * 4), bytes_accessed=32 * blocks, transcendentals=0
        ),
    )(own, small, gate, up, down)


HALVES = 2


def relay_kernel(ticks, *refs):
    (
        lengths,
        picks_ref,
        shares_ref,
        mixing_gain,
        latent_gain,
        expert_gain,
        opening_hbm,
        incoming_hbm,
        stored_hbm,
        asking_hbm,
        compress_hbm,
        lookup_hbm,
        content_hbm,
        merging_hbm,
        gate_hbm,
        up_hbm,
        down_hbm,
    ) = refs[:17]
    results = refs[17]
    (
        asking,
        compress,
        lookup,
        content,
        merging,
        gate,
        up,
        down,
        stage,
        keys,
        inputs,
        residual,
        q_lat,
        rows_all,
        small_all,
        hidden,
        part,
        side_in,
        line_in,
        input_sem,
        load_sem,
        down_sem,
        stage_sem,
        key_sem,
        line_send,
        line_recv,
        side_send,
        side_recv,
        small_send,
        small_recv,
        give_send,
        give_recv,
        back_send,
        back_recv,
        hop_send,
        hop_recv,
    ) = refs[18:]
    chips, pair, mine, spot, side = place_on_line()
    section = lax.axis_index("section")
    sections = lax.axis_size("section")
    _, _, height, width = inputs.shape
    count = chips * pair
    inner = down.shape[1]
    local = gate.shape[0]
    heads, head_size, latent = lookup.shape
    context = keys.shape[1] - HALVES * height
    chunk = width // RETURN_PIECES
    step = height // PIECES
    sibling = mine + 1 - 2 * side
    at_end = (spot == 0) | (spot == chips - 1)
    kind = rows_all.dtype

    def wide(value):
        return value.astype(jnp.float32)

    def local_copy(source, target, sem):
        return pltpu.make_async_copy(source, target, sem)

    def input_copy(t, half):
        source = opening_hbm.at[half] if t == 0 else incoming_hbm.at[t - 1, half]
        return local_copy(source, inputs.at[t, half], input_sem.at[t, half])

    def key_copy(t):
        return local_copy(stored_hbm.at[t], keys.at[t, pl.ds(0, context)], key_sem.at[t])

    attention_loads = [
        local_copy(source, target, load_sem.at[index])
        for index, (source, target) in enumerate(
            (
                (asking_hbm, asking),
                (compress_hbm, compress),
                (lookup_hbm, lookup),
                (content_hbm, content),
                (merging_hbm, merging),
            )
        )
    ]
    down_loads = [local_copy(down_hbm.at[e], down.at[e], down_sem.at[e]) for e in range(local)]
    raw = [(source, target, e) for e in range(local) for source, target in ((gate_hbm, gate), (up_hbm, up))]
    block_rows = stage.shape[1]
    full = inner // block_rows
    tail = inner - full * block_rows

    def stage_copy(matrix, c, size):
        source, _, e = raw[matrix]
        first = pl.multiple_of(c * block_rows, block_rows)
        return local_copy(
            source.at[e, pl.ds(first, size)], stage.at[c, pl.ds(0, size)], stage_sem.at[c]
        )

    def stage_start(matrix):
        for c in range(full):
            stage_copy(matrix, c, block_rows).start()
        if tail:
            stage_copy(matrix, full, tail).start()

    def turn_weights(counts):
        for matrix in range(len(raw)):
            _, target, e = raw[matrix]

            def turn(c, carry):
                stage_copy(matrix, c, block_rows).wait()
                first = pl.multiple_of(c * block_rows, block_rows)
                target[e, :, pl.ds(first, block_rows)] = stage[c].T
                if matrix + 1 < len(raw):
                    stage_copy(matrix + 1, c, block_rows).start()
                return carry

            lax.fori_loop(0, full, turn, 0)
            if tail:
                stage_copy(matrix, full, tail).wait()
                target[e, :, full * block_rows :] = stage[full, :tail].T
                if matrix + 1 < len(raw):
                    stage_copy(matrix + 1, full, tail).start()

            counts = poll(0, counts)
        return counts

    def reach(way):
        return (spot < chips - 1) if way > 0 else (spot > 0)

    def rows(t, block, half, piece):
        first = pl.multiple_of(side * height + piece * step, step)
        return rows_all.at[t, block, half, pl.ds(first, step)]

    def line_copy(t, block, half, piece, way):
        direction = 0 if way > 0 else 1
        place = rows(t, block, half, piece)
        return remote(
            place,
            place,
            line_send.at[direction, block],
            line_recv.at[t, block, half, piece],
            mine + way * pair,
        )

    def side_copy(t, block, half, piece):
        place = rows(t, block, half, piece)
        return remote(
            place,
            place,
            side_send.at[block],
            side_recv.at[t, block, half],
            sibling,
        )

    def whole_rows(t, block, half, other, send, recv):
        place = rows_all.at[t, block, half, pl.ds(pl.multiple_of(side * height, height), height)]
        return remote(place, place, send, recv, other)

    def side_half(t, block, half):
        return whole_rows(t, block, half, sibling, side_send.at[block], side_recv.at[t, block, half])

    def all_sent(target, send):
        remote(target, target, send, side_recv.at[0, 0, 0], sibling).wait_send()

    def small_copy(distance):
        place = small_all.at[spot, side]
        return remote(
            place,
            place,
            small_send.at[distance],
            small_recv.at[distance],
            lax.rem(mine + distance, count),
        )

    def give_copy(block, half, piece):
        return remote(
            part.at[block, half, 1 - side, piece],
            side_in.at[block, half, piece],
            give_send.at[block],
            give_recv.at[block, half, piece],
            sibling,
        )

    def back_copy(block, half, piece, way, sender):
        slot = jnp.where((block == sender + way) & (way < 0), chips, block)
        return remote(
            part.at[block, half, side, piece],
            line_in.at[slot, half, piece],
            back_send.at[block],
            back_recv.at[slot, half, piece],
            mine + way * pair,
        )

    def combine(block, half, piece, way, from_line):
        give_copy(block, half, piece).wait_recv()
        value = wide(part[block, half, side, piece]) + wide(side_in[block, half, piece])
        if from_line:
            back_copy(block, half, piece, way, spot - way).wait_recv()
            value = value + wide(line_in[block, half, piece])
        part[block, half, side, piece] = value.astype(part.dtype)
        back_copy(block, half, piece, way, spot).start()

    def hop_copy(t, half, piece):
        columns = pl.ds(piece * chunk, chunk)
        return pltpu.make_async_remote_copy(
            src_ref=results.at[t, half, :, columns],
            dst_ref=inputs.at[t + 1, half, :, columns],
            send_sem=hop_send.at[t],
            recv_sem=hop_recv.at[t + 1, half],
            device_id={"section": section + 1},
            device_id_type=MESH,
        )

    def stream(way, unit, blocks):
        first = unit < blocks
        near = spot - way * (1 + unit)
        back = unit - blocks
        far = jnp.where(way > 0, back, chips - 1 - back)
        return jnp.where(first, near, far), jnp.where(first, 0, 1)

    def upstream(way):
        return jnp.where(way > 0, spot, chips - 1 - spot)

    def send_own(t, half, way):
        for piece in range(PIECES):

            @pl.when(reach(way))
            def _():
                line_copy(t, spot, half, piece, way).start()

    def arrive(t, way, j):
        blocks = upstream(way)
        block, half = stream(way, lax.div(j, PIECES), blocks)
        piece = lax.rem(j, PIECES)
        line_copy(t, block, half, piece, way).wait_recv()

        @pl.when(reach(way))
        def _():
            line_copy(t, block, half, piece, way).start()

        side_copy(t, block, half, piece).start()

        @pl.when(j == 2 * blocks * PIECES - 1)
        def _():
            send_own(t, 1, way)

    def send_back(way, v):
        ahead = upstream(-way)
        block, half = stream(-way, lax.div(v, RETURN_PIECES), ahead)
        combine(block, half, lax.rem(v, RETURN_PIECES), way, True)

    def normed(values, gain):
        mean = jnp.mean(values * values, axis=-1, keepdims=True)
        return (values * lax.rsqrt(mean + epsilon) * gain).astype(kind)

    def first_only(t, act):
        @pl.when(t == 0)
        def _():
            act()

    def project(t, halves):
        values = jnp.concatenate([inputs[t, half] for half in halves], axis=0)
        rows_in = normed(wide(values), mixing_gain[...])
        queries = jnp.dot(rows_in, asking[...], preferred_element_type=jnp.float32).astype(kind)
        raw = jnp.dot(rows_in, compress[...], preferred_element_type=jnp.float32)
        first = context + halves[0] * height
        keys[t, first : first + len(halves) * height] = normed(raw, latent_gain[...])
        for head in range(heads):
            part_of = queries[:, head * head_size : (head + 1) * head_size]
            lat = jnp.dot(part_of, lookup[head], preferred_element_type=jnp.float32).astype(kind)
            for i, half in enumerate(halves):
                q_lat[half, head * height : (head + 1) * height] = lat[i * height : (i + 1) * height]

    def attend_half(t, half):
        table = keys[t, : context + (half + 1) * height]
        scores = lax.dot_general(q_lat[half], table, NT, preferred_element_type=jnp.float32)
        scores = scores * head_size ** (-0.5)
        position = lax.broadcasted_iota(jnp.int32, (height, table.shape[0]), 1)
        query = lax.broadcasted_iota(jnp.int32, (height, table.shape[0]), 0) + half * height
        limit = jnp.where(position < context, lengths[t - section + sections - 1], query + (context + 1))
        visible = (position < limit)[None]
        scores = scores.reshape((heads,) + position.shape)
        scores = jnp.where(visible, scores, -jnp.inf).reshape(heads * height, -1)
        expd = jnp.exp(scores - jnp.max(scores, axis=-1, keepdims=True))
        weight = (expd * (1.0 / jnp.sum(expd, axis=-1, keepdims=True))).astype(kind)
        o_lat = jnp.dot(weight, table, preferred_element_type=jnp.float32).astype(kind)
        outs = []
        for head in range(heads):
            outs.append(
                jnp.dot(
                    o_lat[head * height : (head + 1) * height],
                    content[head],
                    preferred_element_type=jnp.float32,
                ).astype(kind)
            )
        heads_out = jnp.concatenate(outs, axis=1)
        total = wide(inputs[t, half]) + jnp.dot(
            heads_out, merging[...], preferred_element_type=jnp.float32
        )
        residual[half] = total
        first = pl.multiple_of(side * height, height)
        rows_all[t, spot, half, pl.ds(first, height)] = normed(total, expert_gain[...])

    def poll(t, counts):
        after = []
        for way, count in zip((1, -1), counts):
            total = 2 * upstream(way) * PIECES

            @pl.when(count < total)
            def _():
                arrive(t, way, count)

            after.append(jnp.minimum(count + 1, total))
        return tuple(after)

    def catch_up(t, way, count, goal):
        def one(j, carry):
            arrive(t, way, j)
            return carry

        lax.fori_loop(count, goal, one, 0)

    units = 2 * chips
    short = 2 * jnp.minimum(spot, chips - 1 - spot)
    leftward = spot > chips - 1 - spot
    near_way = jnp.where(leftward, -1, 1)

    def unit_of(k, lead):
        own = (k < lead) | (k >= units - 2 + lead)
        v = jnp.maximum(k - lead, 0)
        paired = v < 2 * short
        unit = jnp.where(paired, lax.div(v, 2), v - short)
        from_left = jnp.where(paired, lax.rem(v, 2) == 0, leftward)
        left_block, left_half = stream(1, unit, upstream(1))
        right_block, right_half = stream(-1, unit, upstream(-1))
        block = jnp.where(own, spot, jnp.where(from_left, left_block, right_block))
        half = jnp.where(own, jnp.where(k < units - 1, 0, 1), jnp.where(from_left, left_half, right_half))
        need = jnp.where(own, 0, (unit + 1) * PIECES)
        return block, half, jnp.where(from_left, need, 0), jnp.where(from_left, 0, need)

    def visit(t, k, carry):
        counts, sent = carry[:2], carry[2:]
        lead = jnp.where(t > 0, 1, 0)
        block, half, _, _ = unit_of(k, lead)
        done_block, done_half, _, _ = unit_of(jnp.maximum(k - 1, 0), lead)
        outward = at_end & (done_block != spot) & (k > 0)
        slack = 28 + 26 * lead
        side_half(t, block, half).wait_recv()

        @pl.when(outward)
        def _():
            way = jnp.where(done_block > spot, 1, -1)
            for piece in range(RETURN_PIECES // 2, RETURN_PIECES):
                combine(done_block, done_half, piece, way, False)

        @pl.when((k == units - 1) & (lead == 0))
        def _():
            finish(t, 0)

        values = rows_all[t, block, half]
        for e in range(local):
            line = mine * local + e + t * (small_all.shape[2] // ticks)
            columns = []
            for core in range(pair):
                table = small_all[block, core]
                here = lax.broadcasted_iota(jnp.int32, table.shape, 0) == line
                row = jnp.sum(jnp.where(here, table, 0.0), axis=0, keepdims=True)
                column = jnp.broadcast_to(row, (row.shape[1], row.shape[1])).T[:, :1]
                columns.append(jnp.where(half == 0, column[:height], column[height:]))
            share = jnp.concatenate(columns, axis=0)
            gated = jnp.dot(values, gate[e], preferred_element_type=jnp.float32)
            upped = jnp.dot(values, up[e], preferred_element_type=jnp.float32)
            hidden[e] = (gated * jax.nn.sigmoid(gated) * upped * share).astype(kind)
            counts = poll(t, counts)
            if e == 0:
                sent = send_due(sent, 2 * k - 1, k - lead, slack)
        for piece in range(RETURN_PIECES):
            total = None
            for e in range(local):
                term = jnp.dot(
                    hidden[e],
                    down[e, :, piece * chunk : (piece + 1) * chunk],
                    preferred_element_type=jnp.float32,
                )
                total = term if total is None else total + term
            total = total.astype(part.dtype)
            for core in range(pair):
                part[block, half, core, piece] = total[core * height : (core + 1) * height]
            give_copy(block, half, piece).start()
            if piece == RETURN_PIECES // 2 - 1:
                counts = poll(t, counts)

        counts = poll(t, counts)

        @pl.when(at_end & (block != spot))
        def _():
            way = jnp.where(block > spot, 1, -1)
            for piece in range(RETURN_PIECES // 2):
                combine(block, half, piece, way, False)

        after = send_due(sent, 2 * k, k - lead + 1, slack)
        needs = unit_of(jnp.minimum(k + 1, units - 1), lead)[2:]
        ready = []
        for direction, count, need in zip((1, -1), counts, needs):
            goal = jnp.maximum(count, need)
            catch_up(t, direction, count, goal)
            ready.append(goal)
        return (*ready, *after)

    def back_total(way):
        ahead = jnp.where(at_end, 0, upstream(-way))
        return 2 * ahead * RETURN_PIECES

    def back_goal(way, moment, seen, slack):
        beyond = upstream(way) - 1
        due = lax.div(jnp.maximum(11 * moment - slack - beyond * (moment + 46), 0), 8)
        seen = jnp.clip(seen, 0, units - 2)
        longer = jnp.where(leftward, way < 0, way > 0)
        paired = lax.div(seen + jnp.where(way < 0, 1, 0), 2)
        held = jnp.where(seen <= 2 * short, paired, jnp.where(longer, seen - short, short))
        return jnp.minimum(jnp.minimum(due, held * RETURN_PIECES), back_total(way))

    def send_due(sent, moment, seen, slack):
        after = []
        for direction, count in zip((near_way, -near_way), sent):
            goal = jnp.maximum(count, back_goal(direction, moment, seen, slack))
            return_up(direction, count, goal)
            after.append(goal)
        return tuple(after)

    def return_up(way, count, goal):
        def one(v, carry):
            send_back(way, v)
            return carry

        lax.fori_loop(count, goal, one, 0)

    def finish(t, half):
        for piece in range(RETURN_PIECES):
            columns = pl.ds(piece * chunk, chunk)
            give_copy(spot, half, piece).wait_recv()
            residual[half, :, columns] += wide(part[spot, half, side, piece]) + wide(
                side_in[spot, half, piece]
            )
            for way in (1, -1):

                @pl.when(reach(-way))
                def _():
                    back_copy(spot, half, piece, way, spot - way).wait_recv()
                    slot = spot if way > 0 else chips
                    residual[half, :, columns] += wide(line_in[slot, half, piece])

            results[t, half, :, columns] = residual[half, :, columns].astype(kind)

            @pl.when((section < sections - 1) & (t < ticks - 1))
            def _():
                hop_copy(t, half, piece).start()

    barrier = pltpu.get_barrier_semaphore()

    def hello(condition, device):
        @pl.when(condition)
        def _():
            pl.semaphore_signal(barrier, inc=1, device_id=device, device_id_type=MESH)

    for half in range(HALVES):
        input_copy(0, half).start()
    for load in attention_loads[:3]:
        load.start()
    key_copy(0).start()
    experts_all = local * count
    tokens = HALVES * height
    for t in range(ticks):
        table = jnp.zeros((experts_all, tokens), jnp.float32)
        expert = lax.broadcasted_iota(jnp.int32, table.shape, 0)
        for choice in range(picks_ref.shape[1]):
            named = picks_ref[t, choice] == expert
            table = table + jnp.where(named, shares_ref[t, choice], 0.0)
        small_all[spot, side, t * experts_all : (t + 1) * experts_all] = table
    for distance in range(1, count):
        other = lax.rem(mine + distance, count)
        pl.semaphore_signal(barrier, inc=1, device_id={"expert": other}, device_id_type=MESH)
    section_neighbours = jnp.where((section == 0) | (section == sections - 1), 1, 2)
    hello(section > 0, {"section": section - 1})
    hello(section < sections - 1, {"section": section + 1})
    pl.semaphore_wait(barrier, count - 1 + section_neighbours)
    for distance in range(1, count):
        small_copy(distance).start()

    def tick(t, carry):
        @pl.when(t == 0)
        def _():
            for half in range(HALVES):
                input_copy(0, half).wait()
            for load in attention_loads[:3]:
                load.wait()
            for load in attention_loads[3:]:
                load.start()
            project(0, tuple(range(HALVES)))
            key_copy(0).wait()
            for load in attention_loads[3:]:
                load.wait()
            stage_start(0)
            for load in down_loads:
                load.start()
            for later in range(1, ticks):
                key_copy(later).start()

                @pl.when(section == 0)
                def _():
                    for half in range(HALVES):
                        input_copy(later, half).start()

        for half in range(HALVES):

            @pl.when(t > 0)
            def _():
                @pl.when(section == 0)
                def _():
                    local_copy(opening_hbm.at[half], inputs.at[t, half], input_sem.at[t, half]).wait()

                @pl.when(section > 0)
                def _():
                    place = inputs.at[t, half]
                    remote(place, place, hop_send.at[0], hop_recv.at[t, half], sibling).wait_recv()

                project(t, (half,))
                if half == 0:
                    key_copy(t).wait()

            attend_half(t, half)
            for piece in range(PIECES):
                side_copy(t, spot, half, piece).start()
            for way in (1, -1):
                if half == 0:
                    send_own(t, half, way)
                else:

                    @pl.when(upstream(way) == 0)
                    def _():
                        send_own(t, half, way)

        none = jnp.int32(0)

        def first_tick():
            counts = turn_weights((none, none))
            for load in down_loads:
                load.wait()
            for distance in range(1, count):
                small_copy(distance).wait_recv()
            ready = []
            for way, start, need in zip((1, -1), counts, unit_of(none, none)[2:]):
                goal = jnp.maximum(start, need)
                catch_up(0, way, start, goal)
                ready.append(goal)
            return tuple(ready)

        counts = lax.cond(t == 0, first_tick, lambda: (none, none))
        state = lax.fori_loop(
            0, units, lambda k, state: visit(t, k, state), (*counts, none, none)
        )
        @pl.when(t > 0)
        def _():
            finish(t, 0)

        def rest(v, carry):
            for way, done in zip((near_way, -near_way), state[2:]):

                @pl.when(done + v < back_total(way))
                def _():
                    send_back(way, done + v)

            return carry

        left_over = [back_total(way) - done for way, done in zip((near_way, -near_way), state[2:])]
        lax.fori_loop(0, jnp.maximum(left_over[0], left_over[1]), rest, 0)
        finish(t, 1)

        def settle(block, inner):
            owned = pl.ds(pl.multiple_of(side * height, height), height)
            for way in (1, -1):
                passes = (block <= spot) if way > 0 else (block >= spot)

                @pl.when(passes & reach(way))
                def _():
                    direction = 0 if way > 0 else 1
                    all_sent(rows_all.at[t, block, :, owned], line_send.at[direction, block])

            all_sent(rows_all.at[t, block, :, owned], side_send.at[block])
            all_sent(part.at[block, :, 1 - side], give_send.at[block])

            @pl.when(block != spot)
            def _():
                all_sent(part.at[block, :, side], back_send.at[block])

            return inner

        lax.fori_loop(0, chips, settle, 0)
        return carry

    lax.fori_loop(0, ticks, tick, 0)

    for distance in range(1, count):
        small_copy(distance).wait_send()
    for t in range(ticks - 1):

        @pl.when(section < sections - 1)
        def _():
            all_sent(results.at[t], hop_send.at[t])


def relay(
    lengths,
    picks,
    shares,
    mixing_gain,
    latent_gain,
    expert_gain,
    opening,
    incoming,
    stored,
    asking,
    compress,
    lookup,
    content,
    merging,
    gate,
    up,
    down,
):
    count = lax.axis_size("expert")
    pair = 2
    chips = count // pair
    ticks, context, latent = stored.shape
    kind = opening.dtype
    height = opening.shape[0] // HALVES
    width = opening.shape[1]
    local, inner = down.shape[:2]
    heads = lookup.shape[0]
    chunk = width // RETURN_PIECES
    dma = pltpu.SemaphoreType.DMA
    hbm = pl.BlockSpec(memory_space=pl.ANY)
    vmem = pl.BlockSpec(memory_space=pltpu.VMEM)
    smem = pl.BlockSpec(memory_space=pltpu.SMEM)
    cut = (HALVES, height, width)
    return pl.pallas_call(
        functools.partial(relay_kernel, ticks),
        out_shape=jax.ShapeDtypeStruct((ticks,) + cut, kind),
        in_specs=[smem] + [vmem] * 5 + [hbm] * 11,
        out_specs=vmem,
        scratch_shapes=[
            *[pltpu.VMEM(w.shape, kind) for w in (asking, compress, lookup, content, merging)],
            *[pltpu.VMEM((local, width, inner), kind) for _ in range(2)],
            pltpu.VMEM((local, inner, width), kind),
            pltpu.VMEM((pl.cdiv(inner, 128), 128, width), kind),
            pltpu.VMEM((ticks, context + HALVES * height, latent), kind),
            pltpu.VMEM((ticks,) + cut, kind),
            pltpu.VMEM(cut, jnp.float32),
            pltpu.VMEM((HALVES, heads * height, latent), kind),
            pltpu.VMEM((ticks, chips, HALVES, pair * height, width), kind),
            pltpu.VMEM((chips, pair, ticks * local * count, HALVES * height), shares.dtype),
            pltpu.VMEM((local, pair * height, inner), kind),
            pltpu.VMEM((chips, HALVES, pair, RETURN_PIECES, height, chunk), kind),
            pltpu.VMEM((chips, HALVES, RETURN_PIECES, height, chunk), kind),
            pltpu.VMEM((chips + 1, HALVES, RETURN_PIECES, height, chunk), kind),
            dma((ticks, HALVES)),
            dma((5,)),
            dma((local,)),
            dma((pl.cdiv(inner, 128),)),
            dma((ticks,)),
            dma((2, chips)),
            dma((ticks, chips, HALVES, PIECES)),
            dma((chips,)),
            dma((ticks, chips, HALVES)),
            dma((count,)),
            dma((count,)),
            dma((chips,)),
            dma((chips, HALVES, RETURN_PIECES)),
            dma((chips,)),
            dma((chips + 1, HALVES, RETURN_PIECES)),
            dma((ticks,)),
            dma((ticks, HALVES)),
        ],
        compiler_params=pltpu.CompilerParams(
            collective_id=0, has_side_effects=True, vmem_limit_bytes=58 * 2**20
        ),
    )(
        lengths,
        picks,
        shares,
        mixing_gain,
        latent_gain,
        expert_gain,
        opening.reshape(cut),
        incoming.reshape((ticks - 1,) + cut),
        stored,
        asking,
        compress,
        lookup,
        content,
        merging,
        gate,
        up,
        down,
    ).reshape(ticks, HALVES * height, width)


def shifted(value, axis, steps):
    count = lax.axis_size(axis)
    initial, last = (max(0, -steps), min(count, count - steps))
    return lax.ppermute(value, axis, [(source, source + steps) for source in range(initial, last)])


def row_norm(values, gain_row):
    return (
        values * lax.rsqrt(jnp.mean(values * values, axis=-1, keepdims=True) + epsilon) * gain_row
    )


def attend(q_lat, cache_rows, new_rows, length, score_scale):
    piece_list = q_lat.shape[0]
    context = cache_rows.shape[0]
    key_rows = jnp.concatenate([cache_rows, new_rows], axis=0)
    scores = (
        jnp.einsum("thl,kl->thk", q_lat, key_rows, preferred_element_type=jnp.float32) * score_scale
    )
    position = lax.broadcasted_iota(jnp.int32, (piece_list, context + piece_list), 1)
    query_pos = lax.broadcasted_iota(jnp.int32, (piece_list, context + piece_list), 0)
    visible = jnp.where(position < context, position < length, position - context <= query_pos)
    scores = jnp.where(visible[:, None, :], scores, -jnp.inf)
    row_max = jnp.max(scores, axis=-1, keepdims=True)
    expd = jnp.where(visible[:, None, :], jnp.exp(scores - row_max), 0.0)
    attention = (expd / jnp.sum(expd, axis=-1, keepdims=True)).astype(jnp.bfloat16)
    return jnp.einsum(
        "thk,kl->thl", attention, key_rows, preferred_element_type=jnp.float32
    ).astype(jnp.bfloat16)


def shards(
    opening_residual,
    incoming_residual,
    stored_summaries,
    stored_counts,
    picked_specialists,
    chooser_mixing_share,
    mixing_scale_factor,
    asking_projection,
    summary_lookup_factor,
    summary_content_factor,
    merging_projection,
    compress_projection,
    summary_scale_factor,
    specialist_scale_factor,
    specialist_switch_factor,
    specialist_widen_factor,
    specialist_contract_factor,
):
    segment_ordinal = lax.axis_index("section")
    section_count = lax.axis_size("section")
    sources = lax.axis_size("expert")
    tick_count = stored_summaries.shape[0]
    piece_list = opening_residual.shape[1]
    inner_feature_midcount = opening_residual.shape[2]
    full_width = mixing_scale_factor.shape[1]
    local_heads = summary_lookup_factor.shape[1]
    head_size = summary_lookup_factor.shape[2]
    top_count = picked_specialists.shape[3]
    expert_local = specialist_switch_factor.shape[1]
    score_scale = head_size ** (-0.5)
    if lax.axis_size("tensor") == 1 and sources % 2 == 0 and section_count > 1 and tick_count > 1:
        results = relay(
            stored_counts[:, 0],
            jnp.transpose(picked_specialists, (0, 3, 1, 2)),
            jnp.transpose(chooser_mixing_share, (0, 3, 1, 2)),
            mixing_scale_factor,
            summary_scale_factor,
            specialist_scale_factor,
            opening_residual[0],
            incoming_residual,
            stored_summaries[:, 0, 0],
            asking_projection[0],
            compress_projection[0],
            summary_lookup_factor[0],
            summary_content_factor[0],
            merging_projection[0],
            jnp.swapaxes(specialist_switch_factor[0], 1, 2),
            jnp.swapaxes(specialist_widen_factor[0], 1, 2),
            specialist_contract_factor[0],
        )
        return results[:, None]
    expert_ids = lax.broadcasted_iota(jnp.int32, (1, 1, 1, expert_local * sources), 3)
    shares_dense = jnp.sum(
        jnp.where(
            picked_specialists[:, 0][..., None] == expert_ids,
            chooser_mixing_share[:, 0][..., None],
            0.0,
        ),
        axis=2,
    )
    shares_dense = jnp.swapaxes(shares_dense, 1, 2)
    outputs = []
    present_carry = opening_residual[0]
    section_out = present_carry
    for step_index in range(tick_count):
        if step_index > 0:
            handed = shifted(section_out, "section", 1)
            present_carry = jnp.where(
                segment_ordinal == 0, incoming_residual[step_index - 1], handed
            )
        micro_index = step_index - segment_ordinal + section_count - 1
        length = lax.dynamic_index_in_dim(stored_counts[:, 0], micro_index, 0, keepdims=False)
        full_rows = lax.all_gather(present_carry, "tensor", axis=1, tiled=True)
        normed = row_norm(full_rows.astype(jnp.float32), mixing_scale_factor[0]).astype(
            jnp.bfloat16
        )
        queries = jnp.dot(normed, asking_projection[0], preferred_element_type=jnp.float32).astype(
            jnp.bfloat16
        )
        queries = queries.reshape(piece_list, local_heads, head_size)
        q_lat = jnp.einsum(
            "thd,hdl->thl", queries, summary_lookup_factor[0], preferred_element_type=jnp.float32
        ).astype(jnp.bfloat16)
        latent_part = jnp.dot(normed, compress_projection[0], preferred_element_type=jnp.float32)
        latent_raw = lax.all_gather(
            latent_part.astype(jnp.bfloat16), "tensor", axis=1, tiled=True
        ).astype(latent_part.dtype)
        new_latent = row_norm(latent_raw, summary_scale_factor[0]).astype(jnp.bfloat16)
        o_lat = attend(q_lat, stored_summaries[step_index, 0, 0], new_latent, length, score_scale)
        heads_out = jnp.einsum(
            "thl,hld->thd", o_lat, summary_content_factor[0], preferred_element_type=jnp.float32
        ).astype(jnp.bfloat16)
        heads_out = heads_out.reshape(piece_list, local_heads * head_size)
        head_terms = jnp.dot(heads_out, merging_projection[0], preferred_element_type=jnp.float32)
        residual = present_carry.astype(jnp.float32) + lax.psum_scatter(
            head_terms.astype(jnp.bfloat16), "tensor", scatter_dimension=1, tiled=True
        ).astype(jnp.float32)
        squares = lax.psum(jnp.sum(residual * residual, axis=1), "tensor")
        moe_input = (
            residual
            * lax.rsqrt(squares / full_width + epsilon)[:, None]
            * specialist_scale_factor[0]
        ).astype(jnp.bfloat16)
        whole_rows = lax.all_gather(moe_input, "tensor", axis=1, tiled=True)
        routed = experts(
            whole_rows,
            shares_dense[step_index],
            jnp.swapaxes(specialist_switch_factor[0], 1, 2),
            jnp.swapaxes(specialist_widen_factor[0], 1, 2),
            specialist_contract_factor[0],
        )
        if lax.axis_size("tensor") > 1:
            routed = lax.psum_scatter(
                routed.astype(jnp.bfloat16), "tensor", scatter_dimension=1, tiled=True
            ).astype(jnp.float32)
        section_out = (residual + routed).astype(jnp.bfloat16)
        outputs.append(section_out)
    return jnp.stack(outputs)[:, None]


def solution(mesh):
    in_specs = (
        P("section", ("groups", "expert"), "tensor"),
        P(None, ("groups", "expert"), "tensor"),
        P(None, "section", ("groups", "expert"), None, None),
        P(None, ("groups", "expert")),
        P(None, "section", ("groups", "expert"), None),
        P(None, "section", ("groups", "expert"), None),
        P("section", None),
        P("section", None, "tensor"),
        P("section", "tensor", None, None),
        P("section", "tensor", None, None),
        P("section", "tensor", None),
        P("section", None, "tensor"),
        P("section", None),
        P("section", "tensor"),
        P("section", "expert", None, "tensor"),
        P("section", "expert", None, "tensor"),
        P("section", "expert", "tensor", None),
    )
    out_specs = P(None, "section", ("groups", "expert"), "tensor")
    return jax.shard_map(shards, mesh=mesh, in_specs=in_specs, out_specs=out_specs, check_vma=False)
```
